32 devices in a mesh: batch: 16 (over z, y, x), mp: 2 (over core).
Axes of the slice: x: 2, y: 2, z: 4, core: 2. Of those that a mesh axis runs over, the one named last changes fastest.
Arguments:
- hidden: bfloat16 [16384, 1024], P(('batch', 'mp')), may hold values from -6 to 6
- cell_ids: int32 [32, 512], P('batch'), may hold values from 0 to 127, never falling along the last dimension, each value on 1 to 60 neighbouring positions
- boxes: int32 [32, 128, 4], P('batch'), may hold values from 0 to 1023
- x_table: bfloat16 [1024, 1024], replicated, may hold values from -3 to 3
- y_table: bfloat16 [1024, 1024], replicated, may hold values from -3 to 3
- w_query: bfloat16 [1024, 1024], P(None, 'mp'), may hold values from -0.1875 to 0.1875
- b_query: bfloat16 [1024], P('mp'), may hold values from -3 to 3
- w_key: bfloat16 [1024, 1024], P(None, 'mp'), may hold values from -0.1875 to 0.1875
- w_value: bfloat16 [1024, 1024], P(None, 'mp'), may hold values from -0.1875 to 0.1875
- b_value: bfloat16 [1024], P('mp'), may hold values from -3 to 3
- w_out: bfloat16 [1024, 1024], P('mp'), may hold values from -3 to 3
- b_out: bfloat16 [1024], replicated, may hold values from -3 to 3
- ln1_gain: bfloat16 [1024], replicated, may hold values from 0.5 to 1.5
- ln1_bias: bfloat16 [1024], replicated, may hold values from -1 to 1
- w_up: bfloat16 [1024, 4096], P(None, 'mp'), may hold values from -0.1875 to 0.1875
- b_up: bfloat16 [4096], P('mp'), may hold values from -3 to 3
- w_down: bfloat16 [4096, 1024], P('mp'), may hold values from -0.09375 to 0.09375
- b_down: bfloat16 [1024], replicated, may hold values from -3 to 3
- ln2_gain: bfloat16 [1024], replicated, may hold values from 0.5 to 1.5
- ln2_bias: bfloat16 [1024], replicated, may hold values from -1 to 1
- d_out: bfloat16 [16384, 1024], P(('batch', 'mp')), may hold values from -6 to 6
Outputs:
- layer_out: bfloat16 [16384, 1024], P(('batch', 'mp'))
- d_hidden: float32 [16384, 1024], P(('batch', 'mp'))
- grad_w_query: float32 [1024, 1024], P(None, 'mp')
- grad_b_query: float32 [1024], P('mp')
- grad_w_key: float32 [1024, 1024], P(None, 'mp')
- grad_w_value: float32 [1024, 1024], P(None, 'mp')
- grad_b_value: float32 [1024], P('mp')
- grad_w_out: float32 [1024, 1024], P('mp')
- grad_b_out: float32 [1024], replicated
- grad_ln1_gain: float32 [1024], replicated
- grad_ln1_bias: float32 [1024], replicated
- grad_w_up: float32 [1024, 4096], P(None, 'mp')
- grad_b_up: float32 [4096], P('mp')
- grad_w_down: float32 [4096, 1024], P('mp')
- grad_b_down: float32 [1024], replicated
- grad_ln2_gain: float32 [1024], replicated
- grad_ln2_bias: float32 [1024], replicated
The draws below stay inside these ranges and needn't reach their ends.
Inputs may be any that keep to these rules, and one draw needn't show every extreme that they name: `cell_ids`: numbered from 0 within each page, never falling along a page; each of the 128 cells has 1 to 60 tokens and one has 60.
All inputs are finite; a program needn't handle non-finite values.
Results may differ from the reference program's by a relative error of at most 0.023.
Values may be sent and summed in bfloat16 or wider, within the bound.
No kernel may reach another device: no remote copies, remote signals or barrier semaphores. Data moves between devices by JAX's collectives and lax.ppermute only.
A program may use at most 128 MiB of HBM per device.

```python
import math
import jax
import jax.numpy as jnp
import numpy as np
from jax import lax

D = 1024
HEADS = 16
HDIM = 64
FF = 4096
POS = 1024
PAGE_LEN = 512
CELLS = 128
CELL_MOST = 60
PAGES = 32
TOKENS = 16384


def with_ends(values, stream_key, least, largest):
    place = [jax.random.randint(jax.random.fold_in(stream_key, axis), (), 0, length) for axis, length in enumerate(values.shape)]
    widest = values.shape.index(max(values.shape))
    next_to = place[:widest] + [(place[widest] + 1) % values.shape[widest]] + place[widest + 1:]
    return values.at[tuple(place)].set(least).at[tuple(next_to)].set(largest)


def steps_of(stream_key, dims, split, low, top_value):
    loudness = 1.0
    for dim, blocks in split:
        heights = jax.random.uniform(jax.random.fold_in(jax.random.fold_in(stream_key, 6), dim), (blocks,), jnp.float32, low / len(split), top_value / len(split))
        loudness = loudness * jnp.repeat(jnp.exp(heights), dims[dim] // blocks).reshape((-1,) + (1,) * (len(dims) - 1 - dim))
    return loudness


def profile(count, total, limit, slope):
    loads = [(1 << 20) // math.isqrt(rank ** slope) + 1 for rank in range(2, count + 1)]
    spare, given = total - limit - (count - 1), [1] * (count - 1)
    while spare > 0:
        movable = [i for i in range(count - 1) if given[i] < limit]
        whole, left = sum([loads[i] for i in movable]), spare
        for i in movable:
            extra = min(limit - given[i], max(1, left * loads[i] // whole), spare)
            given[i] = given[i] + extra
            spare = spare - extra
    return np.array([limit] + given)


def ragged(key, count, total, bound, slope):
    if count == 2:
        one = jax.random.randint(key, (), max(1, total - bound), min(bound, total - 1) + 1)
        return jnp.stack([one, total - one])
    sizes = jnp.asarray(profile(count, total, bound, slope), jnp.int32)
    twos = (count - 1) // 2
    giver, receiver = sizes[1:1 + 2 * twos:2], sizes[2:2 + 2 * twos:2]
    margin = jnp.minimum(giver - 1, bound - receiver)
    passed = jax.random.randint(jax.random.fold_in(key, 1), (twos,), 0, 1 << 20) % (margin + 1)
    sizes = sizes.at[1:1 + 2 * twos:2].set(giver - passed).at[2:2 + 2 * twos:2].set(receiver + passed)
    return sizes[jax.random.permutation(jax.random.fold_in(key, 2), count)]


def normal_values(own_key, extent, width, bound, shards=(), kind=jnp.bfloat16):
    loudness = steps_of(own_key, extent, shards, -0.22, 0.18) if shards else 1.0
    result = jax.random.normal(own_key, extent, jnp.float32) * width * loudness
    return jnp.minimum(jnp.maximum(result, -bound), bound).astype(kind)


def setup_inputs(seed: int = 0) -> dict:
    splits = jax.random.split(jax.random.key(seed), 22)
    return {
        "hidden": normal_values(splits[0], (TOKENS, D), 1.0, 6.0, ((0, 32),)),
        "cell_ids": jax.vmap(lambda own: jnp.searchsorted(jnp.cumsum(ragged(own, CELLS, PAGE_LEN, CELL_MOST, 2)), jnp.arange(PAGE_LEN), side="right"))(jax.random.split(splits[1], PAGES)).reshape((PAGES, PAGE_LEN)).astype(jnp.int32),
        "boxes": with_ends(jax.random.randint(splits[2], (PAGES, CELLS, 4), 0, POS), jax.random.fold_in(splits[2], 1), 0, POS - 1).astype(jnp.int32),
        "x_table": normal_values(splits[3], (POS, D), 0.5, 3.0),
        "y_table": normal_values(splits[4], (POS, D), 0.5, 3.0),
        "w_query": normal_values(splits[5], (D, HEADS * HDIM), D ** -0.5, 0.1875, ((1, 2),)),
        "b_query": normal_values(splits[6], (HEADS * HDIM,), 0.5, 3.0, ((0, 2),)),
        "w_key": normal_values(splits[7], (D, HEADS * HDIM), D ** -0.5, 0.1875, ((1, 2),)),
        "w_value": normal_values(splits[8], (D, HEADS * HDIM), D ** -0.5, 0.1875, ((1, 2),)),
        "b_value": normal_values(splits[9], (HEADS * HDIM,), 0.5, 3.0, ((0, 2),)),
        "w_out": normal_values(splits[10], (HEADS * HDIM, D), (max(D // 256, 1)) ** -0.5, 3.0, ((0, 2),)),
        "b_out": normal_values(splits[11], (D,), 0.5, 3.0),
        "ln1_gain": jnp.clip(1.0 + 0.1 * jax.random.normal(splits[12], (D,), jnp.float32), 0.5, 1.5).astype(jnp.bfloat16),
        "ln1_bias": normal_values(splits[13], (D,), 0.2, 1.0),
        "w_up": normal_values(splits[14], (D, FF), D ** -0.5, 0.1875, ((1, 2),)),
        "b_up": normal_values(splits[15], (FF,), 0.5, 3.0, ((0, 2),)),
        "w_down": normal_values(splits[16], (FF, D), FF ** -0.5, 0.09375, ((0, 2),)),
        "b_down": normal_values(splits[17], (D,), 0.5, 3.0),
        "ln2_gain": jnp.clip(1.0 + 0.1 * jax.random.normal(splits[18], (D,), jnp.float32), 0.5, 1.5).astype(jnp.bfloat16),
        "ln2_bias": normal_values(splits[19], (D,), 0.2, 1.0),
        "d_out": normal_values(splits[20], (TOKENS, D), 1.0, 6.0, ((0, 32),)),
    }


@jax.custom_vjp
def low(v):
    return lax.optimization_barrier(v.astype(jnp.bfloat16)).astype(jnp.float32)

@jax.custom_vjp
def low_back(v):
    return v

def low_keep(v):
    return (low(v), None)

def low_pass(kept, grad):
    return (grad,)

def back_keep(v):
    return (v, None)

def back_low(kept, grad):
    return (low(grad),)
low.defvjp(low_keep, low_pass)
low_back.defvjp(back_keep, back_low)

def product(left, right):
    return jnp.dot(left, right, precision=lax.Precision.HIGHEST, preferred_element_type=jnp.float32)

def layer_norm(values, gain, shift):
    average = lax.optimization_barrier(jnp.mean(values, axis=-1, keepdims=True))
    centred = values - average
    spread = lax.optimization_barrier(jnp.mean(centred * centred, axis=-1, keepdims=True))
    return centred * lax.rsqrt(spread + 1e-12) * gain + shift

def attend(page_block):
    queries, keys_page, values_page = page_block
    scores = jnp.einsum('qhd,khd->hqk', queries, keys_page, precision=lax.Precision.HIGHEST) * HDIM ** (-0.5)
    weights = jax.nn.softmax(low_back(scores), axis=-1)
    return jnp.einsum('hqk,khd->qhd', low(weights), values_page, precision=lax.Precision.HIGHEST)

def forward(params, inputs):
    w_query, b_query, w_key, w_value, b_value, w_out, b_out, ln1_gain, ln1_bias, w_up, b_up, w_down, b_down, ln2_gain, ln2_bias = params
    x_low = low(inputs)
    queries = low(low_back(product(x_low, w_query) + b_query))
    keys_all = low(low_back(product(x_low, w_key)))
    values_all = low(low_back(product(x_low, w_value) + b_value))
    page_shape = (-1, PAGE_LEN, HEADS, HDIM)
    context = lax.map(jax.checkpoint(attend), (queries.reshape(page_shape), keys_all.reshape(page_shape), values_all.reshape(page_shape)))
    context = low(low_back(context.reshape(-1, HEADS * HDIM)))
    resid = inputs + low_back(product(context, w_out)) + b_out
    hidden_mid = layer_norm(resid, ln1_gain, ln1_bias)
    pre_act = low_back(product(low(hidden_mid), w_up) + b_up)
    activ = low(jax.nn.gelu(pre_act, approximate=False))
    second = hidden_mid + low_back(product(activ, w_down)) + b_down
    return layer_norm(second, ln2_gain, ln2_bias)

def reference(hidden, cell_ids, boxes, x_table, y_table, w_query, b_query, w_key, w_value, b_value, w_out, b_out, ln1_gain, ln1_bias, w_up, b_up, w_down, b_down, ln2_gain, ln2_bias, d_out):
    params = tuple((weight_arg.astype(jnp.float32) for weight_arg in (w_query, b_query, w_key, w_value, b_value, w_out, b_out, ln1_gain, ln1_bias, w_up, b_up, w_down, b_down, ln2_gain, ln2_bias)))
    page_index = jnp.arange(PAGES, dtype=jnp.int32)[:, None] * CELLS + cell_ids
    cell_boxes = jnp.take(boxes.reshape(PAGES * CELLS, 4), page_index.reshape(-1), axis=0)
    x_float = x_table.astype(jnp.float32)
    y_float = y_table.astype(jnp.float32)
    layout = jnp.take(x_float, cell_boxes[:, 0], axis=0) + jnp.take(y_float, cell_boxes[:, 1], axis=0) + jnp.take(x_float, cell_boxes[:, 2], axis=0) + jnp.take(y_float, cell_boxes[:, 3], axis=0)
    inputs = hidden.astype(jnp.float32) + layout
    group = math.gcd(PAGES, 8)
    blocks = PAGES // group
    stacked = inputs.reshape(blocks, group * PAGE_LEN, D)
    cotangent = d_out.astype(jnp.float32).reshape(blocks, group * PAGE_LEN, D)

    def step(totals, item):
        outputs, pull = jax.vjp(forward, params, item[0])
        grads_params, grads_input = pull(item[1])
        return (jax.tree.map(jnp.add, totals, grads_params), (outputs, grads_input))
    totals, (outputs, grads_input) = lax.scan(step, jax.tree.map(jnp.zeros_like, params), (stacked, cotangent))
    return (outputs.reshape(TOKENS, D).astype(jnp.bfloat16), grads_input.reshape(TOKENS, D), totals[0], totals[1], totals[2], totals[3], totals[4], totals[5], totals[6], totals[7], totals[8], totals[9], totals[10], totals[11], totals[12], totals[13], totals[14])
```

```python
import jax
import jax.numpy as jnp
from jax import lax
from jax.experimental import pallas as pl
from jax.experimental.pallas import tpu as pltpu
from jax.sharding import PartitionSpec as P

HDIM = 64
PAGE_LEN = 512
CELLS = 128


def contract_rows(left, right):
    return lax.dot_general(
        left, right, (((0,), (0,)), ((), ())), preferred_element_type=jnp.float32
    )


def contract_last(left, right):
    return lax.dot_general(
        left, right, (((1,), (1,)), ((), ())), preferred_element_type=jnp.float32
    )


def layer_norm(values, gain, shift):
    average = jnp.mean(values, axis=-1, keepdims=True)
    centred = values - average
    rstd_rows = lax.rsqrt(jnp.mean(centred * centred, axis=-1, keepdims=True) + 1e-12)
    normed = centred * rstd_rows
    return (normed * gain + shift, normed, rstd_rows)


def norm_back(upstream, normed, rstd_rows, gain):
    scaled = upstream * gain
    return rstd_rows * (
        scaled
        - jnp.mean(scaled, axis=-1, keepdims=True)
        - normed * jnp.mean(scaled * normed, axis=-1, keepdims=True)
    )


def gelu_slope(values):
    return (
        0.5 * (1.0 + lax.erf(values * 0.7071067811865476))
        + values * jnp.exp(-0.5 * values * values) * 0.3989422804014327
    )


def page_scores(queries, keys_page):
    return jnp.einsum(
        "qhd,khd->hqk", queries, keys_page, preferred_element_type=jnp.float32
    ) * HDIM ** (-0.5)


def attend(page_block):
    queries, keys_page, values_page = page_block
    scores = page_scores(queries, keys_page)
    maximum = jnp.max(scores, axis=-1, keepdims=True)
    log_total = maximum + jnp.log(jnp.sum(jnp.exp(scores - maximum), axis=-1, keepdims=True))
    weights = jnp.exp(scores - log_total).astype(jnp.bfloat16)
    context = jnp.einsum("hqk,khd->qhd", weights, values_page, preferred_element_type=jnp.float32)
    return (context.astype(jnp.bfloat16), log_total[..., 0])


def attend_back(page_block):
    queries, keys_page, values_page, log_total, d_context = page_block
    weights = jnp.exp(page_scores(queries, keys_page) - log_total[..., None])
    d_weights = jnp.einsum(
        "qhd,khd->hqk", d_context, values_page, preferred_element_type=jnp.float32
    )
    d_values = jnp.einsum(
        "hqk,qhd->khd", weights.astype(jnp.bfloat16), d_context, preferred_element_type=jnp.float32
    )
    d_scores = (
        weights * (d_weights - jnp.sum(weights * d_weights, axis=-1, keepdims=True))
    ).astype(jnp.bfloat16)
    factor = HDIM ** (-0.5)
    d_queries = (
        jnp.einsum("hqk,khd->qhd", d_scores, keys_page, preferred_element_type=jnp.float32) * factor
    )
    d_keys = (
        jnp.einsum("hqk,qhd->khd", d_scores, queries, preferred_element_type=jnp.float32) * factor
    )
    return (
        d_queries.astype(jnp.bfloat16),
        d_keys.astype(jnp.bfloat16),
        d_values.astype(jnp.bfloat16),
    )


def shards_general(
    hidden,
    cell_ids,
    boxes,
    x_table,
    y_table,
    w_query,
    b_query,
    w_key,
    w_value,
    b_value,
    w_out,
    b_out,
    ln1_gain,
    ln1_bias,
    w_up,
    b_up,
    w_down,
    b_down,
    ln2_gain,
    ln2_bias,
    d_out,
):
    row_count = hidden.shape[0]
    width_local = w_query.shape[1]
    first_row = lax.axis_index("mp") * row_count
    own_cells = lax.dynamic_slice_in_dim(cell_ids.reshape(-1), first_row, row_count)
    page_local = (first_row + jnp.arange(row_count, dtype=jnp.int32)) // PAGE_LEN
    cell_boxes = jnp.take(boxes.reshape(-1, 4), page_local * CELLS + own_cells, axis=0)
    layout = (
        jnp.take(x_table, cell_boxes[:, 0], axis=0).astype(jnp.float32)
        + jnp.take(y_table, cell_boxes[:, 1], axis=0).astype(jnp.float32)
        + jnp.take(x_table, cell_boxes[:, 2], axis=0).astype(jnp.float32)
        + jnp.take(y_table, cell_boxes[:, 3], axis=0).astype(jnp.float32)
    )
    inputs = hidden.astype(jnp.float32) + layout
    x_all = lax.all_gather(inputs.astype(jnp.bfloat16), "mp", axis=0, tiled=True)
    queries = (
        jnp.dot(x_all, w_query, preferred_element_type=jnp.float32) + b_query.astype(jnp.float32)
    ).astype(jnp.bfloat16)
    keys_all = jnp.dot(x_all, w_key, preferred_element_type=jnp.float32).astype(jnp.bfloat16)
    values_all = (
        jnp.dot(x_all, w_value, preferred_element_type=jnp.float32) + b_value.astype(jnp.float32)
    ).astype(jnp.bfloat16)
    page_shape = (-1, PAGE_LEN, width_local // HDIM, HDIM)
    page_split = (
        queries.reshape(page_shape),
        keys_all.reshape(page_shape),
        values_all.reshape(page_shape),
    )
    context, log_total = lax.map(attend, page_split)
    context = context.reshape(-1, width_local)
    attn_rows = lax.psum_scatter(
        jnp.dot(context, w_out, preferred_element_type=jnp.float32),
        "mp",
        scatter_dimension=0,
        tiled=True,
    )
    resid = inputs + attn_rows + b_out.astype(jnp.float32)
    hidden_mid, normed_one, rstd_one = layer_norm(
        resid, ln1_gain.astype(jnp.float32), ln1_bias.astype(jnp.float32)
    )
    mid_low = hidden_mid.astype(jnp.bfloat16)
    mid_all = lax.all_gather(mid_low, "mp", axis=0, tiled=True)
    pre_act = jnp.dot(mid_all, w_up, preferred_element_type=jnp.float32) + b_up.astype(jnp.float32)
    activ = jax.nn.gelu(pre_act, approximate=False).astype(jnp.bfloat16)
    ffn_rows = lax.psum_scatter(
        jnp.dot(activ, w_down, preferred_element_type=jnp.float32),
        "mp",
        scatter_dimension=0,
        tiled=True,
    )
    second = hidden_mid + ffn_rows + b_down.astype(jnp.float32)
    final, normed_two, rstd_two = layer_norm(
        second, ln2_gain.astype(jnp.float32), ln2_bias.astype(jnp.float32)
    )
    layer_out = final.astype(jnp.bfloat16)
    upstream = d_out.astype(jnp.float32)
    grad_ln2_gain = jnp.sum(upstream * normed_two, axis=0)
    grad_ln2_bias = jnp.sum(upstream, axis=0)
    d_second = norm_back(upstream, normed_two, rstd_two, ln2_gain.astype(jnp.float32))
    grad_b_down = jnp.sum(d_second, axis=0)
    second_low = d_second.astype(jnp.bfloat16)
    grads_all = lax.all_gather(second_low, "mp", axis=0, tiled=True)
    grad_w_down = contract_rows(activ, grads_all)
    d_pre = (contract_last(grads_all, w_down) * gelu_slope(pre_act)).astype(jnp.bfloat16)
    grad_w_up = contract_rows(mid_all, d_pre)
    grad_b_up = jnp.sum(d_pre.astype(jnp.float32), axis=0)
    d_mid_ffn = lax.psum_scatter(contract_last(d_pre, w_up), "mp", scatter_dimension=0, tiled=True)
    d_mid = d_second + d_mid_ffn
    grad_ln1_gain = jnp.sum(d_mid * normed_one, axis=0)
    grad_ln1_bias = jnp.sum(d_mid, axis=0)
    d_resid = norm_back(d_mid, normed_one, rstd_one, ln1_gain.astype(jnp.float32))
    grad_b_out = jnp.sum(d_resid, axis=0)
    resid_all = lax.all_gather(d_resid.astype(jnp.bfloat16), "mp", axis=0, tiled=True)
    grad_w_out = contract_rows(context, resid_all)
    d_context = contract_last(resid_all, w_out).astype(jnp.bfloat16).reshape(page_shape)
    d_queries, d_keys, d_values = lax.map(attend_back, page_split + (log_total, d_context))
    d_queries = d_queries.reshape(-1, width_local)
    d_keys = d_keys.reshape(-1, width_local)
    d_values = d_values.reshape(-1, width_local)
    grad_w_query = contract_rows(x_all, d_queries)
    grad_w_key = contract_rows(x_all, d_keys)
    grad_w_value = contract_rows(x_all, d_values)
    grad_b_query = jnp.sum(d_queries.astype(jnp.float32), axis=0)
    grad_b_value = jnp.sum(d_values.astype(jnp.float32), axis=0)
    d_hidden = d_resid + lax.psum_scatter(
        (
            contract_last(d_queries, w_query)
            + contract_last(d_keys, w_key)
            + contract_last(d_values, w_value)
        ).astype(jnp.bfloat16),
        "mp",
        scatter_dimension=0,
        tiled=True,
    ).astype(jnp.float32)
    (
        grad_w_query,
        grad_b_query,
        grad_w_key,
        grad_w_value,
        grad_b_value,
        grad_w_out,
        grad_w_up,
        grad_b_up,
        grad_w_down,
    ) = (
        lax.psum(grad_w_query.astype(jnp.bfloat16), "batch").astype(jnp.float32),
        lax.psum(grad_b_query.astype(jnp.bfloat16), "batch").astype(jnp.float32),
        lax.psum(grad_w_key.astype(jnp.bfloat16), "batch").astype(jnp.float32),
        lax.psum(grad_w_value.astype(jnp.bfloat16), "batch").astype(jnp.float32),
        lax.psum(grad_b_value.astype(jnp.bfloat16), "batch").astype(jnp.float32),
        lax.psum(grad_w_out.astype(jnp.bfloat16), "batch").astype(jnp.float32),
        lax.psum(grad_w_up.astype(jnp.bfloat16), "batch").astype(jnp.float32),
        lax.psum(grad_b_up.astype(jnp.bfloat16), "batch").astype(jnp.float32),
        lax.psum(grad_w_down.astype(jnp.bfloat16), "batch").astype(jnp.float32),
    )
    grad_b_out, grad_ln1_gain, grad_ln1_bias, grad_b_down, grad_ln2_gain, grad_ln2_bias = lax.psum(
        (grad_b_out, grad_ln1_gain, grad_ln1_bias, grad_b_down, grad_ln2_gain, grad_ln2_bias),
        ("batch", "mp"),
    )
    return (
        layer_out,
        d_hidden,
        grad_w_query,
        grad_b_query,
        grad_w_key,
        grad_w_value,
        grad_b_value,
        grad_w_out,
        grad_b_out,
        grad_ln1_gain,
        grad_ln1_bias,
        grad_w_up,
        grad_b_up,
        grad_w_down,
        grad_b_down,
        grad_ln2_gain,
        grad_ln2_bias,
    )


def dot(left, right):
    return jnp.dot(left, right, preferred_element_type=jnp.float32)


def fixed(shape):
    return pl.BlockSpec(shape, lambda i: (0,) * len(shape))


def room(mebibytes):
    return pltpu.CompilerParams(vmem_limit_bytes=mebibytes * 2**20)


def rows_of(values):
    return values.reshape(1, -1)


def like(shape, kind=jnp.bfloat16):
    return jax.ShapeDtypeStruct(shape, kind)


def embed_kernel(page_ref, cells_ref, boxes_ref, x_ref, y_ref, hidden_ref, inputs_ref, low_ref):
    page = page_ref[0]
    tokens = hidden_ref.shape[0]
    positions = x_ref.shape[0]
    boxes = boxes_ref[page]
    place = lax.broadcasted_iota(jnp.int32, (CELLS, positions), 1)

    def counts(first, second):
        return (
            (place == boxes[:, first : first + 1]).astype(jnp.float32)
            + (place == boxes[:, second : second + 1]).astype(jnp.float32)
        ).astype(jnp.bfloat16)

    cells = dot(counts(0, 2), x_ref[...]) + dot(counts(1, 3), y_ref[...])
    high = cells.astype(jnp.bfloat16)
    rest = cells - high.astype(jnp.float32)
    middle = rest.astype(jnp.bfloat16)
    low = (rest - middle.astype(jnp.float32)).astype(jnp.bfloat16)
    ids = cells_ref[pl.ds(page, 1), :]
    member = (
        (lax.broadcasted_iota(jnp.int32, (CELLS, tokens), 0) == ids)
        .astype(jnp.float32)
        .astype(jnp.bfloat16)
    )
    layout = (
        contract_rows(member, high) + contract_rows(member, middle) + contract_rows(member, low)
    )
    inputs = hidden_ref[...].astype(jnp.float32) + layout
    inputs_ref[...] = inputs
    low_ref[...] = inputs.astype(jnp.bfloat16)


def embed(page, cell_ids, boxes, x_table, y_table, hidden):
    tokens, width = hidden.shape
    positions = x_table.shape[0]
    columns = 256
    return pl.pallas_call(
        embed_kernel,
        grid_spec=pltpu.PrefetchScalarGridSpec(
            num_scalar_prefetch=1,
            grid=(width // columns,),
            in_specs=[
                pl.BlockSpec(cell_ids.shape, lambda i, p: (0, 0)),
                pl.BlockSpec(boxes.shape, lambda i, p: (0, 0, 0)),
                pl.BlockSpec((positions, columns), lambda i, p: (0, i)),
                pl.BlockSpec((positions, columns), lambda i, p: (0, i)),
                pl.BlockSpec((tokens, columns), lambda i, p: (0, i)),
            ],
            out_specs=[
                pl.BlockSpec((tokens, columns), lambda i, p: (0, i)),
                pl.BlockSpec((tokens, columns), lambda i, p: (0, i)),
            ],
        ),
        out_shape=[like((tokens, width), jnp.float32), like((tokens, width))],
        compiler_params=room(16),
        name="embed",
    )(page, cell_ids, boxes, x_table, y_table, hidden)


def pick(values, head):
    lanes = lax.broadcasted_iota(jnp.int32, values.shape, 1) // HDIM
    return jnp.where(lanes == head, values, jnp.zeros_like(values))


def attend_kernel(x_ref, wq_ref, wk_ref, wv_ref, bq_ref, bv_ref, qkv_ref, context_ref, weights_ref):
    rows = 256
    pair = 2 * HDIM
    factor = HDIM ** (-0.5) * 1.4426950408889634
    x = x_ref[...]
    q = (dot(x, wq_ref[...]) + bq_ref[...].astype(jnp.float32)).astype(jnp.bfloat16)
    k = dot(x, wk_ref[...]).astype(jnp.bfloat16)
    v = (dot(x, wv_ref[...]) + bv_ref[...].astype(jnp.float32)).astype(jnp.bfloat16)
    qkv_ref[0] = q
    qkv_ref[1] = k
    qkv_ref[2] = v
    for start in range(0, x.shape[0], rows):
        here = slice(start, start + rows)
        for left in range(0, q.shape[1], pair):
            lanes = slice(left, left + pair)
            total = None
            for head in range(2):
                scores = contract_last(pick(q[here, lanes], head), k[:, lanes])
                maximum = jnp.max(scores, axis=-1, keepdims=True)
                powers = jnp.exp2((scores - maximum) * factor)
                weights = (powers * (1.0 / jnp.sum(powers, axis=-1, keepdims=True))).astype(
                    jnp.bfloat16
                )
                weights_ref[left // HDIM + head, here, :] = weights
                part = dot(weights, pick(v[:, lanes], head))
                total = part if total is None else total + part
            context_ref[here, lanes] = total.astype(jnp.bfloat16)


def attend_heads(x_low, w_query, w_key, w_value, b_query, b_value):
    tokens, depth = x_low.shape
    width = w_query.shape[1]
    columns = 4 * HDIM
    weight = pl.BlockSpec((depth, columns), lambda i: (0, i))
    bias = pl.BlockSpec((1, columns), lambda i: (0, i))
    return pl.pallas_call(
        attend_kernel,
        grid=(width // columns,),
        in_specs=[fixed((tokens, depth)), weight, weight, weight, bias, bias],
        out_specs=[
            pl.BlockSpec((3, tokens, columns), lambda i: (0, 0, i)),
            pl.BlockSpec((tokens, columns), lambda i: (0, i)),
            pl.BlockSpec((4, tokens, tokens), lambda i: (i, 0, 0)),
        ],
        out_shape=[
            like((3, tokens, width)),
            like((tokens, width)),
            like((width // HDIM, tokens, tokens)),
        ],
        compiler_params=room(24),
        name="attend",
    )(x_low, w_query, w_key, w_value, rows_of(b_query), rows_of(b_value))


def resid_kernel(
    inputs_ref, c0_ref, c1_ref, w0_ref, w1_ref, b_ref, gain_ref, bias_ref, low_ref, normed_ref, rstd_ref
):
    resid = (
        inputs_ref[...]
        + (dot(c0_ref[...], w0_ref[...]) + dot(c1_ref[...], w1_ref[...]))
        + b_ref[...].astype(jnp.float32)
    )
    mid, normed, rstd = layer_norm(
        resid, gain_ref[...].astype(jnp.float32), bias_ref[...].astype(jnp.float32)
    )
    low_ref[...] = mid.astype(jnp.bfloat16)
    normed_ref[...] = normed
    rstd_ref[...] = rstd


def resid_norm(inputs, context, w_out, b_out, gain, bias):
    tokens, width = inputs.shape
    part = context[0].shape[1]
    rows = 128
    wide = pl.BlockSpec((rows, width), lambda i: (i, 0))
    half = pl.BlockSpec((rows, part), lambda i: (i, 0))
    row = fixed((1, width))
    weight = fixed((part, width))
    return pl.pallas_call(
        resid_kernel,
        grid=(tokens // rows,),
        in_specs=[wide, half, half, weight, weight, row, row, row],
        out_specs=[wide, wide, pl.BlockSpec((rows, 1), lambda i: (i, 0))],
        out_shape=[
            like((tokens, width)),
            like((tokens, width), jnp.float32),
            like((tokens, 1), jnp.float32),
        ],
        compiler_params=room(16),
        name="resid_norm",
    )(inputs, *context, *w_out, rows_of(b_out), rows_of(gain), rows_of(bias))


def up_kernel(mid_ref, w_ref, b_ref, activ_ref, slope_ref):
    rows = 128
    bias = b_ref[...].astype(jnp.float32)
    for start in range(0, mid_ref.shape[0], rows):
        here = slice(start, start + rows)
        pre = dot(mid_ref[here, :], w_ref[...]) + bias
        below = 0.5 * (1.0 + lax.erf(pre * 0.7071067811865476))
        density = jnp.exp(-0.5 * pre * pre) * 0.3989422804014327
        activ_ref[here, :] = (pre * below).astype(jnp.bfloat16)
        slope_ref[here, :] = (below + pre * density).astype(jnp.bfloat16)


def up(mid_low, w_up, b_up):
    tokens, width = mid_low.shape
    units = w_up.shape[1]
    columns = 512
    out = pl.BlockSpec((tokens, columns), lambda i: (0, i))
    return pl.pallas_call(
        up_kernel,
        grid=(units // columns,),
        in_specs=[
            fixed((tokens, width)),
            pl.BlockSpec((width, columns), lambda i: (0, i)),
            pl.BlockSpec((1, columns), lambda i: (0, i)),
        ],
        out_specs=[out, out],
        out_shape=[like((tokens, units))] * 2,
        compiler_params=room(16),
        name="up",
    )(mid_low, w_up, rows_of(b_up))


def column_sum(values):
    return jnp.sum(values, axis=0, keepdims=True)


def turn_kernel(
    a0_ref, a1_ref, w0_ref, w1_ref, b_ref, normed_ref, gain1_ref, bias1_ref, gain_ref, bias_ref,
    d_out_ref, out_ref, d_second_ref, low_ref, sums_ref, acc_ref,
):
    step = pl.program_id(0)
    part = dot(a0_ref[...], w0_ref[...]) + dot(a1_ref[...], w1_ref[...])

    @pl.when(step == 0)
    def _():
        acc_ref[...] = part

    @pl.when(step > 0)
    def _():
        acc_ref[...] += part

    @pl.when(step == pl.num_programs(0) - 1)
    def _():
        rows = 64
        f32 = lambda ref: ref[...].astype(jnp.float32)
        gain1, bias1, gain, bias, b_down = [
            f32(r) for r in (gain1_ref, bias1_ref, gain_ref, bias_ref, b_ref)
        ]
        sums = None
        for start in range(0, acc_ref.shape[0], rows):
            here = slice(start, start + rows)
            second = normed_ref[here, :] * gain1 + bias1 + acc_ref[here, :] + b_down
            final, normed, rstd = layer_norm(second, gain, bias)
            out_ref[here, :] = final.astype(jnp.bfloat16)
            upstream = d_out_ref[here, :].astype(jnp.float32)
            d_second = norm_back(upstream, normed, rstd, gain)
            d_second_ref[here, :] = d_second
            low_ref[here, :] = d_second.astype(jnp.bfloat16)
            parts = (column_sum(upstream * normed), column_sum(upstream), column_sum(d_second))
            sums = parts if sums is None else tuple(a + b for a, b in zip(sums, parts))
        for j in range(3):
            sums_ref[j : j + 1, :] = sums[j]


def turn_back(activ, w_down, b_down, normed_one, gain1, bias1, gain, bias, d_out):
    tokens, units = activ[0].shape
    width = w_down[0].shape[1]
    columns = 512
    wide = fixed((tokens, width))
    row = fixed((1, width))
    act = pl.BlockSpec((tokens, columns), lambda i: (0, i))
    weight = pl.BlockSpec((columns, width), lambda i: (i, 0))
    return pl.pallas_call(
        turn_kernel,
        grid=(units // columns,),
        in_specs=[act, act, weight, weight, row, wide, row, row, row, row, wide],
        out_specs=[wide, wide, wide, fixed((8, width))],
        out_shape=[
            like((tokens, width)),
            like((tokens, width), jnp.float32),
            like((tokens, width)),
            like((8, width), jnp.float32),
        ],
        scratch_shapes=[pltpu.VMEM((tokens, width), jnp.float32)],
        compiler_params=room(30),
        name="turn_back",
    )(
        *activ, *w_down, rows_of(b_down), normed_one, rows_of(gain1), rows_of(bias1),
        rows_of(gain), rows_of(bias), d_out,
    )


def grad_kernel(left_ref, right_ref, *refs):
    out = contract_rows(left_ref[...], right_ref[...])
    if len(refs) == 2:
        out = out + refs[0][...].astype(jnp.float32)
    refs[-1][...] = out.astype(jnp.bfloat16)


def weight_grad(left, right, sent=None):
    tokens, rows = left.shape
    columns = right.shape[1]
    take = min(rows, 2**19 // columns)
    out = pl.BlockSpec((take, columns), lambda i: (i, 0))
    return pl.pallas_call(
        grad_kernel,
        grid=(rows // take,),
        in_specs=[pl.BlockSpec((tokens, take), lambda i: (0, i)), fixed((tokens, columns))]
        + ([] if sent is None else [out]),
        out_specs=out,
        out_shape=like((rows, columns)),
        compiler_params=room(12),
        name="weight_grad",
    )(left, right, *(() if sent is None else (sent,)))


def heads_grad_kernel(left_ref, right_ref, *refs):
    out = contract_rows(left_ref[...], right_ref[0])
    if len(refs) == 2:
        out = out + refs[0][0].astype(jnp.float32)
    refs[-1][0] = out.astype(jnp.bfloat16)


def heads_grad(left, right, sent=None):
    tokens, rows = left.shape
    kinds, _, columns = right.shape
    out = pl.BlockSpec((1, rows, columns), lambda i: (i, 0, 0))
    return pl.pallas_call(
        heads_grad_kernel,
        grid=(kinds,),
        in_specs=[fixed((tokens, rows)), pl.BlockSpec((1, tokens, columns), lambda i: (i, 0, 0))]
        + ([] if sent is None else [out]),
        out_specs=out,
        out_shape=like((kinds, rows, columns)),
        compiler_params=room(12),
        name="heads_grad",
    )(left, right, *(() if sent is None else (sent,)))


def pre_kernel(low_ref, w_ref, slope_ref, out_ref, sums_ref):
    d_pre = (contract_last(low_ref[...], w_ref[...]) * slope_ref[...].astype(jnp.float32)).astype(
        jnp.bfloat16
    )
    out_ref[...] = d_pre
    sums_ref[...] = column_sum(d_pre.astype(jnp.float32))


def pre_back(second_low, w_down, slope):
    tokens, width = second_low.shape
    units = w_down.shape[0]
    columns = 512
    out = pl.BlockSpec((tokens, columns), lambda i: (0, i))
    return pl.pallas_call(
        pre_kernel,
        grid=(units // columns,),
        in_specs=[fixed((tokens, width)), pl.BlockSpec((columns, width), lambda i: (i, 0)), out],
        out_specs=[out, pl.BlockSpec((1, columns), lambda i: (0, i))],
        out_shape=[like((tokens, units)), like((1, units), jnp.float32)],
        compiler_params=room(14),
        name="pre_back",
    )(second_low, w_down, slope)


def mid_kernel(
    p0_ref, p1_ref, w0_ref, w1_ref, d_second_ref, normed_ref, rstd_ref, gain_ref,
    resid_ref, low_ref, sums_ref, acc_ref,
):
    step = pl.program_id(0)
    part = contract_last(p0_ref[...], w0_ref[...]) + contract_last(p1_ref[...], w1_ref[...])

    @pl.when(step == 0)
    def _():
        acc_ref[...] = part

    @pl.when(step > 0)
    def _():
        acc_ref[...] += part

    @pl.when(step == pl.num_programs(0) - 1)
    def _():
        rows = 64
        gain = gain_ref[...].astype(jnp.float32)
        sums = None
        for start in range(0, acc_ref.shape[0], rows):
            here = slice(start, start + rows)
            d_mid = d_second_ref[here, :] + acc_ref[here, :]
            normed = normed_ref[here, :]
            d_resid = norm_back(d_mid, normed, rstd_ref[here, :], gain)
            resid_ref[here, :] = d_resid
            low_ref[here, :] = d_resid.astype(jnp.bfloat16)
            parts = (column_sum(d_resid), column_sum(d_mid * normed), column_sum(d_mid))
            sums = parts if sums is None else tuple(a + b for a, b in zip(sums, parts))
        for j in range(3):
            sums_ref[j : j + 1, :] = sums[j]


def mid_back(d_pre, w_up, d_second, normed, rstd, gain):
    tokens, units = d_pre[0].shape
    width = w_up[0].shape[0]
    columns = 512
    wide = fixed((tokens, width))
    part = pl.BlockSpec((tokens, columns), lambda i: (0, i))
    weight = pl.BlockSpec((width, columns), lambda i: (0, i))
    return pl.pallas_call(
        mid_kernel,
        grid=(units // columns,),
        in_specs=[
            part, part, weight, weight, wide, wide, fixed((tokens, 1)), fixed((1, width)),
        ],
        out_specs=[wide, wide, fixed((8, width))],
        out_shape=[
            like((tokens, width), jnp.float32),
            like((tokens, width)),
            like((8, width), jnp.float32),
        ],
        scratch_shapes=[pltpu.VMEM((tokens, width), jnp.float32)],
        compiler_params=room(30),
        name="mid_back",
    )(*d_pre, *w_up, d_second, normed, rstd, rows_of(gain))


def attend_back_kernel(qkv_ref, context_ref, weights_ref, low_ref, w_ref, out_ref, sums_ref):
    factor = HDIM ** (-0.5)
    queries, keys, values = qkv_ref[0], qkv_ref[1], qkv_ref[2]
    d_context = contract_last(low_ref[...], w_ref[...]).astype(jnp.bfloat16)
    product = d_context.astype(jnp.float32) * context_ref[...].astype(jnp.float32)
    grads = None
    for head in range(2):
        d_head = pick(d_context, head)
        d_weights = contract_last(d_head, values)
        inner = jnp.sum(pick(product, head), axis=-1, keepdims=True)
        weights = weights_ref[head]
        d_scores = (weights.astype(jnp.float32) * (d_weights - inner)).astype(jnp.bfloat16)
        parts = (
            dot(d_scores, pick(keys, head)),
            contract_rows(d_scores, pick(queries, head)),
            contract_rows(weights, d_head),
        )
        grads = parts if grads is None else tuple(a + b for a, b in zip(grads, parts))
    for j, scale in enumerate((factor, factor, 1.0)):
        grad = (grads[j] * scale).astype(jnp.bfloat16)
        out_ref[j] = grad
        sums_ref[j : j + 1, :] = column_sum(grad.astype(jnp.float32))


def attend_back_heads(qkv, context, weights, resid_low, w_out):
    _, tokens, width = qkv.shape
    depth = resid_low.shape[1]
    pair = 2 * HDIM
    block = pl.BlockSpec((3, tokens, pair), lambda i: (0, 0, i))
    return pl.pallas_call(
        attend_back_kernel,
        grid=(width // pair,),
        in_specs=[
            block,
            pl.BlockSpec((tokens, pair), lambda i: (0, i)),
            pl.BlockSpec((2, tokens, tokens), lambda i: (i, 0, 0)),
            fixed((tokens, depth)),
            pl.BlockSpec((pair, depth), lambda i: (i, 0)),
        ],
        out_specs=[block, pl.BlockSpec((8, pair), lambda i: (0, i))],
        out_shape=[like((3, tokens, width)), like((8, width), jnp.float32)],
        compiler_params=room(16),
        name="attend_back",
    )(qkv, context, weights, resid_low, w_out)


def last_kernel(d0_ref, d1_ref, *refs):
    resid_ref, out_ref = refs[6:]
    out = resid_ref[...]
    for j in range(3):
        out = out + (
            contract_last(d0_ref[j], refs[2 * j][...]) + contract_last(d1_ref[j], refs[2 * j + 1][...])
        )
    out_ref[...] = out


def last_back(d_heads, w_query, w_key, w_value, d_resid):
    tokens, width = d_resid.shape
    part = d_heads[0].shape[2]
    columns = 256
    heads = fixed((3, tokens, part))
    wide = pl.BlockSpec((tokens, columns), lambda i: (0, i))
    weight = pl.BlockSpec((columns, part), lambda i: (i, 0))
    return pl.pallas_call(
        last_kernel,
        grid=(width // columns,),
        in_specs=[heads, heads] + [weight] * 6 + [wide],
        out_specs=wide,
        out_shape=like((tokens, width), jnp.float32),
        compiler_params=room(16),
        name="last_back",
    )(*d_heads, *w_query, *w_key, *w_value, d_resid)


def move(values, target):
    pairs = []
    for z in range(4):
        for y in range(2):
            for x in range(2):
                for core in range(2):
                    there = target(x, y, z, core)
                    if there is not None:
                        tx, ty, tz, tcore = there
                        pairs.append(
                            ((z * 4 + y * 2 + x) * 2 + core, (tz * 4 + ty * 2 + tx) * 2 + tcore)
                        )
    return lax.ppermute(values, ("batch", "mp"), pairs)


def swap_core(values):
    return move(values, lambda x, y, z, core: (x, y, z, 1 - core))


def turn(x, y, z, core, along):
    return (1 - x, y, z, core) if along == 0 else (x, 1 - y, z, core)


def swap_first(values):
    return move(values, lambda x, y, z, core: turn(x, y, z, core, core))


def swap_second(values):
    return move(values, lambda x, y, z, core: turn(x, y, z, core, 1 - core))


def swap_first_ends(values):
    return move(values, lambda x, y, z, core: turn(x, y, z, core, core) if z in (0, 3) else None)


def swap_second_ends(values):
    return move(values, lambda x, y, z, core: turn(x, y, z, core, 1 - core) if z in (0, 3) else None)


def move_in(values):
    return move(values, lambda x, y, z, core: (x, y, (1, None, None, 2)[z], core) if z in (0, 3) else None)


def swap_middle(values):
    return move(values, lambda x, y, z, core: (x, y, 3 - z, core) if z in (1, 2) else None)


def move_out(values):
    return move(values, lambda x, y, z, core: (x, y, (None, 0, 3, None)[z], core) if z in (1, 2) else None)


def half_of(values, index):
    rows = values.shape[-2] // 2
    return lax.dynamic_slice_in_dim(values, index * rows, rows, axis=values.ndim - 2)


def total(*terms):
    return sum(t.astype(jnp.float32) for t in terms).astype(terms[0].dtype)


def join(own, other, index, kind=jnp.bfloat16):
    first = index == 0
    own, other = own.astype(kind), other.astype(kind)
    return jnp.concatenate([jnp.where(first, own, other), jnp.where(first, other, own)], axis=-2)


def own_bits():
    batch, core = lax.axis_index("batch"), lax.axis_index("mp")
    x, y = batch % 2, batch // 2 % 2
    return jnp.where(core == 0, x, y), jnp.where(core == 0, y, x), batch // 4


ORDER = (
    "down", "pre", "pre", "down", "D", "up", "mid", "up", "U", "out", "attn", "D",
    "out", "O", "attn", "U", "O", "heads", "last", "D", "heads", "small", "U", "H",
    "small", "O", "D", "small", "O", "H", "small", "O", "H", "small", "O", "U", "small",
    "O", "D", "small", "O", "H", "U", "O", "D", "H", "D", "U", "O", "H", "D", "O", "U",
    "H", "U", "H",
)


class Line:
    def __init__(self):
        self.last = ()

    def after(self, *values):
        tied = lax.optimization_barrier(values + self.last)
        return tied[0] if len(values) == 1 else tied[: len(values)]

    def did(self, *results):
        self.last = results
        return results[0] if len(results) == 1 else results


def line_sum(line, values):
    z = own_bits()[2]
    got = move_in(values)
    yield
    values, got = line.after(values, got)
    values = line.did(total(values, got))
    got = swap_middle(values)
    yield
    values, got = line.after(values, got)
    values = line.did(total(values, got))
    got = move_out(values)
    yield
    values, got = line.after(values, got)
    return jnp.where((z == 0) | (z == 3), got, values)


def sum_plane_first(line, values, finish):
    first, second, z = own_bits()
    values = line.after(values)
    got = swap_first(line.did(half_of(values, 1 - first)))
    yield
    values, got = line.after(values, got)
    own = half_of(values, first)
    more = swap_second(line.did(total(half_of(own, 1 - second), half_of(got, 1 - second))))
    yield
    own, got, more = line.after(own, got, more)
    quarter = line.did(total(half_of(own, second), half_of(got, second), more))
    quarter = yield from line_sum(line, quarter)
    quarter = line.did(quarter)
    got = swap_second(quarter)
    yield
    quarter, got = line.after(quarter, got)
    half = line.did(join(quarter, got, second))
    got = swap_first(half)
    yield
    half, got = line.after(half, got)
    finish(half, got, first)
    yield


def sum_ends_first(line, values, finish):
    first, second, z = own_bits()
    side = jnp.where(z <= 1, 0, 1)
    ends = (z == 0) | (z == 3)
    values = line.after(values)
    got = move_in(line.did(half_of(values, 1 - side)))
    yield
    values, got = line.after(values, got)
    got = swap_middle(line.did(total(half_of(values, 1 - side), got)))
    yield
    values, got = line.after(values, got)
    got = move_out(line.did(total(half_of(values, side), got)))
    yield
    values, got = line.after(values, got)
    half = line.did(total(half_of(values, side), got))
    got = swap_first_ends(half_of(half, 1 - first))
    yield
    half, got = line.after(half, got)
    own = half_of(half, first)
    more = swap_second_ends(line.did(total(half_of(own, 1 - second), half_of(got, 1 - second))))
    yield
    own, got, more = line.after(own, got, more)
    eighth = line.did(total(half_of(own, second), half_of(got, second), more))
    got = swap_second_ends(eighth)
    yield
    eighth, got = line.after(eighth, got)
    quarter = line.did(join(eighth, got, second))
    got = swap_first_ends(quarter)
    yield
    quarter, got = line.after(quarter, got)
    half = line.did(join(quarter, got, first))
    into = move_in(half)
    yield
    half, into = line.after(half, into)
    over = swap_middle(line.did(jnp.where(ends, half, into)))
    yield
    half, into, over = line.after(half, into, over)
    out = move_out(line.did(over))
    yield
    half, into, over, out = line.after(half, into, over, out)
    finish(jnp.where(ends, half, into), jnp.where(ends, out, over), side)
    yield


def sum_small(line, values):
    values = line.did(line.after(values))
    got = swap_first(values)
    yield
    values, got = line.after(values, got)
    values = line.did(values + got)
    got = swap_second(values)
    yield
    values, got = line.after(values, got)
    values = line.did(values + got)
    return (yield from line_sum(line, values))


def shards_paged(
    hidden,
    cell_ids,
    boxes,
    x_table,
    y_table,
    w_query,
    b_query,
    w_key,
    w_value,
    b_value,
    w_out,
    b_out,
    ln1_gain,
    ln1_bias,
    w_up,
    b_up,
    w_down,
    b_down,
    ln2_gain,
    ln2_bias,
    d_out,
):
    page = lax.axis_index("mp").reshape(1)
    biases = jnp.concatenate([b_query, b_value, b_up])
    biases = (biases, swap_core(biases))
    heads_width = b_query.shape[0]
    b_query = [b[:heads_width] for b in biases]
    b_value = [b[heads_width : 2 * heads_width] for b in biases]
    b_up = [b[2 * heads_width :] for b in biases]
    w_query = (w_query, swap_core(w_query))
    w_key = (w_key, swap_core(w_key))
    w_value = (w_value, swap_core(w_value))
    w_out = (w_out, swap_core(w_out))
    w_up = (w_up, swap_core(w_up))
    w_down = (w_down, swap_core(w_down))
    both = (0, 1)

    inputs, x_low = embed(page, cell_ids, boxes, x_table, y_table, hidden)
    attended = [
        attend_heads(x_low, w_query[i], w_key[i], w_value[i], b_query[i], b_value[i]) for i in both
    ]
    qkv, context, weights = zip(*attended)
    mid_low, normed_one, rstd_one = resid_norm(inputs, context, w_out, b_out, ln1_gain, ln1_bias)
    activ, slope = zip(*[up(mid_low, w_up[i], b_up[i]) for i in both])
    layer_out, d_second, second_low, second_sums = turn_back(
        activ, w_down, b_down, normed_one, ln1_gain, ln1_bias, ln2_gain, ln2_bias, d_out
    )

    line = Line()
    line.did(second_low)
    found = {"d_pre": {}, "pre sums": {}, "heads": {}, "heads sums": {}}

    def grads(name, product, left, right):
        sent = swap_core(line.did(product(line.after(left(1)), right(1))))
        yield
        mine, sent = line.after(left(0), sent)
        found[name] = line.did(product(mine, right(0), sent))
        yield

    def pre_steps():
        for i in (1, 0):
            low = line.after(second_low)
            found["d_pre"][i], found["pre sums"][i] = pre_back(low, w_down[i], slope[i])
            line.did(found["d_pre"][i])
            yield

    def mid_steps():
        d_pre = [found["d_pre"][i] for i in both]
        d_pre[0] = line.after(d_pre[0])
        found["d_resid"], found["resid_low"], found["mid sums"] = mid_back(
            d_pre, w_up, d_second, normed_one, rstd_one, ln1_gain
        )
        line.did(found["resid_low"])
        yield

    def attend_steps():
        for i in (1, 0):
            low = line.after(found["resid_low"])
            found["heads"][i], found["heads sums"][i] = attend_back_heads(
                qkv[i], context[i], weights[i], low, w_out[i]
            )
            line.did(found["heads"][i])
            yield

    def last_steps():
        d_heads = [found["heads"][i] for i in both]
        d_heads[0] = line.after(d_heads[0])
        found["d_hidden"] = line.did(
            last_back(d_heads, w_query, w_key, w_value, found["d_resid"])
        )
        yield

    def small_steps():
        split = []
        for i in both:
            sums = found["heads sums"][i]
            split.append([sums[0], sums[2], found["pre sums"][i][0]])
        copied = [found["mid sums"][j] for j in range(3)]
        copied += [second_sums[j] for j in (2, 0, 1)]
        found["sizes"] = [g.shape[0] for g in split[0] + copied]
        own, other = [jnp.concatenate(s + copied).reshape(-1, 1024) for s in split]
        got = swap_core(line.did(line.after(other)))
        yield
        own, got = line.after(own, got)
        small = yield from sum_small(line, own + got)
        found["small"] = line.did(small).reshape(-1)
        yield

    def finish(name):
        def store(half, got, index):
            found["grad " + name] = line.did(join(half, got, index, jnp.float32))

        return store

    steps = {
        "down": grads("down", weight_grad, lambda i: activ[i], lambda i: second_low),
        "pre": pre_steps(),
        "up": grads("up", weight_grad, lambda i: mid_low, lambda i: found["d_pre"][i]),
        "mid": mid_steps(),
        "out": grads("out", weight_grad, lambda i: context[i], lambda i: found["resid_low"]),
        "attn": attend_steps(),
        "heads": grads("heads", heads_grad, lambda i: x_low, lambda i: found["heads"][i]),
        "last": last_steps(),
        "small": small_steps(),
    }
    chunks = {
        "D": ("down", sum_plane_first),
        "U": ("up", sum_plane_first),
        "O": ("out", sum_ends_first),
        "H": ("heads", sum_plane_first),
    }
    for name in ORDER:
        if name not in steps:
            key, order = chunks[name]
            steps[name] = order(line, found[key], finish(key))
        next(steps[name])
    d_hidden = found["d_hidden"]
    grad_w_down, grad_w_up, grad_w_out = [found["grad " + n] for n in ("down", "up", "out")]
    grad_w_query, grad_w_key, grad_w_value = [found["grad heads"][j] for j in range(3)]
    sizes = found["sizes"]
    offsets = [sum(sizes[:i]) for i in range(len(sizes))]
    small = [found["small"][o : o + s] for o, s in zip(offsets, sizes)]
    grad_b_query, grad_b_value, grad_b_up = small[:3]
    grad_b_out, grad_ln1_gain, grad_ln1_bias, grad_b_down, grad_ln2_gain, grad_ln2_bias = small[3:]
    return (
        layer_out,
        d_hidden,
        grad_w_query,
        grad_b_query,
        grad_w_key,
        grad_w_value,
        grad_b_value,
        grad_w_out,
        grad_b_out,
        grad_ln1_gain,
        grad_ln1_bias,
        grad_w_up,
        grad_b_up,
        grad_w_down,
        grad_b_down,
        grad_ln2_gain,
        grad_ln2_bias,
    )


def solution(mesh):
    in_specs = (
        P(("batch", "mp"), None),
        P("batch", None),
        P("batch", None, None),
        P(),
        P(),
        P(None, "mp"),
        P("mp"),
        P(None, "mp"),
        P(None, "mp"),
        P("mp"),
        P("mp", None),
        P(),
        P(),
        P(),
        P(None, "mp"),
        P("mp"),
        P("mp", None),
        P(),
        P(),
        P(),
        P(("batch", "mp"), None),
    )
    out_specs = (
        P(("batch", "mp"), None),
        P(("batch", "mp"), None),
        P(None, "mp"),
        P("mp"),
        P(None, "mp"),
        P(None, "mp"),
        P("mp"),
        P("mp", None),
        P(),
        P(),
        P(),
        P(None, "mp"),
        P("mp"),
        P("mp", None),
        P(),
        P(),
        P(),
    )
    paged = mesh.shape["mp"] == 2 and mesh.shape["batch"] == 16
    shards = shards_paged if paged else shards_general
    return jax.shard_map(shards, mesh=mesh, in_specs=in_specs, out_specs=out_specs, check_vma=False)
```

```python
import functools

import jax
import jax.numpy as jnp
from jax import lax
from jax.experimental import pallas as pl
from jax.experimental.pallas import tpu as pltpu
from jax.sharding import PartitionSpec as P

HDIM = 64
PAGE_LEN = 512
CELLS = 128


def contract_rows(left, right):
    return lax.dot_general(
        left, right, (((0,), (0,)), ((), ())), preferred_element_type=jnp.float32
    )


def contract_last(left, right):
    return lax.dot_general(
        left, right, (((1,), (1,)), ((), ())), preferred_element_type=jnp.float32
    )


def layer_norm(values, gain, shift):
    average = jnp.mean(values, axis=-1, keepdims=True)
    centred = values - average
    rstd_rows = lax.rsqrt(jnp.mean(centred * centred, axis=-1, keepdims=True) + 1e-12)
    normed = centred * rstd_rows
    return (normed * gain + shift, normed, rstd_rows)


def norm_back(upstream, normed, rstd_rows, gain):
    scaled = upstream * gain
    return rstd_rows * (
        scaled
        - jnp.mean(scaled, axis=-1, keepdims=True)
        - normed * jnp.mean(scaled * normed, axis=-1, keepdims=True)
    )


def gelu_slope(values):
    return (
        0.5 * (1.0 + lax.erf(values * 0.7071067811865476))
        + values * jnp.exp(-0.5 * values * values) * 0.3989422804014327
    )


def page_scores(queries, keys_page):
    return jnp.einsum(
        "qhd,khd->hqk", queries, keys_page, preferred_element_type=jnp.float32
    ) * HDIM ** (-0.5)


def attend(page_block):
    queries, keys_page, values_page = page_block
    scores = page_scores(queries, keys_page)
    maximum = jnp.max(scores, axis=-1, keepdims=True)
    log_total = maximum + jnp.log(jnp.sum(jnp.exp(scores - maximum), axis=-1, keepdims=True))
    weights = jnp.exp(scores - log_total).astype(jnp.bfloat16)
    context = jnp.einsum("hqk,khd->qhd", weights, values_page, preferred_element_type=jnp.float32)
    return (context.astype(jnp.bfloat16), log_total[..., 0])


def attend_back(page_block):
    queries, keys_page, values_page, log_total, d_context = page_block
    weights = jnp.exp(page_scores(queries, keys_page) - log_total[..., None])
    d_weights = jnp.einsum(
        "qhd,khd->hqk", d_context, values_page, preferred_element_type=jnp.float32
    )
    d_values = jnp.einsum(
        "hqk,qhd->khd", weights.astype(jnp.bfloat16), d_context, preferred_element_type=jnp.float32
    )
    d_scores = (
        weights * (d_weights - jnp.sum(weights * d_weights, axis=-1, keepdims=True))
    ).astype(jnp.bfloat16)
    factor = HDIM ** (-0.5)
    d_queries = (
        jnp.einsum("hqk,khd->qhd", d_scores, keys_page, preferred_element_type=jnp.float32) * factor
    )
    d_keys = (
        jnp.einsum("hqk,qhd->khd", d_scores, queries, preferred_element_type=jnp.float32) * factor
    )
    return (
        d_queries.astype(jnp.bfloat16),
        d_keys.astype(jnp.bfloat16),
        d_values.astype(jnp.bfloat16),
    )


def shards_general(
    hidden,
    cell_ids,
    boxes,
    x_table,
    y_table,
    w_query,
    b_query,
    w_key,
    w_value,
    b_value,
    w_out,
    b_out,
    ln1_gain,
    ln1_bias,
    w_up,
    b_up,
    w_down,
    b_down,
    ln2_gain,
    ln2_bias,
    d_out,
):
    row_count = hidden.shape[0]
    width_local = w_query.shape[1]
    first_row = lax.axis_index("mp") * row_count
    own_cells = lax.dynamic_slice_in_dim(cell_ids.reshape(-1), first_row, row_count)
    page_local = (first_row + jnp.arange(row_count, dtype=jnp.int32)) // PAGE_LEN
    cell_boxes = jnp.take(boxes.reshape(-1, 4), page_local * CELLS + own_cells, axis=0)
    layout = (
        jnp.take(x_table, cell_boxes[:, 0], axis=0).astype(jnp.float32)
        + jnp.take(y_table, cell_boxes[:, 1], axis=0).astype(jnp.float32)
        + jnp.take(x_table, cell_boxes[:, 2], axis=0).astype(jnp.float32)
        + jnp.take(y_table, cell_boxes[:, 3], axis=0).astype(jnp.float32)
    )
    inputs = hidden.astype(jnp.float32) + layout
    x_all = lax.all_gather(inputs.astype(jnp.bfloat16), "mp", axis=0, tiled=True)
    queries = (
        jnp.dot(x_all, w_query, preferred_element_type=jnp.float32) + b_query.astype(jnp.float32)
    ).astype(jnp.bfloat16)
    keys_all = jnp.dot(x_all, w_key, preferred_element_type=jnp.float32).astype(jnp.bfloat16)
    values_all = (
        jnp.dot(x_all, w_value, preferred_element_type=jnp.float32) + b_value.astype(jnp.float32)
    ).astype(jnp.bfloat16)
    page_shape = (-1, PAGE_LEN, width_local // HDIM, HDIM)
    page_split = (
        queries.reshape(page_shape),
        keys_all.reshape(page_shape),
        values_all.reshape(page_shape),
    )
    context, log_total = lax.map(attend, page_split)
    context = context.reshape(-1, width_local)
    attn_rows = lax.psum_scatter(
        jnp.dot(context, w_out, preferred_element_type=jnp.float32),
        "mp",
        scatter_dimension=0,
        tiled=True,
    )
    resid = inputs + attn_rows + b_out.astype(jnp.float32)
    hidden_mid, normed_one, rstd_one = layer_norm(
        resid, ln1_gain.astype(jnp.float32), ln1_bias.astype(jnp.float32)
    )
    mid_low = hidden_mid.astype(jnp.bfloat16)
    mid_all = lax.all_gather(mid_low, "mp", axis=0, tiled=True)
    pre_act = jnp.dot(mid_all, w_up, preferred_element_type=jnp.float32) + b_up.astype(jnp.float32)
    activ = jax.nn.gelu(pre_act, approximate=False).astype(jnp.bfloat16)
    ffn_rows = lax.psum_scatter(
        jnp.dot(activ, w_down, preferred_element_type=jnp.float32),
        "mp",
        scatter_dimension=0,
        tiled=True,
    )
    second = hidden_mid + ffn_rows + b_down.astype(jnp.float32)
    final, normed_two, rstd_two = layer_norm(
        second, ln2_gain.astype(jnp.float32), ln2_bias.astype(jnp.float32)
    )
    layer_out = final.astype(jnp.bfloat16)
    upstream = d_out.astype(jnp.float32)
    grad_ln2_gain = jnp.sum(upstream * normed_two, axis=0)
    grad_ln2_bias = jnp.sum(upstream, axis=0)
    d_second = norm_back(upstream, normed_two, rstd_two, ln2_gain.astype(jnp.float32))
    grad_b_down = jnp.sum(d_second, axis=0)
    second_low = d_second.astype(jnp.bfloat16)
    grads_all = lax.all_gather(second_low, "mp", axis=0, tiled=True)
    grad_w_down = contract_rows(activ, grads_all)
    d_pre = (contract_last(grads_all, w_down) * gelu_slope(pre_act)).astype(jnp.bfloat16)
    grad_w_up = contract_rows(mid_all, d_pre)
    grad_b_up = jnp.sum(d_pre.astype(jnp.float32), axis=0)
    d_mid_ffn = lax.psum_scatter(contract_last(d_pre, w_up), "mp", scatter_dimension=0, tiled=True)
    d_mid = d_second + d_mid_ffn
    grad_ln1_gain = jnp.sum(d_mid * normed_one, axis=0)
    grad_ln1_bias = jnp.sum(d_mid, axis=0)
    d_resid = norm_back(d_mid, normed_one, rstd_one, ln1_gain.astype(jnp.float32))
    grad_b_out = jnp.sum(d_resid, axis=0)
    resid_all = lax.all_gather(d_resid.astype(jnp.bfloat16), "mp", axis=0, tiled=True)
    grad_w_out = contract_rows(context, resid_all)
    d_context = contract_last(resid_all, w_out).astype(jnp.bfloat16).reshape(page_shape)
    d_queries, d_keys, d_values = lax.map(attend_back, page_split + (log_total, d_context))
    d_queries = d_queries.reshape(-1, width_local)
    d_keys = d_keys.reshape(-1, width_local)
    d_values = d_values.reshape(-1, width_local)
    grad_w_query = contract_rows(x_all, d_queries)
    grad_w_key = contract_rows(x_all, d_keys)
    grad_w_value = contract_rows(x_all, d_values)
    grad_b_query = jnp.sum(d_queries.astype(jnp.float32), axis=0)
    grad_b_value = jnp.sum(d_values.astype(jnp.float32), axis=0)
    d_hidden = d_resid + lax.psum_scatter(
        (
            contract_last(d_queries, w_query)
            + contract_last(d_keys, w_key)
            + contract_last(d_values, w_value)
        ).astype(jnp.bfloat16),
        "mp",
        scatter_dimension=0,
        tiled=True,
    ).astype(jnp.float32)
    (
        grad_w_query,
        grad_b_query,
        grad_w_key,
        grad_w_value,
        grad_b_value,
        grad_w_out,
        grad_w_up,
        grad_b_up,
        grad_w_down,
    ) = (
        lax.psum(grad_w_query.astype(jnp.bfloat16), "batch").astype(jnp.float32),
        lax.psum(grad_b_query.astype(jnp.bfloat16), "batch").astype(jnp.float32),
        lax.psum(grad_w_key.astype(jnp.bfloat16), "batch").astype(jnp.float32),
        lax.psum(grad_w_value.astype(jnp.bfloat16), "batch").astype(jnp.float32),
        lax.psum(grad_b_value.astype(jnp.bfloat16), "batch").astype(jnp.float32),
        lax.psum(grad_w_out.astype(jnp.bfloat16), "batch").astype(jnp.float32),
        lax.psum(grad_w_up.astype(jnp.bfloat16), "batch").astype(jnp.float32),
        lax.psum(grad_b_up.astype(jnp.bfloat16), "batch").astype(jnp.float32),
        lax.psum(grad_w_down.astype(jnp.bfloat16), "batch").astype(jnp.float32),
    )
    grad_b_out, grad_ln1_gain, grad_ln1_bias, grad_b_down, grad_ln2_gain, grad_ln2_bias = lax.psum(
        (grad_b_out, grad_ln1_gain, grad_ln1_bias, grad_b_down, grad_ln2_gain, grad_ln2_bias),
        ("batch", "mp"),
    )
    return (
        layer_out,
        d_hidden,
        grad_w_query,
        grad_b_query,
        grad_w_key,
        grad_w_value,
        grad_b_value,
        grad_w_out,
        grad_b_out,
        grad_ln1_gain,
        grad_ln1_bias,
        grad_w_up,
        grad_b_up,
        grad_w_down,
        grad_b_down,
        grad_ln2_gain,
        grad_ln2_bias,
    )


def dot(left, right):
    return jnp.dot(left, right, preferred_element_type=jnp.float32)


def fixed(shape):
    return pl.BlockSpec(shape, lambda i: (0,) * len(shape))


LITTLE = pl.CostEstimate(flops=1, transcendentals=0, bytes_accessed=1)


def room(mebibytes):
    return pltpu.CompilerParams(vmem_limit_bytes=mebibytes * 2**20)


def stay(values):
    return pltpu.with_memory_space_constraint(values, pltpu.HBM)


def like(shape, kind=jnp.bfloat16):
    return jax.ShapeDtypeStruct(shape, kind)


def embed_kernel(
    page_ref, cells_ref, boxes_ref, x_ref, y_ref, hidden_ref, inputs_ref, low_ref, counts_ref, member_ref
):
    @pl.when(pl.program_id(0) == 0)
    def _():
        page = page_ref[0]
        boxes = boxes_ref[page]
        place = lax.broadcasted_iota(jnp.int32, counts_ref.shape[1:], 1)
        for j in range(2):
            counts = (place == boxes[:, j : j + 1]).astype(jnp.float32)
            counts = counts + (place == boxes[:, j + 2 : j + 3]).astype(jnp.float32)
            counts_ref[j] = counts.astype(jnp.bfloat16)
        ids = cells_ref[pl.ds(page, 1), :]
        member = lax.broadcasted_iota(jnp.int32, member_ref.shape, 0) == ids
        member_ref[...] = member.astype(jnp.float32).astype(jnp.bfloat16)

    cells = dot(counts_ref[0], x_ref[...]) + dot(counts_ref[1], y_ref[...])
    high = cells.astype(jnp.bfloat16)
    rest = cells - high.astype(jnp.float32)
    middle = rest.astype(jnp.bfloat16)
    low = (rest - middle.astype(jnp.float32)).astype(jnp.bfloat16)
    member = member_ref[...]
    layout = (
        contract_rows(member, high) + contract_rows(member, middle) + contract_rows(member, low)
    )
    inputs = hidden_ref[...].astype(jnp.float32) + layout
    inputs_ref[...] = inputs
    low_ref[...] = inputs.astype(jnp.bfloat16)


def embed(page, cell_ids, boxes, x_table, y_table, hidden):
    tokens, width = hidden.shape
    positions = x_table.shape[0]
    columns = 256
    return pl.pallas_call(
        embed_kernel,
        grid_spec=pltpu.PrefetchScalarGridSpec(
            num_scalar_prefetch=1,
            grid=(width // columns,),
            in_specs=[
                pl.BlockSpec(cell_ids.shape, lambda i, p: (0, 0)),
                pl.BlockSpec(boxes.shape, lambda i, p: (0, 0, 0)),
                pl.BlockSpec((positions, columns), lambda i, p: (0, i)),
                pl.BlockSpec((positions, columns), lambda i, p: (0, i)),
                pl.BlockSpec((tokens, columns), lambda i, p: (0, i)),
            ],
            out_specs=[
                pl.BlockSpec((tokens, columns), lambda i, p: (0, i)),
                pl.BlockSpec((tokens, columns), lambda i, p: (0, i)),
            ],
            scratch_shapes=[
                pltpu.VMEM((2, CELLS, positions), jnp.bfloat16),
                pltpu.VMEM((CELLS, tokens), jnp.bfloat16),
            ],
        ),
        out_shape=[like((tokens, width), jnp.float32), like((tokens, width))],
        cost_estimate=LITTLE,
        compiler_params=room(16),
        name="embed",
    )(page, cell_ids, boxes, x_table, y_table, hidden)


def pick(values, head):
    lanes = lax.broadcasted_iota(jnp.int32, values.shape, 1) // HDIM
    return jnp.where(lanes == head, values, jnp.zeros_like(values))


def attend_kernel(x_ref, wq_ref, wk_ref, wv_ref, b_ref, qkv_ref, context_ref, weights_ref):
    rows = 256
    pair = 2 * HDIM
    factor = HDIM ** (-0.5) * 1.4426950408889634
    x = x_ref[...]
    q = (dot(x, wq_ref[...]) + b_ref[0:1, :]).astype(jnp.bfloat16)
    k = dot(x, wk_ref[...]).astype(jnp.bfloat16)
    v = (dot(x, wv_ref[...]) + b_ref[1:2, :]).astype(jnp.bfloat16)
    qkv_ref[0] = q
    qkv_ref[1] = k
    qkv_ref[2] = v
    for start in range(0, x.shape[0], rows):
        here = slice(start, start + rows)
        for left in range(0, q.shape[1], pair):
            lanes = slice(left, left + pair)
            total = None
            for head in range(2):
                scores = contract_last(pick(q[here, lanes], head), k[:, lanes])
                maximum = jnp.max(scores, axis=-1, keepdims=True)
                powers = jnp.exp2((scores - maximum) * factor)
                weights = (powers * (1.0 / jnp.sum(powers, axis=-1, keepdims=True))).astype(
                    jnp.bfloat16
                )
                weights_ref[left // HDIM + head, here, :] = weights
                part = dot(weights, pick(v[:, lanes], head))
                total = part if total is None else total + part
            context_ref[here, lanes] = total.astype(jnp.bfloat16)


def attend_heads(x_low, w_query, w_key, w_value, biases):
    tokens, depth = x_low.shape
    width = w_query.shape[1]
    columns = 4 * HDIM
    weight = pl.BlockSpec((depth, columns), lambda i: (0, i))
    bias = pl.BlockSpec((biases.shape[0], columns), lambda i: (0, i))
    return pl.pallas_call(
        attend_kernel,
        grid=(width // columns,),
        in_specs=[fixed((tokens, depth)), weight, weight, weight, bias],
        out_specs=[
            pl.BlockSpec((3, tokens, columns), lambda i: (0, 0, i)),
            pl.BlockSpec((tokens, columns), lambda i: (0, i)),
            pl.BlockSpec((4, tokens, tokens), lambda i: (i, 0, 0)),
        ],
        out_shape=[
            like((3, tokens, width)),
            like((tokens, width)),
            pltpu.HBM((width // HDIM, tokens, tokens), jnp.bfloat16),
        ],
        cost_estimate=LITTLE,
        compiler_params=room(24),
        name="attend",
    )(x_low, w_query, w_key, w_value, biases)


def resid_kernel(
    inputs_ref, c0_ref, c1_ref, w0_ref, w1_ref, rows_ref, low_ref, normed_ref, rstd_ref
):
    resid = (
        inputs_ref[...]
        + (dot(c0_ref[...], w0_ref[...]) + dot(c1_ref[...], w1_ref[...]))
        + rows_ref[0:1, :]
    )
    mid, normed, rstd = layer_norm(resid, rows_ref[1:2, :], rows_ref[2:3, :])
    low_ref[...] = mid.astype(jnp.bfloat16)
    normed_ref[...] = normed
    rstd_ref[...] = rstd


def resid_norm(inputs, context, w_out, vectors):
    tokens, width = inputs.shape
    part = context[0].shape[1]
    rows = 128
    wide = pl.BlockSpec((rows, width), lambda i: (i, 0))
    half = pl.BlockSpec((rows, part), lambda i: (i, 0))
    weight = fixed((part, width))
    return pl.pallas_call(
        resid_kernel,
        grid=(tokens // rows,),
        in_specs=[wide, half, half, weight, weight, fixed(vectors.shape)],
        out_specs=[wide, wide, pl.BlockSpec((rows, 1), lambda i: (i, 0))],
        out_shape=[
            like((tokens, width)),
            like((tokens, width), jnp.float32),
            like((tokens, 1), jnp.float32),
        ],
        cost_estimate=LITTLE,
        compiler_params=room(16),
        name="resid_norm",
    )(inputs, *context, *w_out, vectors)


def up_kernel(mid_ref, w_ref, b_ref, activ_ref, slope_ref):
    rows = 128
    bias = b_ref[pl.ds(pl.program_id(0) + 2, 1), :]
    for start in range(0, mid_ref.shape[0], rows):
        here = slice(start, start + rows)
        pre = dot(mid_ref[here, :], w_ref[...]) + bias
        below = 0.5 * (1.0 + lax.erf(pre * 0.7071067811865476))
        density = jnp.exp(-0.5 * pre * pre) * 0.3989422804014327
        activ_ref[here, :] = (pre * below).astype(jnp.bfloat16)
        slope_ref[here, :] = (below + pre * density).astype(jnp.bfloat16)


def up(mid_low, w_up, biases):
    tokens, width = mid_low.shape
    units = w_up.shape[1]
    columns = biases.shape[1]
    out = pl.BlockSpec((tokens, columns), lambda i: (0, i))
    return pl.pallas_call(
        up_kernel,
        grid=(units // columns,),
        in_specs=[
            fixed((tokens, width)),
            pl.BlockSpec((width, columns), lambda i: (0, i)),
            fixed(biases.shape),
        ],
        out_specs=[out, out],
        out_shape=[like((tokens, units))] * 2,
        cost_estimate=LITTLE,
        compiler_params=room(16),
        name="up",
    )(mid_low, w_up, biases)


def column_sum(values):
    return jnp.sum(values, axis=0, keepdims=True)


def turn_kernel(
    a0_ref, a1_ref, w0_ref, w1_ref, normed_ref, rows_ref, d_out_ref,
    out_ref, d_second_ref, low_ref, sums_ref, acc_ref,
):
    step = pl.program_id(0)
    rows = out_ref.shape[0]
    sums_of = pl.num_programs(0) - acc_ref.shape[0] // rows

    def products():
        return dot(a0_ref[...], w0_ref[...]) + dot(a1_ref[...], w1_ref[...])

    @pl.when(step == 0)
    def _():
        acc_ref[...] = products()
        sums_ref[...] = jnp.zeros_like(sums_ref)

    @pl.when((step > 0) & (step < sums_of))
    def _():
        acc_ref[...] += products()

    @pl.when(step >= sums_of)
    def _():
        gain1, bias1, b_down, gain, bias = [rows_ref[j : j + 1, :] for j in range(1, 6)]
        first = (step - sums_of) * rows
        for start in range(0, rows, 64):
            here = slice(start, start + 64)
            acc = acc_ref[pl.ds(pl.multiple_of(first + start, 64), 64), :]
            second = normed_ref[here, :] * gain1 + bias1 + acc + b_down
            final, normed, rstd = layer_norm(second, gain, bias)
            out_ref[here, :] = final.astype(jnp.bfloat16)
            upstream = d_out_ref[here, :].astype(jnp.float32)
            d_second = norm_back(upstream, normed, rstd, gain)
            d_second_ref[here, :] = d_second
            low_ref[here, :] = d_second.astype(jnp.bfloat16)
            parts = (column_sum(upstream * normed), column_sum(upstream), column_sum(d_second))
            for j in range(3):
                sums_ref[j : j + 1, :] += parts[j]


def turn_back(activ, w_down, normed_one, vectors, d_out):
    tokens, units = activ[0].shape
    width = w_down[0].shape[1]
    columns, rows = 512, 128
    steps = units // columns
    wide = pl.BlockSpec((rows, width), lambda i: (jnp.maximum(i - steps, 0), 0))
    act = pl.BlockSpec((tokens, columns), lambda i: (0, jnp.minimum(i, steps - 1)))
    weight = pl.BlockSpec((columns, width), lambda i: (jnp.minimum(i, steps - 1), 0))
    return pl.pallas_call(
        turn_kernel,
        grid=(steps + tokens // rows,),
        in_specs=[act, act, weight, weight, wide, fixed(vectors.shape), wide],
        out_specs=[wide, wide, wide, fixed((8, width))],
        out_shape=[
            like((tokens, width)),
            like((tokens, width), jnp.float32),
            like((tokens, width)),
            like((8, width), jnp.float32),
        ],
        scratch_shapes=[pltpu.VMEM((tokens, width), jnp.float32)],
        cost_estimate=LITTLE,
        compiler_params=room(30),
        name="turn_back",
    )(*activ, *w_down, normed_one, vectors, d_out)


def grad_kernel(at_ref, left_ref, right_ref, *refs):
    right = right_ref[...] if len(right_ref.shape) == 2 else right_ref[0]
    out = contract_rows(left_ref[...], right)
    if len(refs) == 2:
        out = out + refs[0][...].astype(jnp.float32)
    refs[-1][...] = out.astype(jnp.bfloat16)


def weight_grad(at, left, right, start, rows, sent=None, which=None):
    tokens = left.shape[0]
    columns = right.shape[1]
    count = rows if which is None else rows // 2
    which = which or (lambda p: 0)
    take = min(count, 2**19 // columns)
    steps = count // take
    first = start // take
    assert start % take == 0 and count % take == 0
    return pl.pallas_call(
        grad_kernel,
        grid_spec=pltpu.PrefetchScalarGridSpec(
            num_scalar_prefetch=1,
            grid=(steps,),
            in_specs=[
                pl.BlockSpec((tokens, take), lambda i, p: (0, first + which(p) * steps + i)),
                pl.BlockSpec((tokens, columns), lambda i, p: (0, 0)),
            ]
            + [pl.BlockSpec((take, columns), lambda i, p: (first + which(p) * steps + i, 0))]
            * (sent is not None),
            out_specs=pl.BlockSpec((take, columns), lambda i, p: (i, 0)),
        ),
        out_shape=like((count, columns)),
        cost_estimate=LITTLE,
        compiler_params=room(12),
        name="weight_grad",
    )(at, left, right, *(() if sent is None else (sent,)))


def heads_grad(at, left, right, sent=None, which=None):
    tokens, rows = left.shape
    kinds, _, columns = right.shape
    count = rows if which is None else rows // 2
    parts = rows // count
    which = which or (lambda p: 0)
    return pl.pallas_call(
        grad_kernel,
        grid_spec=pltpu.PrefetchScalarGridSpec(
            num_scalar_prefetch=1,
            grid=(kinds,),
            in_specs=[
                pl.BlockSpec((tokens, count), lambda i, p: (0, which(p))),
                pl.BlockSpec((1, tokens, columns), lambda i, p: (i, 0, 0)),
            ]
            + [pl.BlockSpec((count, columns), lambda i, p: (i * parts + which(p), 0))]
            * (sent is not None),
            out_specs=pl.BlockSpec((count, columns), lambda i, p: (i, 0)),
        ),
        out_shape=like((kinds * count, columns)),
        cost_estimate=LITTLE,
        compiler_params=room(12),
        name="heads_grad",
    )(at, left, right, *(() if sent is None else (sent,)))


def combine_kernel(count, at_ref, *refs):
    terms = refs[:count]
    out = terms[0][...].astype(jnp.float32)
    for term in terms[1:]:
        out = out + term[...].astype(jnp.float32)
    refs[-1][...] = out.astype(refs[-1].dtype)


def combine(at, terms, rows, kind=jnp.bfloat16, slab=None, slabs=1, into=None):
    columns = terms[0][0].shape[1]
    blocks = 1
    while rows * columns // blocks > 2**19 or rows % blocks:
        blocks += 1
    take = rows // blocks
    slab = slab or (lambda p: 0)

    def spec(number):
        return pl.BlockSpec((take, columns), lambda i, p: (number(p) * blocks + i, 0))

    extra = [] if into is None else [into]
    return pl.pallas_call(
        functools.partial(combine_kernel, len(terms)),
        grid_spec=pltpu.PrefetchScalarGridSpec(
            num_scalar_prefetch=1,
            grid=(blocks,),
            in_specs=[spec(number) for _, number in terms]
            + [pl.BlockSpec(memory_space=pl.ANY) for _ in extra],
            out_specs=spec(slab),
        ),
        out_shape=like((rows * slabs, columns), kind),
        input_output_aliases={} if into is None else {1 + len(terms): 0},
        cost_estimate=LITTLE,
        compiler_params=room(10),
        name="combine",
    )(at, *[array for array, _ in terms], *extra)


def whole(p):
    return 0


def spread_kernel(count, at_ref, *refs):
    for j in range(count):
        refs[j - count][...] = refs[j][...].astype(jnp.float32)


def spread(at, values, count, slab, into):
    rows, columns = values.shape[0] // count, values.shape[1]
    extra = into or ()
    run = lambda j: pl.BlockSpec((rows, columns), lambda i, p: (j, 0))
    return pl.pallas_call(
        functools.partial(spread_kernel, count),
        grid_spec=pltpu.PrefetchScalarGridSpec(
            num_scalar_prefetch=1,
            grid=(1,),
            in_specs=[run(j) for j in range(count)]
            + [pl.BlockSpec(memory_space=pl.ANY) for _ in extra],
            out_specs=[pl.BlockSpec((rows, columns), lambda i, p: (slab(p), 0))] * count,
        ),
        out_shape=[like((2 * rows, columns), jnp.float32)] * count,
        input_output_aliases={1 + count + j: j for j in range(len(extra))},
        cost_estimate=LITTLE,
        compiler_params=room(16),
        name="spread",
    )(at, *[values] * count, *extra)


def pre_kernel(low_ref, w_ref, slope_ref, out_ref, sums_ref):
    d_pre = (contract_last(low_ref[...], w_ref[...]) * slope_ref[...].astype(jnp.float32)).astype(
        jnp.bfloat16
    )
    out_ref[...] = d_pre
    sums_ref[...] = column_sum(d_pre.astype(jnp.float32))


def pre_back(second_low, w_down, slope):
    tokens, width = second_low.shape
    units = w_down.shape[0]
    columns = 512
    out = pl.BlockSpec((tokens, columns), lambda i: (0, i))
    return pl.pallas_call(
        pre_kernel,
        grid=(units // columns,),
        in_specs=[fixed((tokens, width)), pl.BlockSpec((columns, width), lambda i: (i, 0)), out],
        out_specs=[out, pl.BlockSpec((1, columns), lambda i: (0, i))],
        out_shape=[like((tokens, units)), like((1, units), jnp.float32)],
        cost_estimate=LITTLE,
        compiler_params=room(14),
        name="pre_back",
    )(second_low, w_down, slope)


def mid_kernel(
    p0_ref, p1_ref, w0_ref, w1_ref, d_second_ref, normed_ref, rstd_ref, rows_ref,
    resid_ref, low_ref, sums_ref, acc_ref,
):
    step = pl.program_id(0)
    rows = low_ref.shape[0]
    sums_of = pl.num_programs(0) - acc_ref.shape[0] // rows

    def products():
        return contract_last(p0_ref[...], w0_ref[...]) + contract_last(p1_ref[...], w1_ref[...])

    @pl.when(step == 0)
    def _():
        acc_ref[...] = products()
        sums_ref[...] = jnp.zeros_like(sums_ref)

    @pl.when((step > 0) & (step < sums_of))
    def _():
        acc_ref[...] += products()

    @pl.when(step >= sums_of)
    def _():
        gain = rows_ref[1:2, :]
        first = (step - sums_of) * rows
        for start in range(0, rows, 64):
            here = slice(start, start + 64)
            acc = acc_ref[pl.ds(pl.multiple_of(first + start, 64), 64), :]
            d_mid = d_second_ref[here, :] + acc
            normed = normed_ref[here, :]
            d_resid = norm_back(d_mid, normed, rstd_ref[here, :], gain)
            resid_ref[here, :] = d_resid
            low_ref[here, :] = d_resid.astype(jnp.bfloat16)
            parts = (column_sum(d_resid), column_sum(d_mid * normed), column_sum(d_mid))
            for j in range(3):
                sums_ref[j : j + 1, :] += parts[j]


def mid_back(d_pre, w_up, d_second, normed, rstd, vectors):
    tokens, units = d_pre[0].shape
    width = w_up[0].shape[0]
    columns, rows = 512, 128
    steps = units // columns
    wide = pl.BlockSpec((rows, width), lambda i: (jnp.maximum(i - steps, 0), 0))
    part = pl.BlockSpec((tokens, columns), lambda i: (0, jnp.minimum(i, steps - 1)))
    weight = pl.BlockSpec((width, columns), lambda i: (0, jnp.minimum(i, steps - 1)))
    return pl.pallas_call(
        mid_kernel,
        grid=(steps + tokens // rows,),
        in_specs=[
            part, part, weight, weight, wide, wide,
            pl.BlockSpec((rows, 1), lambda i: (jnp.maximum(i - steps, 0), 0)), fixed(vectors.shape),
        ],
        out_specs=[wide, wide, fixed((8, width))],
        out_shape=[
            like((tokens, width), jnp.float32),
            like((tokens, width)),
            like((8, width), jnp.float32),
        ],
        scratch_shapes=[pltpu.VMEM((tokens, width), jnp.float32)],
        cost_estimate=LITTLE,
        compiler_params=room(30),
        name="mid_back",
    )(*d_pre, *w_up, d_second, normed, rstd, vectors)


def attend_back_kernel(qkv_ref, context_ref, weights_ref, low_ref, w_ref, out_ref, sums_ref):
    factor = HDIM ** (-0.5)
    queries, keys, values = qkv_ref[0], qkv_ref[1], qkv_ref[2]
    d_context = contract_last(low_ref[...], w_ref[...]).astype(jnp.bfloat16)
    product = d_context.astype(jnp.float32) * context_ref[...].astype(jnp.float32)
    grads = None
    for head in range(2):
        d_head = pick(d_context, head)
        d_weights = contract_last(d_head, values)
        inner = jnp.sum(pick(product, head), axis=-1, keepdims=True)
        weights = weights_ref[head]
        d_scores = (weights.astype(jnp.float32) * (d_weights - inner)).astype(jnp.bfloat16)
        parts = (
            dot(d_scores, pick(keys, head)),
            contract_rows(d_scores, pick(queries, head)),
            contract_rows(weights, d_head),
        )
        grads = parts if grads is None else tuple(a + b for a, b in zip(grads, parts))
    for j, scale in enumerate((factor, factor, 1.0)):
        grad = (grads[j] * scale).astype(jnp.bfloat16)
        out_ref[j] = grad
        sums_ref[j : j + 1, :] = column_sum(grad.astype(jnp.float32))


def attend_back_heads(qkv, context, weights, resid_low, w_out):
    _, tokens, width = qkv.shape
    depth = resid_low.shape[1]
    pair = 2 * HDIM
    block = pl.BlockSpec((3, tokens, pair), lambda i: (0, 0, i))
    return pl.pallas_call(
        attend_back_kernel,
        grid=(width // pair,),
        in_specs=[
            block,
            pl.BlockSpec((tokens, pair), lambda i: (0, i)),
            pl.BlockSpec((2, tokens, tokens), lambda i: (i, 0, 0)),
            fixed((tokens, depth)),
            pl.BlockSpec((pair, depth), lambda i: (i, 0)),
        ],
        out_specs=[block, pl.BlockSpec((8, pair), lambda i: (0, i))],
        out_shape=[like((3, tokens, width)), like((8, width), jnp.float32)],
        cost_estimate=LITTLE,
        compiler_params=room(16),
        name="attend_back",
    )(qkv, context, weights, resid_low, w_out)


def gather_kernel(h0_ref, h1_ref, p0_ref, p1_ref, mid_ref, second_ref, own_ref, other_ref):
    width = own_ref.shape[1]
    part = h0_ref.shape[1]
    for h_ref, p_ref, out_ref in ((h0_ref, p0_ref, own_ref), (h1_ref, p1_ref, other_ref)):
        out_ref[...] = jnp.zeros_like(out_ref)
        out_ref[0:1, :part] = h_ref[0:1, :]
        out_ref[0:1, part : 2 * part] = h_ref[2:3, :]
        for j in range(p_ref.shape[1] // width):
            out_ref[1 + j : 2 + j, :] = p_ref[:, j * width : (j + 1) * width]
        out_ref[8:11, :] = mid_ref[0:3, :]
        out_ref[11:14, :] = second_ref[0:3, :]


def gather_sums(heads, pre, mid, second):
    out = like((16, mid.shape[1]), jnp.float32)
    return pl.pallas_call(
        gather_kernel,
        out_shape=[out, out],
        cost_estimate=LITTLE,
        compiler_params=room(4),
        name="gather_sums",
    )(*heads, *pre, mid, second)


def last_kernel(d0_ref, d1_ref, *refs):
    resid_ref, out_ref = refs[6:]
    out = resid_ref[...]
    for j in range(3):
        out = out + (
            contract_last(d0_ref[j], refs[2 * j][...]) + contract_last(d1_ref[j], refs[2 * j + 1][...])
        )
    out_ref[...] = out


def last_back(d_heads, w_query, w_key, w_value, d_resid):
    tokens, width = d_resid.shape
    part = d_heads[0].shape[2]
    columns = 256
    heads = fixed((3, tokens, part))
    wide = pl.BlockSpec((tokens, columns), lambda i: (0, i))
    weight = pl.BlockSpec((columns, part), lambda i: (i, 0))
    return pl.pallas_call(
        last_kernel,
        grid=(width // columns,),
        in_specs=[heads, heads] + [weight] * 6 + [wide],
        out_specs=wide,
        out_shape=like((tokens, width), jnp.float32),
        cost_estimate=LITTLE,
        compiler_params=room(16),
        name="last_back",
    )(*d_heads, *w_query, *w_key, *w_value, d_resid)


def move(values, target):
    pairs = []
    for z in range(4):
        for y in range(2):
            for x in range(2):
                for core in range(2):
                    there = target(x, y, z, core)
                    if there is not None:
                        tx, ty, tz, tcore = there
                        pairs.append(
                            ((z * 4 + y * 2 + x) * 2 + core, (tz * 4 + ty * 2 + tx) * 2 + tcore)
                        )
    return lax.ppermute(values, ("batch", "mp"), pairs)


def swap_core(values):
    return move(values, lambda x, y, z, core: (x, y, z, 1 - core))


def turn(x, y, z, core, along):
    return (1 - x, y, z, core) if along == 0 else (x, 1 - y, z, core)


def swap_first(values):
    return move(values, lambda x, y, z, core: turn(x, y, z, core, core))


def swap_second(values):
    return move(values, lambda x, y, z, core: turn(x, y, z, core, 1 - core))


def swap_near(values):
    return move(values, lambda x, y, z, core: (x, y, z ^ 1, core))


def swap_far(values):
    return move(values, lambda x, y, z, core: (x, y, 3 - z, core))


def placement():
    batch, core = lax.axis_index("batch"), lax.axis_index("mp")
    x, y, z = batch % 2, batch // 2 % 2, batch // 4
    first, second = jnp.where(core == 0, x, y), jnp.where(core == 0, y, x)
    near = jnp.where((z == 1) | (z == 2), 1, 0)
    return jnp.stack([first, second, near, z // 2, core]).astype(jnp.int32)


PLANE_FIRST = ((0, swap_first), (1, swap_second), (2, swap_near), (3, swap_far))
LINE_FIRST = ((2, swap_near), (3, swap_far), (0, swap_first), (1, swap_second))


ORDER = (
    "down", "pre", "up", "D", "pre", "mid", "out", "U", "O", "D", "D", "attn", "O", "O",
    "heads", "U", "U", "attn", "small", "U", "O", "H", "H", "U", "D", "O", "small", "U",
    "H", "D", "U", "H", "U", "O", "small", "small", "H", "O", "D", "D", "H", "H", "D",
    "U", "H", "small", "small", "O", "last", "D", "O", "H",
)


class Line:
    def __init__(self):
        self.last = ()

    def after(self, *values):
        tied = lax.optimization_barrier((values, self.last))[0]
        return tied[0] if len(values) == 1 else tied

    def did(self, *results):
        self.last = results
        return results[0] if len(results) == 1 else results


def sum_chips(line, at, order, make, finish):
    (a, move_a), (b, move_b), (c, move_c), (_, move_d) = order
    mine = lambda k: lambda p: p[k]
    theirs = lambda k: lambda p: 1 - p[k]
    got_a = move_a(make(theirs(a)))
    yield
    half = make(mine(a))
    yield
    half, got_a = line.after(half, got_a)
    rows = half.shape[0] // 2
    got_b = move_b(line.did(combine(at, [(half, theirs(b)), (got_a, theirs(b))], rows)))
    yield
    got_b = line.after(got_b)
    rows //= 2
    there = lambda p: 2 * p[b] + 1 - p[c]
    here = lambda p: 2 * p[b] + p[c]
    got_c = move_c(line.did(combine(at, [(half, there), (got_a, there), (got_b, theirs(c))], rows)))
    yield
    got_c = line.after(got_c)
    part = line.did(combine(at, [(half, here), (got_a, here), (got_b, mine(c)), (got_c, whole)], rows))
    got_d = move_d(part)
    yield
    part, got_d = line.after(part, got_d)
    part = line.did(combine(at, [(part, whole), (got_d, whole)], rows))
    got_c = move_c(part)
    quarter = line.did(combine(at, [(part, whole)], rows, slab=mine(c), slabs=2))
    yield
    quarter, got_c = line.after(quarter, got_c)
    quarter = line.did(combine(at, [(got_c, whole)], rows, slab=theirs(c), slabs=2, into=quarter))
    got_b = move_b(quarter)
    half = line.did(combine(at, [(quarter, whole)], 2 * rows, slab=mine(b), slabs=2))
    yield
    half, got_b = line.after(half, got_b)
    half = line.did(combine(at, [(got_b, whole)], 2 * rows, slab=theirs(b), slabs=2, into=half))
    got_a = move_a(half)
    out = line.did(finish(half, mine(a), None))
    yield
    got_a = line.after(got_a)
    line.did(finish(got_a, theirs(a), out))
    yield


def sum_small(line, values):
    for move_on in (swap_first, swap_second, swap_near, swap_far):
        values = line.did(line.after(values))
        got = move_on(values)
        yield
        values, got = line.after(values, got)
        values = line.did(values + got)
    return values


def shards_paged(
    hidden,
    cell_ids,
    boxes,
    x_table,
    y_table,
    w_query,
    b_query,
    w_key,
    w_value,
    b_value,
    w_out,
    b_out,
    ln1_gain,
    ln1_bias,
    w_up,
    b_up,
    w_down,
    b_down,
    ln2_gain,
    ln2_bias,
    d_out,
):
    at = placement()
    page = lax.axis_index("mp").reshape(1)
    line = Line()
    split = jnp.concatenate([b_query, b_value, b_up])
    part = b_query.shape[0]
    split = (split, line.did(swap_core(split)))
    hidden = line.after(hidden)
    split = [v.astype(jnp.float32).reshape(-1, part) for v in split]
    rows = jnp.concatenate([b_out, ln1_gain, ln1_bias, b_down, ln2_gain, ln2_bias])
    rows = rows.astype(jnp.float32).reshape(6, -1)
    x_table, y_table, hidden, d_out = [stay(v) for v in (x_table, y_table, hidden, d_out)]
    w_query, w_key, w_value = [(stay(w), stay(swap_core(w))) for w in (w_query, w_key, w_value)]
    both = (0, 1)

    inputs, x_low = embed(page, cell_ids, boxes, x_table, y_table, hidden)
    attended = [attend_heads(x_low, w_query[i], w_key[i], w_value[i], split[i]) for i in both]
    qkv, context, weights = zip(*attended)
    line.did(x_low, w_query[1], w_key[1], w_value[1])
    w_out, w_up, w_down = [
        (stay(w), stay(swap_core(line.after(w)))) for w in (w_out, w_up, w_down)
    ]
    mid_low, normed_one, rstd_one = resid_norm(inputs, context, w_out, rows)
    activ, slope = zip(*[up(mid_low, w_up[i], split[i]) for i in both])
    layer_out, d_second, second_low, second_sums = turn_back(
        activ, w_down, normed_one, rows, d_out
    )
    line.did(second_low)
    found = {"d_pre": {}, "pre sums": {}, "heads": {}, "heads sums": {}}

    def grads(name, product, left, right):
        found[name] = swap_core(line.did(product(line.after(left(1)), right(1))))
        yield

    def halves(name, product, left, right):
        def make(which):
            mine, sent = line.after(left(0), found[name])
            return line.did(product(mine, right(0), sent, which))

        return make

    def pre_steps():
        for i in (1, 0):
            low = line.after(second_low)
            found["d_pre"][i], found["pre sums"][i] = pre_back(low, w_down[i], slope[i])
            line.did(found["d_pre"][i])
            yield

    def mid_steps():
        d_pre = [found["d_pre"][i] for i in both]
        d_pre[0] = line.after(d_pre[0])
        found["d_resid"], found["resid_low"], found["mid sums"] = mid_back(
            d_pre, w_up, d_second, normed_one, rstd_one, rows
        )
        line.did(found["resid_low"])
        yield

    def attend_steps():
        for i in (1, 0):
            low = line.after(found["resid_low"])
            found["heads"][i], found["heads sums"][i] = attend_back_heads(
                qkv[i], context[i], weights[i], low, w_out[i]
            )
            line.did(found["heads"][i])
            yield

    def last_steps():
        d_heads = [found["heads"][i] for i in both]
        d_heads[0] = line.after(d_heads[0])
        found["d_hidden"] = line.did(
            last_back(d_heads, w_query, w_key, w_value, found["d_resid"])
        )
        yield

    def small_steps():
        own, other = line.did(
            gather_sums(
                [line.after(found["heads sums"][i]) for i in both],
                [found["pre sums"][i] for i in both],
                found["mid sums"],
                second_sums,
            )
        )
        got = swap_core(other)
        yield
        own, got = line.after(own, got)
        found["small"] = yield from sum_small(line, own + got)
        line.did(found["small"])
        yield

    def store(name):
        def finish(values, slab, into):
            rows = values.shape[0]
            found[name] = combine(
                at, [(values, whole)], rows, kind=jnp.float32, slab=slab, slabs=2, into=into
            )
            return found[name]

        return finish

    def store_heads(values, slab, into):
        found["heads grads"] = tuple(spread(at, values, 3, slab, into))
        return found["heads grads"]

    units, depth = activ[0].shape[1], mid_low.shape[1]
    second_of = lambda i: second_low
    mid_of = lambda i: mid_low
    pre_of = lambda i: found["d_pre"][i]
    resid_of = lambda i: found["resid_low"]
    activ_of = lambda i: activ[i]
    context_of = lambda i: context[i]
    x_of = lambda i: x_low
    heads_of = lambda i: found["heads"][i]

    def span(start, rows):
        def product(left, right, sent=None, which=None):
            return weight_grad(at, left, right, start, rows, sent, which)

        return product

    def heads_product(left, right, sent=None, which=None):
        return heads_grad(at, left, right, sent, which)

    cut = depth * 3 // 4
    steps = {
        "down": grads("down", span(0, units), activ_of, second_of),
        "pre": pre_steps(),
        "up": grads("up", span(0, depth), mid_of, pre_of),
        "mid": mid_steps(),
        "out": grads("out", span(0, context[0].shape[1]), context_of, resid_of),
        "attn": attend_steps(),
        "heads": grads("qkv", heads_product, x_of, heads_of),
        "last": last_steps(),
        "small": small_steps(),
    }
    chunks = {
        "D": (PLANE_FIRST, lambda: halves("down", span(0, units), activ_of, second_of), store("grad down")),
        "U": (PLANE_FIRST, lambda: halves("up", span(0, depth), mid_of, pre_of), store("grad up")),
        "O": (LINE_FIRST, lambda: halves("out", span(0, context[0].shape[1]), context_of, resid_of), store("grad out")),
        "H": (PLANE_FIRST, lambda: halves("qkv", heads_product, x_of, heads_of), store_heads),
    }
    for name in ORDER:
        if name not in steps:
            order, make, finish = chunks[name]
            steps[name] = sum_chips(line, at, order, make(), finish)
        next(steps[name])
    d_hidden = found["d_hidden"]
    grad_w_down, grad_w_up, grad_w_out = [found["grad " + n] for n in ("down", "up", "out")]
    grad_w_query, grad_w_key, grad_w_value = found["heads grads"]
    small = found["small"]
    grad_b_query, grad_b_value = small[0, :part], small[0, part : 2 * part]
    grad_b_up = small[1 : 1 + units // depth].reshape(-1)
    grad_b_out, grad_ln1_gain, grad_ln1_bias, grad_ln2_gain, grad_ln2_bias, grad_b_down = [
        small[j] for j in range(8, 14)
    ]
    return (
        layer_out,
        d_hidden,
        grad_w_query,
        grad_b_query,
        grad_w_key,
        grad_w_value,
        grad_b_value,
        grad_w_out,
        grad_b_out,
        grad_ln1_gain,
        grad_ln1_bias,
        grad_w_up,
        grad_b_up,
        grad_w_down,
        grad_b_down,
        grad_ln2_gain,
        grad_ln2_bias,
    )


def solution(mesh):
    in_specs = (
        P(("batch", "mp"), None),
        P("batch", None),
        P("batch", None, None),
        P(),
        P(),
        P(None, "mp"),
        P("mp"),
        P(None, "mp"),
        P(None, "mp"),
        P("mp"),
        P("mp", None),
        P(),
        P(),
        P(),
        P(None, "mp"),
        P("mp"),
        P("mp", None),
        P(),
        P(),
        P(),
        P(("batch", "mp"), None),
    )
    out_specs = (
        P(("batch", "mp"), None),
        P(("batch", "mp"), None),
        P(None, "mp"),
        P("mp"),
        P(None, "mp"),
        P(None, "mp"),
        P("mp"),
        P("mp", None),
        P(),
        P(),
        P(),
        P(None, "mp"),
        P("mp"),
        P("mp", None),
        P(),
        P(),
        P(),
    )
    paged = mesh.shape["mp"] == 2 and mesh.shape["batch"] == 16
    shards = shards_paged if paged else shards_general
    return jax.shard_map(shards, mesh=mesh, in_specs=in_specs, out_specs=out_specs, check_vma=False)
```

```python
import functools

import jax
import jax.numpy as jnp
from jax import lax
from jax.experimental import pallas as pl
from jax.experimental.pallas import tpu as pltpu
from jax.sharding import PartitionSpec as P

HDIM = 64
PAGE_LEN = 512
CELLS = 128


def contract_rows(left, right):
    return lax.dot_general(
        left, right, (((0,), (0,)), ((), ())), preferred_element_type=jnp.float32
    )


def contract_last(left, right):
    return lax.dot_general(
        left, right, (((1,), (1,)), ((), ())), preferred_element_type=jnp.float32
    )


def layer_norm(values, gain, shift):
    average = jnp.mean(values, axis=-1, keepdims=True)
    centred = values - average
    rstd_rows = lax.rsqrt(jnp.mean(centred * centred, axis=-1, keepdims=True) + 1e-12)
    normed = centred * rstd_rows
    return (normed * gain + shift, normed, rstd_rows)


def norm_back(upstream, normed, rstd_rows, gain):
    scaled = upstream * gain
    return rstd_rows * (
        scaled
        - jnp.mean(scaled, axis=-1, keepdims=True)
        - normed * jnp.mean(scaled * normed, axis=-1, keepdims=True)
    )


def gelu_slope(values):
    return (
        0.5 * (1.0 + lax.erf(values * 0.7071067811865476))
        + values * jnp.exp(-0.5 * values * values) * 0.3989422804014327
    )


def page_scores(queries, keys_page):
    return jnp.einsum(
        "qhd,khd->hqk", queries, keys_page, preferred_element_type=jnp.float32
    ) * HDIM ** (-0.5)


def attend(page_block):
    queries, keys_page, values_page = page_block
    scores = page_scores(queries, keys_page)
    maximum = jnp.max(scores, axis=-1, keepdims=True)
    log_total = maximum + jnp.log(jnp.sum(jnp.exp(scores - maximum), axis=-1, keepdims=True))
    weights = jnp.exp(scores - log_total).astype(jnp.bfloat16)
    context = jnp.einsum("hqk,khd->qhd", weights, values_page, preferred_element_type=jnp.float32)
    return (context.astype(jnp.bfloat16), log_total[..., 0])


def attend_back(page_block):
    queries, keys_page, values_page, log_total, d_context = page_block
    weights = jnp.exp(page_scores(queries, keys_page) - log_total[..., None])
    d_weights = jnp.einsum(
        "qhd,khd->hqk", d_context, values_page, preferred_element_type=jnp.float32
    )
    d_values = jnp.einsum(
        "hqk,qhd->khd", weights.astype(jnp.bfloat16), d_context, preferred_element_type=jnp.float32
    )
    d_scores = (
        weights * (d_weights - jnp.sum(weights * d_weights, axis=-1, keepdims=True))
    ).astype(jnp.bfloat16)
    factor = HDIM ** (-0.5)
    d_queries = (
        jnp.einsum("hqk,khd->qhd", d_scores, keys_page, preferred_element_type=jnp.float32) * factor
    )
    d_keys = (
        jnp.einsum("hqk,qhd->khd", d_scores, queries, preferred_element_type=jnp.float32) * factor
    )
    return (
        d_queries.astype(jnp.bfloat16),
        d_keys.astype(jnp.bfloat16),
        d_values.astype(jnp.bfloat16),
    )


def shards_general(
    hidden,
    cell_ids,
    boxes,
    x_table,
    y_table,
    w_query,
    b_query,
    w_key,
    w_value,
    b_value,
    w_out,
    b_out,
    ln1_gain,
    ln1_bias,
    w_up,
    b_up,
    w_down,
    b_down,
    ln2_gain,
    ln2_bias,
    d_out,
):
    row_count = hidden.shape[0]
    width_local = w_query.shape[1]
    first_row = lax.axis_index("mp") * row_count
    own_cells = lax.dynamic_slice_in_dim(cell_ids.reshape(-1), first_row, row_count)
    page_local = (first_row + jnp.arange(row_count, dtype=jnp.int32)) // PAGE_LEN
    cell_boxes = jnp.take(boxes.reshape(-1, 4), page_local * CELLS + own_cells, axis=0)
    layout = (
        jnp.take(x_table, cell_boxes[:, 0], axis=0).astype(jnp.float32)
        + jnp.take(y_table, cell_boxes[:, 1], axis=0).astype(jnp.float32)
        + jnp.take(x_table, cell_boxes[:, 2], axis=0).astype(jnp.float32)
        + jnp.take(y_table, cell_boxes[:, 3], axis=0).astype(jnp.float32)
    )
    inputs = hidden.astype(jnp.float32) + layout
    x_all = lax.all_gather(inputs.astype(jnp.bfloat16), "mp", axis=0, tiled=True)
    queries = (
        jnp.dot(x_all, w_query, preferred_element_type=jnp.float32) + b_query.astype(jnp.float32)
    ).astype(jnp.bfloat16)
    keys_all = jnp.dot(x_all, w_key, preferred_element_type=jnp.float32).astype(jnp.bfloat16)
    values_all = (
        jnp.dot(x_all, w_value, preferred_element_type=jnp.float32) + b_value.astype(jnp.float32)
    ).astype(jnp.bfloat16)
    page_shape = (-1, PAGE_LEN, width_local // HDIM, HDIM)
    page_split = (
        queries.reshape(page_shape),
        keys_all.reshape(page_shape),
        values_all.reshape(page_shape),
    )
    context, log_total = lax.map(attend, page_split)
    context = context.reshape(-1, width_local)
    attn_rows = lax.psum_scatter(
        jnp.dot(context, w_out, preferred_element_type=jnp.float32),
        "mp",
        scatter_dimension=0,
        tiled=True,
    )
    resid = inputs + attn_rows + b_out.astype(jnp.float32)
    hidden_mid, normed_one, rstd_one = layer_norm(
        resid, ln1_gain.astype(jnp.float32), ln1_bias.astype(jnp.float32)
    )
    mid_low = hidden_mid.astype(jnp.bfloat16)
    mid_all = lax.all_gather(mid_low, "mp", axis=0, tiled=True)
    pre_act = jnp.dot(mid_all, w_up, preferred_element_type=jnp.float32) + b_up.astype(jnp.float32)
    activ = jax.nn.gelu(pre_act, approximate=False).astype(jnp.bfloat16)
    ffn_rows = lax.psum_scatter(
        jnp.dot(activ, w_down, preferred_element_type=jnp.float32),
        "mp",
        scatter_dimension=0,
        tiled=True,
    )
    second = hidden_mid + ffn_rows + b_down.astype(jnp.float32)
    final, normed_two, rstd_two = layer_norm(
        second, ln2_gain.astype(jnp.float32), ln2_bias.astype(jnp.float32)
    )
    layer_out = final.astype(jnp.bfloat16)
    upstream = d_out.astype(jnp.float32)
    grad_ln2_gain = jnp.sum(upstream * normed_two, axis=0)
    grad_ln2_bias = jnp.sum(upstream, axis=0)
    d_second = norm_back(upstream, normed_two, rstd_two, ln2_gain.astype(jnp.float32))
    grad_b_down = jnp.sum(d_second, axis=0)
    second_low = d_second.astype(jnp.bfloat16)
    grads_all = lax.all_gather(second_low, "mp", axis=0, tiled=True)
    grad_w_down = contract_rows(activ, grads_all)
    d_pre = (contract_last(grads_all, w_down) * gelu_slope(pre_act)).astype(jnp.bfloat16)
    grad_w_up = contract_rows(mid_all, d_pre)
    grad_b_up = jnp.sum(d_pre.astype(jnp.float32), axis=0)
    d_mid_ffn = lax.psum_scatter(contract_last(d_pre, w_up), "mp", scatter_dimension=0, tiled=True)
    d_mid = d_second + d_mid_ffn
    grad_ln1_gain = jnp.sum(d_mid * normed_one, axis=0)
    grad_ln1_bias = jnp.sum(d_mid, axis=0)
    d_resid = norm_back(d_mid, normed_one, rstd_one, ln1_gain.astype(jnp.float32))
    grad_b_out = jnp.sum(d_resid, axis=0)
    resid_all = lax.all_gather(d_resid.astype(jnp.bfloat16), "mp", axis=0, tiled=True)
    grad_w_out = contract_rows(context, resid_all)
    d_context = contract_last(resid_all, w_out).astype(jnp.bfloat16).reshape(page_shape)
    d_queries, d_keys, d_values = lax.map(attend_back, page_split + (log_total, d_context))
    d_queries = d_queries.reshape(-1, width_local)
    d_keys = d_keys.reshape(-1, width_local)
    d_values = d_values.reshape(-1, width_local)
    grad_w_query = contract_rows(x_all, d_queries)
    grad_w_key = contract_rows(x_all, d_keys)
    grad_w_value = contract_rows(x_all, d_values)
    grad_b_query = jnp.sum(d_queries.astype(jnp.float32), axis=0)
    grad_b_value = jnp.sum(d_values.astype(jnp.float32), axis=0)
    d_hidden = d_resid + lax.psum_scatter(
        (
            contract_last(d_queries, w_query)
            + contract_last(d_keys, w_key)
            + contract_last(d_values, w_value)
        ).astype(jnp.bfloat16),
        "mp",
        scatter_dimension=0,
        tiled=True,
    ).astype(jnp.float32)
    (
        grad_w_query,
        grad_b_query,
        grad_w_key,
        grad_w_value,
        grad_b_value,
        grad_w_out,
        grad_w_up,
        grad_b_up,
        grad_w_down,
    ) = (
        lax.psum(grad_w_query.astype(jnp.bfloat16), "batch").astype(jnp.float32),
        lax.psum(grad_b_query.astype(jnp.bfloat16), "batch").astype(jnp.float32),
        lax.psum(grad_w_key.astype(jnp.bfloat16), "batch").astype(jnp.float32),
        lax.psum(grad_w_value.astype(jnp.bfloat16), "batch").astype(jnp.float32),
        lax.psum(grad_b_value.astype(jnp.bfloat16), "batch").astype(jnp.float32),
        lax.psum(grad_w_out.astype(jnp.bfloat16), "batch").astype(jnp.float32),
        lax.psum(grad_w_up.astype(jnp.bfloat16), "batch").astype(jnp.float32),
        lax.psum(grad_b_up.astype(jnp.bfloat16), "batch").astype(jnp.float32),
        lax.psum(grad_w_down.astype(jnp.bfloat16), "batch").astype(jnp.float32),
    )
    grad_b_out, grad_ln1_gain, grad_ln1_bias, grad_b_down, grad_ln2_gain, grad_ln2_bias = lax.psum(
        (grad_b_out, grad_ln1_gain, grad_ln1_bias, grad_b_down, grad_ln2_gain, grad_ln2_bias),
        ("batch", "mp"),
    )
    return (
        layer_out,
        d_hidden,
        grad_w_query,
        grad_b_query,
        grad_w_key,
        grad_w_value,
        grad_b_value,
        grad_w_out,
        grad_b_out,
        grad_ln1_gain,
        grad_ln1_bias,
        grad_w_up,
        grad_b_up,
        grad_w_down,
        grad_b_down,
        grad_ln2_gain,
        grad_ln2_bias,
    )


def dot(left, right):
    return jnp.dot(left, right, preferred_element_type=jnp.float32)


def fixed(shape):
    return pl.BlockSpec(shape, lambda i: (0,) * len(shape))


LITTLE = pl.CostEstimate(flops=1, transcendentals=0, bytes_accessed=1)


def room(mebibytes):
    return pltpu.CompilerParams(vmem_limit_bytes=mebibytes * 2**20)


def stay(values):
    return pltpu.with_memory_space_constraint(values, pltpu.HBM)


def row_of(ref):
    return ref[...].astype(jnp.float32).reshape(1, -1)


def part_of(row, step, columns):
    out = row[:, :columns]
    for j in range(1, row.shape[1] // columns):
        out = jnp.where(step == j, row[:, j * columns : (j + 1) * columns], out)
    return out


def like(shape, kind=jnp.bfloat16):
    return jax.ShapeDtypeStruct(shape, kind)


def embed_kernel(
    page_ref, cells_ref, boxes_ref, x_ref, y_ref, hidden_ref, inputs_ref, low_ref, counts_ref, member_ref
):
    @pl.when(pl.program_id(0) == 0)
    def _():
        page = page_ref[0]
        boxes = boxes_ref[page]
        place = lax.broadcasted_iota(jnp.int32, counts_ref.shape[1:], 1)
        for j in range(2):
            counts = (place == boxes[:, j : j + 1]).astype(jnp.float32)
            counts = counts + (place == boxes[:, j + 2 : j + 3]).astype(jnp.float32)
            counts_ref[j] = counts.astype(jnp.bfloat16)
        ids = cells_ref[pl.ds(page, 1), :]
        member = lax.broadcasted_iota(jnp.int32, member_ref.shape, 0) == ids
        member_ref[...] = member.astype(jnp.float32).astype(jnp.bfloat16)

    cells = dot(counts_ref[0], x_ref[...]) + dot(counts_ref[1], y_ref[...])
    high = cells.astype(jnp.bfloat16)
    rest = cells - high.astype(jnp.float32)
    middle = rest.astype(jnp.bfloat16)
    low = (rest - middle.astype(jnp.float32)).astype(jnp.bfloat16)
    member = member_ref[...]
    layout = (
        contract_rows(member, high) + contract_rows(member, middle) + contract_rows(member, low)
    )
    inputs = hidden_ref[...].astype(jnp.float32) + layout
    inputs_ref[...] = inputs
    low_ref[...] = inputs.astype(jnp.bfloat16)


def embed(page, cell_ids, boxes, x_table, y_table, hidden):
    tokens, width = hidden.shape
    positions = x_table.shape[0]
    columns = 256
    return pl.pallas_call(
        embed_kernel,
        grid_spec=pltpu.PrefetchScalarGridSpec(
            num_scalar_prefetch=1,
            grid=(width // columns,),
            in_specs=[
                pl.BlockSpec(cell_ids.shape, lambda i, p: (0, 0)),
                pl.BlockSpec(boxes.shape, lambda i, p: (0, 0, 0)),
                pl.BlockSpec((positions, columns), lambda i, p: (0, i)),
                pl.BlockSpec((positions, columns), lambda i, p: (0, i)),
                pl.BlockSpec((tokens, columns), lambda i, p: (0, i)),
            ],
            out_specs=[
                pl.BlockSpec((tokens, columns), lambda i, p: (0, i)),
                pl.BlockSpec((tokens, columns), lambda i, p: (0, i)),
            ],
            scratch_shapes=[
                pltpu.VMEM((2, CELLS, positions), jnp.bfloat16),
                pltpu.VMEM((CELLS, tokens), jnp.bfloat16),
            ],
        ),
        out_shape=[like((tokens, width), jnp.float32), like((tokens, width))],
        cost_estimate=LITTLE,
        compiler_params=room(16),
        name="embed",
    )(page, cell_ids, boxes, x_table, y_table, hidden)


def pick(values, head):
    lanes = lax.broadcasted_iota(jnp.int32, values.shape, 1) // HDIM
    return jnp.where(lanes == head, values, jnp.zeros_like(values))


def attend_kernel(
    x_ref, wq_ref, wk_ref, wv_ref, bq_ref, bv_ref, qkv_ref, context_ref, weights_ref
):
    rows = 512
    pair = 2 * HDIM
    factor = HDIM ** (-0.5) * 1.4426950408889634
    x = x_ref[...]
    step = pl.program_id(0)
    q = (dot(x, wq_ref[...]) + part_of(row_of(bq_ref), step, wq_ref.shape[1])).astype(jnp.bfloat16)
    k = dot(x, wk_ref[...]).astype(jnp.bfloat16)
    v = (dot(x, wv_ref[...]) + part_of(row_of(bv_ref), step, wv_ref.shape[1])).astype(jnp.bfloat16)
    qkv_ref[0] = q
    qkv_ref[1] = k
    qkv_ref[2] = v
    for start in range(0, x.shape[0], rows):
        here = slice(start, start + rows)
        for left in range(0, q.shape[1], pair):
            lanes = slice(left, left + pair)
            total = None
            for head in range(2):
                scores = contract_last(pick(q[here, lanes], head), k[:, lanes])
                maximum = jnp.max(scores, axis=-1, keepdims=True)
                powers = jnp.exp2((scores - maximum) * factor)
                weights = (powers * (1.0 / jnp.sum(powers, axis=-1, keepdims=True))).astype(
                    jnp.bfloat16
                )
                weights_ref[left // HDIM + head, here, :] = weights
                part = dot(weights, pick(v[:, lanes], head))
                total = part if total is None else total + part
            context_ref[here, lanes] = total.astype(jnp.bfloat16)


def attend_heads(x_low, w_query, w_key, w_value, b_query, b_value):
    tokens, depth = x_low.shape
    width = w_query.shape[1]
    columns = 4 * HDIM
    weight = pl.BlockSpec((depth, columns), lambda i: (0, i))
    bias = fixed(b_query.shape)
    return pl.pallas_call(
        attend_kernel,
        grid=(width // columns,),
        in_specs=[fixed((tokens, depth)), weight, weight, weight, bias, bias],
        out_specs=[
            pl.BlockSpec((3, tokens, columns), lambda i: (0, 0, i)),
            pl.BlockSpec((tokens, columns), lambda i: (0, i)),
            pl.BlockSpec((4, tokens, tokens), lambda i: (i, 0, 0)),
        ],
        out_shape=[
            pltpu.HBM((3, tokens, width), jnp.bfloat16),
            like((tokens, width)),
            pltpu.HBM((width // HDIM, tokens, tokens), jnp.bfloat16),
        ],
        cost_estimate=LITTLE,
        compiler_params=room(24),
        name="attend",
    )(x_low, w_query, w_key, w_value, b_query, b_value)


def resid_kernel(
    inputs_ref, c0_ref, c1_ref, w0_ref, w1_ref, b_ref, gain_ref, bias_ref, low_ref, normed_ref, rstd_ref
):
    resid = (
        inputs_ref[...]
        + (dot(c0_ref[...], w0_ref[...]) + dot(c1_ref[...], w1_ref[...]))
        + row_of(b_ref)
    )
    mid, normed, rstd = layer_norm(resid, row_of(gain_ref), row_of(bias_ref))
    low_ref[...] = mid.astype(jnp.bfloat16)
    normed_ref[...] = normed
    rstd_ref[...] = rstd


def resid_norm(inputs, context, w_out, b_out, gain, bias):
    tokens, width = inputs.shape
    part = context[0].shape[1]
    rows = 128
    wide = pl.BlockSpec((rows, width), lambda i: (i, 0))
    half = pl.BlockSpec((rows, part), lambda i: (i, 0))
    weight = fixed((part, width))
    return pl.pallas_call(
        resid_kernel,
        grid=(tokens // rows,),
        in_specs=[wide, half, half, weight, weight] + [fixed(b_out.shape)] * 3,
        out_specs=[wide, wide, pl.BlockSpec((rows, 1), lambda i: (i, 0))],
        out_shape=[
            like((tokens, width)),
            like((tokens, width), jnp.float32),
            like((tokens, 1), jnp.float32),
        ],
        cost_estimate=LITTLE,
        compiler_params=room(16),
        name="resid_norm",
    )(inputs, *context, *w_out, b_out, gain, bias)


def up_kernel(mid_ref, w0_ref, w1_ref, b0_ref, b1_ref, a0_ref, a1_ref, s0_ref, s1_ref):
    rows = 128
    step = pl.program_id(0)
    steps = pl.num_programs(0) // 2

    def part(w_ref, b_ref, activ_ref, slope_ref, number):
        bias = part_of(row_of(b_ref), number, w_ref.shape[1])
        for start in range(0, mid_ref.shape[0], rows):
            here = slice(start, start + rows)
            pre = dot(mid_ref[here, :], w_ref[...]) + bias
            below = 0.5 * (1.0 + lax.erf(pre * 0.7071067811865476))
            density = jnp.exp(-0.5 * pre * pre) * 0.3989422804014327
            activ_ref[here, :] = (pre * below).astype(jnp.bfloat16)
            slope_ref[here, :] = (below + pre * density).astype(jnp.bfloat16)

    @pl.when(step < steps)
    def _():
        part(w0_ref, b0_ref, a0_ref, s0_ref, step)

    @pl.when(step >= steps)
    def _():
        part(w1_ref, b1_ref, a1_ref, s1_ref, step - steps)


def up(mid_low, w_up, b_up):
    tokens, width = mid_low.shape
    units = w_up[0].shape[1]
    columns = 512
    steps = units // columns
    turns = (lambda i: jnp.minimum(i, steps - 1), lambda i: jnp.maximum(i - steps, 0))
    block = lambda rows: [pl.BlockSpec((rows, columns), lambda i, t=t: (0, t(i))) for t in turns]
    out = block(tokens)
    return pl.pallas_call(
        up_kernel,
        grid=(2 * steps,),
        in_specs=[fixed((tokens, width))] + block(width) + [fixed(b_up[0].shape)] * 2,
        out_specs=out + out,
        out_shape=[like((tokens, units))] * 4,
        cost_estimate=LITTLE,
        compiler_params=room(14),
        name="up",
    )(mid_low, *w_up, *b_up)


def column_sum(values):
    return jnp.sum(values, axis=0, keepdims=True)


def turn_kernel(
    a0_ref, a1_ref, w0_ref, w1_ref, normed_ref, gain1_ref, bias1_ref, b_ref, gain_ref, bias_ref, d_out_ref,
    out_ref, d_second_ref, low_ref, sums_ref, acc_ref,
):
    step = pl.program_id(0)
    rows = out_ref.shape[0]
    sums_of = pl.num_programs(0) - acc_ref.shape[0] // rows

    def products():
        return dot(a0_ref[...], w0_ref[...]) + dot(a1_ref[...], w1_ref[...])

    @pl.when(step == 0)
    def _():
        acc_ref[...] = products()
        sums_ref[...] = jnp.zeros_like(sums_ref)

    @pl.when((step > 0) & (step < sums_of))
    def _():
        acc_ref[...] += products()

    @pl.when(step >= sums_of)
    def _():
        gain1, bias1, b_down, gain, bias = [
            row_of(r) for r in (gain1_ref, bias1_ref, b_ref, gain_ref, bias_ref)
        ]
        first = (step - sums_of) * rows
        for start in range(0, rows, 64):
            here = slice(start, start + 64)
            acc = acc_ref[pl.ds(pl.multiple_of(first + start, 64), 64), :]
            second = normed_ref[here, :] * gain1 + bias1 + acc + b_down
            final, normed, rstd = layer_norm(second, gain, bias)
            out_ref[here, :] = final.astype(jnp.bfloat16)
            upstream = d_out_ref[here, :].astype(jnp.float32)
            d_second = norm_back(upstream, normed, rstd, gain)
            d_second_ref[here, :] = d_second
            low_ref[here, :] = d_second.astype(jnp.bfloat16)
            parts = (column_sum(upstream * normed), column_sum(upstream), column_sum(d_second))
            for j in range(3):
                sums_ref[j : j + 1, :] += parts[j]


def turn_back(activ, w_down, normed_one, vectors, d_out):
    tokens, units = activ[0].shape
    width = w_down[0].shape[1]
    columns, rows = 512, 128
    steps = units // columns
    wide = pl.BlockSpec((rows, width), lambda i: (jnp.maximum(i - steps, 0), 0))
    act = pl.BlockSpec((tokens, columns), lambda i: (0, jnp.minimum(i, steps - 1)))
    weight = pl.BlockSpec((columns, width), lambda i: (jnp.minimum(i, steps - 1), 0))
    return pl.pallas_call(
        turn_kernel,
        grid=(steps + tokens // rows,),
        in_specs=[act, act, weight, weight, wide] + [fixed(v.shape) for v in vectors] + [wide],
        out_specs=[wide, wide, wide, fixed((8, width))],
        out_shape=[
            like((tokens, width)),
            like((tokens, width), jnp.float32),
            like((tokens, width)),
            like((8, width), jnp.float32),
        ],
        scratch_shapes=[pltpu.VMEM((tokens, width), jnp.float32)],
        cost_estimate=LITTLE,
        compiler_params=room(30),
        name="turn_back",
    )(*activ, *w_down, normed_one, *vectors, d_out)


def grad_kernel(at_ref, left_ref, right_ref, *refs):
    right = right_ref[...] if len(right_ref.shape) == 2 else right_ref[0]
    out = contract_rows(left_ref[...], right)
    if len(refs) == 2:
        out = out + refs[0][...].astype(jnp.float32)
    refs[-1][...] = out.astype(jnp.bfloat16)


def weight_grad(at, left, right, start, rows, sent=None, which=None):
    tokens = left.shape[0]
    columns = right.shape[1]
    count = rows if which is None else rows // 2
    which = which or (lambda p: 0)
    take = min(count, 2**19 // columns)
    steps = count // take
    first = start // take
    assert start % take == 0 and count % take == 0
    return pl.pallas_call(
        grad_kernel,
        grid_spec=pltpu.PrefetchScalarGridSpec(
            num_scalar_prefetch=1,
            grid=(steps,),
            in_specs=[
                pl.BlockSpec((tokens, take), lambda i, p: (0, first + which(p) * steps + i)),
                pl.BlockSpec((tokens, columns), lambda i, p: (0, 0)),
            ]
            + [pl.BlockSpec((take, columns), lambda i, p: (first + which(p) * steps + i, 0))]
            * (sent is not None),
            out_specs=pl.BlockSpec((take, columns), lambda i, p: (i, 0)),
        ),
        out_shape=like((count, columns)),
        cost_estimate=LITTLE,
        compiler_params=room(12),
        name="weight_grad",
    )(at, left, right, *(() if sent is None else (sent,)))


def heads_grad(at, left, right, sent=None, which=None):
    tokens, rows = left.shape
    kinds, _, columns = right.shape
    count = rows if which is None else rows // 2
    parts = rows // count
    which = which or (lambda p: 0)
    return pl.pallas_call(
        grad_kernel,
        grid_spec=pltpu.PrefetchScalarGridSpec(
            num_scalar_prefetch=1,
            grid=(kinds,),
            in_specs=[
                pl.BlockSpec((tokens, count), lambda i, p: (0, which(p))),
                pl.BlockSpec((1, tokens, columns), lambda i, p: (i, 0, 0)),
            ]
            + [pl.BlockSpec((count, columns), lambda i, p: (i * parts + which(p), 0))]
            * (sent is not None),
            out_specs=pl.BlockSpec((count, columns), lambda i, p: (i, 0)),
        ),
        out_shape=like((kinds * count, columns)),
        cost_estimate=LITTLE,
        compiler_params=room(12),
        name="heads_grad",
    )(at, left, right, *(() if sent is None else (sent,)))


def combine_kernel(count, at_ref, *refs):
    terms = refs[:count]
    out = terms[0][...].astype(jnp.float32)
    for term in terms[1:]:
        out = out + term[...].astype(jnp.float32)
    refs[-1][...] = out.astype(refs[-1].dtype)


def combine(at, terms, rows, kind=jnp.bfloat16, slab=None, slabs=1, into=None):
    columns = terms[0][0].shape[1]
    blocks = 1
    while rows * columns // blocks > 2**19 or rows % blocks:
        blocks += 1
    take = rows // blocks
    slab = slab or (lambda p: 0)

    def spec(number):
        return pl.BlockSpec((take, columns), lambda i, p: (number(p) * blocks + i, 0))

    extra = [] if into is None else [into]
    return pl.pallas_call(
        functools.partial(combine_kernel, len(terms)),
        grid_spec=pltpu.PrefetchScalarGridSpec(
            num_scalar_prefetch=1,
            grid=(blocks,),
            in_specs=[spec(number) for _, number in terms]
            + [pl.BlockSpec(memory_space=pl.ANY) for _ in extra],
            out_specs=spec(slab),
        ),
        out_shape=like((rows * slabs, columns), kind),
        input_output_aliases={} if into is None else {1 + len(terms): 0},
        cost_estimate=LITTLE,
        compiler_params=room(10),
        name="combine",
    )(at, *[array for array, _ in terms], *extra)


def whole(p):
    return 0


def spread_kernel(count, at_ref, *refs):
    for j in range(count):
        refs[j - count][...] = refs[j][...].astype(jnp.float32)


def spread(at, values, count, slab, into):
    rows, columns = values.shape[0] // count, values.shape[1]
    extra = into or ()
    run = lambda j: pl.BlockSpec((rows, columns), lambda i, p: (j, 0))
    return pl.pallas_call(
        functools.partial(spread_kernel, count),
        grid_spec=pltpu.PrefetchScalarGridSpec(
            num_scalar_prefetch=1,
            grid=(1,),
            in_specs=[run(j) for j in range(count)]
            + [pl.BlockSpec(memory_space=pl.ANY) for _ in extra],
            out_specs=[pl.BlockSpec((rows, columns), lambda i, p: (slab(p), 0))] * count,
        ),
        out_shape=[like((2 * rows, columns), jnp.float32)] * count,
        input_output_aliases={1 + count + j: j for j in range(len(extra))},
        cost_estimate=LITTLE,
        compiler_params=room(16),
        name="spread",
    )(at, *[values] * count, *extra)


def pre_kernel(low_ref, w_ref, slope_ref, out_ref, sums_ref):
    d_pre = (contract_last(low_ref[...], w_ref[...]) * slope_ref[...].astype(jnp.float32)).astype(
        jnp.bfloat16
    )
    out_ref[...] = d_pre
    sums_ref[...] = column_sum(d_pre.astype(jnp.float32))


def pre_back(second_low, w_down, slope):
    tokens, width = second_low.shape
    units = w_down.shape[0]
    columns = 512
    out = pl.BlockSpec((tokens, columns), lambda i: (0, i))
    return pl.pallas_call(
        pre_kernel,
        grid=(units // columns,),
        in_specs=[fixed((tokens, width)), pl.BlockSpec((columns, width), lambda i: (i, 0)), out],
        out_specs=[out, pl.BlockSpec((1, columns), lambda i: (0, i))],
        out_shape=[like((tokens, units)), like((1, units), jnp.float32)],
        cost_estimate=LITTLE,
        compiler_params=room(14),
        name="pre_back",
    )(second_low, w_down, slope)


def mid_kernel(
    p0_ref, p1_ref, w0_ref, w1_ref, d_second_ref, normed_ref, rstd_ref, gain_ref,
    resid_ref, low_ref, sums_ref, acc_ref,
):
    step = pl.program_id(0)
    rows = low_ref.shape[0]
    sums_of = pl.num_programs(0) - acc_ref.shape[0] // rows

    def products():
        return contract_last(p0_ref[...], w0_ref[...]) + contract_last(p1_ref[...], w1_ref[...])

    @pl.when(step == 0)
    def _():
        acc_ref[...] = products()
        sums_ref[...] = jnp.zeros_like(sums_ref)

    @pl.when((step > 0) & (step < sums_of))
    def _():
        acc_ref[...] += products()

    @pl.when(step >= sums_of)
    def _():
        gain = row_of(gain_ref)
        first = (step - sums_of) * rows
        for start in range(0, rows, 64):
            here = slice(start, start + 64)
            acc = acc_ref[pl.ds(pl.multiple_of(first + start, 64), 64), :]
            d_mid = d_second_ref[here, :] + acc
            normed = normed_ref[here, :]
            d_resid = norm_back(d_mid, normed, rstd_ref[here, :], gain)
            resid_ref[here, :] = d_resid
            low_ref[here, :] = d_resid.astype(jnp.bfloat16)
            parts = (column_sum(d_resid), column_sum(d_mid * normed), column_sum(d_mid))
            for j in range(3):
                sums_ref[j : j + 1, :] += parts[j]


def mid_back(d_pre, w_up, d_second, normed, rstd, gain):
    tokens, units = d_pre[0].shape
    width = w_up[0].shape[0]
    columns, rows = 512, 128
    steps = units // columns
    wide = pl.BlockSpec((rows, width), lambda i: (jnp.maximum(i - steps, 0), 0))
    part = pl.BlockSpec((tokens, columns), lambda i: (0, jnp.minimum(i, steps - 1)))
    weight = pl.BlockSpec((width, columns), lambda i: (0, jnp.minimum(i, steps - 1)))
    return pl.pallas_call(
        mid_kernel,
        grid=(steps + tokens // rows,),
        in_specs=[
            part, part, weight, weight, wide, wide,
            pl.BlockSpec((rows, 1), lambda i: (jnp.maximum(i - steps, 0), 0)), fixed(gain.shape),
        ],
        out_specs=[wide, wide, fixed((8, width))],
        out_shape=[
            like((tokens, width), jnp.float32),
            like((tokens, width)),
            like((8, width), jnp.float32),
        ],
        scratch_shapes=[pltpu.VMEM((tokens, width), jnp.float32)],
        cost_estimate=LITTLE,
        compiler_params=room(30),
        name="mid_back",
    )(*d_pre, *w_up, d_second, normed, rstd, gain)


def attend_back_kernel(qkv_ref, context_ref, weights_ref, low_ref, w_ref, out_ref, sums_ref):
    factor = HDIM ** (-0.5)
    queries, keys, values = qkv_ref[0], qkv_ref[1], qkv_ref[2]
    d_context = contract_last(low_ref[...], w_ref[...]).astype(jnp.bfloat16)
    product = d_context.astype(jnp.float32) * context_ref[...].astype(jnp.float32)
    grads = None
    for head in range(2):
        d_head = pick(d_context, head)
        d_weights = contract_last(d_head, values)
        inner = jnp.sum(pick(product, head), axis=-1, keepdims=True)
        weights = weights_ref[head]
        d_scores = (weights.astype(jnp.float32) * (d_weights - inner)).astype(jnp.bfloat16)
        parts = (
            dot(d_scores, pick(keys, head)),
            contract_rows(d_scores, pick(queries, head)),
            contract_rows(weights, d_head),
        )
        grads = parts if grads is None else tuple(a + b for a, b in zip(grads, parts))
    for j, scale in enumerate((factor, factor, 1.0)):
        grad = (grads[j] * scale).astype(jnp.bfloat16)
        out_ref[j] = grad
        sums_ref[j : j + 1, :] = column_sum(grad.astype(jnp.float32))


def attend_back_heads(qkv, context, weights, resid_low, w_out):
    _, tokens, width = qkv.shape
    depth = resid_low.shape[1]
    pair = 2 * HDIM
    block = pl.BlockSpec((3, tokens, pair), lambda i: (0, 0, i))
    return pl.pallas_call(
        attend_back_kernel,
        grid=(width // pair,),
        in_specs=[
            block,
            pl.BlockSpec((tokens, pair), lambda i: (0, i)),
            pl.BlockSpec((2, tokens, tokens), lambda i: (i, 0, 0)),
            fixed((tokens, depth)),
            pl.BlockSpec((pair, depth), lambda i: (i, 0)),
        ],
        out_specs=[block, pl.BlockSpec((8, pair), lambda i: (0, i))],
        out_shape=[like((3, tokens, width)), like((8, width), jnp.float32)],
        cost_estimate=LITTLE,
        compiler_params=room(16),
        name="attend_back",
    )(qkv, context, weights, resid_low, w_out)


def gather_kernel(h0_ref, h1_ref, p0_ref, p1_ref, mid_ref, second_ref, own_ref, other_ref):
    width = own_ref.shape[1]
    part = h0_ref.shape[1]
    for h_ref, p_ref, out_ref in ((h0_ref, p0_ref, own_ref), (h1_ref, p1_ref, other_ref)):
        out_ref[...] = jnp.zeros_like(out_ref)
        out_ref[0:1, :part] = h_ref[0:1, :]
        out_ref[0:1, part : 2 * part] = h_ref[2:3, :]
        for j in range(p_ref.shape[1] // width):
            out_ref[1 + j : 2 + j, :] = p_ref[:, j * width : (j + 1) * width]
        out_ref[8:11, :] = mid_ref[0:3, :]
        out_ref[11:14, :] = second_ref[0:3, :]


def gather_sums(heads, pre, mid, second):
    out = like((16, mid.shape[1]), jnp.float32)
    return pl.pallas_call(
        gather_kernel,
        out_shape=[out, out],
        cost_estimate=LITTLE,
        compiler_params=room(4),
        name="gather_sums",
    )(*heads, *pre, mid, second)


def last_kernel(d0_ref, d1_ref, *refs):
    resid_ref, out_ref = refs[6:]
    out = resid_ref[...]
    for j in range(3):
        out = out + (
            contract_last(d0_ref[j], refs[2 * j][...]) + contract_last(d1_ref[j], refs[2 * j + 1][...])
        )
    out_ref[...] = out


def last_back(d_heads, w_query, w_key, w_value, d_resid):
    tokens, width = d_resid.shape
    part = d_heads[0].shape[2]
    columns = 256
    heads = fixed((3, tokens, part))
    wide = pl.BlockSpec((tokens, columns), lambda i: (0, i))
    weight = pl.BlockSpec((columns, part), lambda i: (i, 0))
    return pl.pallas_call(
        last_kernel,
        grid=(width // columns,),
        in_specs=[heads, heads] + [weight] * 6 + [wide],
        out_specs=wide,
        out_shape=like((tokens, width), jnp.float32),
        cost_estimate=LITTLE,
        compiler_params=room(16),
        name="last_back",
    )(*d_heads, *w_query, *w_key, *w_value, d_resid)


def move(values, target):
    pairs = []
    for z in range(4):
        for y in range(2):
            for x in range(2):
                for core in range(2):
                    there = target(x, y, z, core)
                    if there is not None:
                        tx, ty, tz, tcore = there
                        pairs.append(
                            ((z * 4 + y * 2 + x) * 2 + core, (tz * 4 + ty * 2 + tx) * 2 + tcore)
                        )
    return lax.ppermute(values, ("batch", "mp"), pairs)


def swap_core(values):
    return move(values, lambda x, y, z, core: (x, y, z, 1 - core))


def turn(x, y, z, core, along):
    return (1 - x, y, z, core) if along == 0 else (x, 1 - y, z, core)


def swap_first(values):
    return move(values, lambda x, y, z, core: turn(x, y, z, core, core))


def swap_second(values):
    return move(values, lambda x, y, z, core: turn(x, y, z, core, 1 - core))


def swap_near(values):
    return move(values, lambda x, y, z, core: (x, y, z ^ 1, core))


def swap_far(values):
    return move(values, lambda x, y, z, core: (x, y, 3 - z, core))


def placement():
    batch, core = lax.axis_index("batch"), lax.axis_index("mp")
    x, y, z = batch % 2, batch // 2 % 2, batch // 4
    first, second = jnp.where(core == 0, x, y), jnp.where(core == 0, y, x)
    near = jnp.where((z == 1) | (z == 2), 1, 0)
    return jnp.stack([first, second, near, z // 2, core]).astype(jnp.int32)


PLANE_FIRST = ((0, swap_first), (1, swap_second), (2, swap_near), (3, swap_far))
LINE_FIRST = ((2, swap_near), (3, swap_far), (0, swap_first), (1, swap_second))


ORDER = (
    "down", "pre", "up", "D", "pre", "mid", "out", "U", "O", "attn", "D", "D", "O", "O",
    "heads", "U", "U", "attn", "U", "small", "O", "H", "U", "D", "O", "U", "D", "H",
    "H", "U", "small", "H", "U", "small", "O", "O", "H", "D", "small", "D", "H", "H",
    "D", "O", "U", "small", "small", "H", "last", "D", "O", "H",
)


class Line:
    def __init__(self):
        self.last = ()

    def after(self, *values):
        tied = lax.optimization_barrier((values, self.last))[0]
        return tied[0] if len(values) == 1 else tied

    def did(self, *results):
        self.last = results
        return results[0] if len(results) == 1 else results


def sum_chips(line, at, order, make, finish):
    (a, move_a), (b, move_b), (c, move_c), (_, move_d) = order
    mine = lambda k: lambda p: p[k]
    theirs = lambda k: lambda p: 1 - p[k]
    got_a = move_a(make(theirs(a)))
    yield
    half = make(mine(a))
    yield
    half, got_a = line.after(half, got_a)
    rows = half.shape[0] // 2
    got_b = move_b(line.did(combine(at, [(half, theirs(b)), (got_a, theirs(b))], rows)))
    yield
    got_b = line.after(got_b)
    rows //= 2
    there = lambda p: 2 * p[b] + 1 - p[c]
    here = lambda p: 2 * p[b] + p[c]
    got_c = move_c(line.did(combine(at, [(half, there), (got_a, there), (got_b, theirs(c))], rows)))
    yield
    got_c = line.after(got_c)
    part = line.did(combine(at, [(half, here), (got_a, here), (got_b, mine(c)), (got_c, whole)], rows))
    got_d = move_d(part)
    yield
    part, got_d = line.after(part, got_d)
    part = line.did(combine(at, [(part, whole), (got_d, whole)], rows))
    got_c = move_c(part)
    quarter = line.did(combine(at, [(part, whole)], rows, slab=mine(c), slabs=2))
    yield
    quarter, got_c = line.after(quarter, got_c)
    quarter = line.did(combine(at, [(got_c, whole)], rows, slab=theirs(c), slabs=2, into=quarter))
    got_b = move_b(quarter)
    half = line.did(combine(at, [(quarter, whole)], 2 * rows, slab=mine(b), slabs=2))
    yield
    half, got_b = line.after(half, got_b)
    half = line.did(combine(at, [(got_b, whole)], 2 * rows, slab=theirs(b), slabs=2, into=half))
    got_a = move_a(half)
    out = line.did(finish(half, mine(a), None))
    yield
    got_a = line.after(got_a)
    line.did(finish(got_a, theirs(a), out))
    yield


def sum_small(line, values):
    for move_on in (swap_first, swap_second, swap_near, swap_far):
        values = line.did(line.after(values))
        got = move_on(values)
        yield
        values, got = line.after(values, got)
        values = line.did(values + got)
    return values


def shards_paged(
    hidden,
    cell_ids,
    boxes,
    x_table,
    y_table,
    w_query,
    b_query,
    w_key,
    w_value,
    b_value,
    w_out,
    b_out,
    ln1_gain,
    ln1_bias,
    w_up,
    b_up,
    w_down,
    b_down,
    ln2_gain,
    ln2_bias,
    d_out,
):
    at = placement()
    page = lax.axis_index("mp").reshape(1)
    line = Line()
    part = b_query.shape[0]
    b_query, b_value, b_up = [(b, swap_core(b)) for b in (b_query, b_value, b_up)]
    line.did(b_query[1], b_value[1], b_up[1])
    hidden = line.after(hidden)
    x_table, y_table, hidden, d_out = [stay(v) for v in (x_table, y_table, hidden, d_out)]
    w_query, w_key, w_value = [(stay(w), stay(swap_core(w))) for w in (w_query, w_key, w_value)]
    both = (0, 1)

    inputs, x_low = embed(page, cell_ids, boxes, x_table, y_table, hidden)
    attended = [
        attend_heads(x_low, w_query[i], w_key[i], w_value[i], b_query[i], b_value[i]) for i in both
    ]
    qkv, context, weights = zip(*attended)
    line.did(x_low, w_query[1], w_key[1], w_value[1])
    w_out, w_up, w_down = [
        (stay(w), stay(swap_core(line.after(w)))) for w in (w_out, w_up, w_down)
    ]
    mid_low, normed_one, rstd_one = resid_norm(inputs, context, w_out, b_out, ln1_gain, ln1_bias)
    raised = up(mid_low, w_up, b_up)
    activ, slope = raised[:2], raised[2:]
    layer_out, d_second, second_low, second_sums = turn_back(
        activ, w_down, normed_one, (ln1_gain, ln1_bias, b_down, ln2_gain, ln2_bias), d_out
    )
    line.did(second_low)
    found = {"d_pre": {}, "pre sums": {}, "heads": {}, "heads sums": {}}

    def grads(name, product, left, right):
        found[name] = swap_core(line.did(product(line.after(left(1)), right(1))))
        yield

    def halves(name, product, left, right):
        def make(which):
            mine, sent = line.after(left(0), found[name])
            return line.did(product(mine, right(0), sent, which))

        return make

    def pre_steps():
        for i in (1, 0):
            low = line.after(second_low)
            found["d_pre"][i], found["pre sums"][i] = pre_back(low, w_down[i], slope[i])
            line.did(found["d_pre"][i])
            yield

    def mid_steps():
        d_pre = [found["d_pre"][i] for i in both]
        d_pre[0] = line.after(d_pre[0])
        found["d_resid"], found["resid_low"], found["mid sums"] = mid_back(
            d_pre, w_up, d_second, normed_one, rstd_one, ln1_gain
        )
        line.did(found["resid_low"])
        yield

    def attend_steps():
        for i in (1, 0):
            low = line.after(found["resid_low"])
            found["heads"][i], found["heads sums"][i] = attend_back_heads(
                stay(qkv[i]), context[i], stay(weights[i]), low, w_out[i]
            )
            line.did(found["heads"][i])
            yield

    def last_steps():
        d_heads = [found["heads"][i] for i in both]
        d_heads[0] = line.after(d_heads[0])
        found["d_hidden"] = line.did(
            last_back(d_heads, w_query, w_key, w_value, found["d_resid"])
        )
        yield

    def small_steps():
        own, other = line.did(
            gather_sums(
                [line.after(found["heads sums"][i]) for i in both],
                [found["pre sums"][i] for i in both],
                found["mid sums"],
                second_sums,
            )
        )
        got = swap_core(other)
        yield
        own, got = line.after(own, got)
        found["small"] = yield from sum_small(line, own + got)
        line.did(found["small"])
        yield

    def store(name):
        def finish(values, slab, into):
            rows = values.shape[0]
            found[name] = combine(
                at, [(values, whole)], rows, kind=jnp.float32, slab=slab, slabs=2, into=into
            )
            return found[name]

        return finish

    def store_heads(values, slab, into):
        found["heads grads"] = tuple(spread(at, values, 3, slab, into))
        return found["heads grads"]

    units, depth = activ[0].shape[1], mid_low.shape[1]
    second_of = lambda i: second_low
    mid_of = lambda i: mid_low
    pre_of = lambda i: found["d_pre"][i]
    resid_of = lambda i: found["resid_low"]
    activ_of = lambda i: activ[i]
    context_of = lambda i: context[i]
    x_of = lambda i: x_low
    heads_of = lambda i: found["heads"][i]

    def span(start, rows):
        def product(left, right, sent=None, which=None):
            return weight_grad(at, left, right, start, rows, sent, which)

        return product

    def heads_product(left, right, sent=None, which=None):
        return heads_grad(at, left, right, sent, which)

    cut = depth * 3 // 4
    steps = {
        "down": grads("down", span(0, units), activ_of, second_of),
        "pre": pre_steps(),
        "up": grads("up", span(0, depth), mid_of, pre_of),
        "mid": mid_steps(),
        "out": grads("out", span(0, context[0].shape[1]), context_of, resid_of),
        "attn": attend_steps(),
        "heads": grads("qkv", heads_product, x_of, heads_of),
        "last": last_steps(),
        "small": small_steps(),
    }
    chunks = {
        "D": (PLANE_FIRST, lambda: halves("down", span(0, units), activ_of, second_of), store("grad down")),
        "U": (PLANE_FIRST, lambda: halves("up", span(0, depth), mid_of, pre_of), store("grad up")),
        "O": (LINE_FIRST, lambda: halves("out", span(0, context[0].shape[1]), context_of, resid_of), store("grad out")),
        "H": (PLANE_FIRST, lambda: halves("qkv", heads_product, x_of, heads_of), store_heads),
    }
    for name in ORDER:
        if name not in steps:
            order, make, finish = chunks[name]
            steps[name] = sum_chips(line, at, order, make(), finish)
        next(steps[name])
    d_hidden = found["d_hidden"]
    grad_w_down, grad_w_up, grad_w_out = [found["grad " + n] for n in ("down", "up", "out")]
    grad_w_query, grad_w_key, grad_w_value = found["heads grads"]
    small = found["small"]
    grad_b_query, grad_b_value = small[0, :part], small[0, part : 2 * part]
    grad_b_up = small[1 : 1 + units // depth].reshape(-1)
    grad_b_out, grad_ln1_gain, grad_ln1_bias, grad_ln2_gain, grad_ln2_bias, grad_b_down = [
        small[j] for j in range(8, 14)
    ]
    return (
        layer_out,
        d_hidden,
        grad_w_query,
        grad_b_query,
        grad_w_key,
        grad_w_value,
        grad_b_value,
        grad_w_out,
        grad_b_out,
        grad_ln1_gain,
        grad_ln1_bias,
        grad_w_up,
        grad_b_up,
        grad_w_down,
        grad_b_down,
        grad_ln2_gain,
        grad_ln2_bias,
    )


def solution(mesh):
    in_specs = (
        P(("batch", "mp"), None),
        P("batch", None),
        P("batch", None, None),
        P(),
        P(),
        P(None, "mp"),
        P("mp"),
        P(None, "mp"),
        P(None, "mp"),
        P("mp"),
        P("mp", None),
        P(),
        P(),
        P(),
        P(None, "mp"),
        P("mp"),
        P("mp", None),
        P(),
        P(),
        P(),
        P(("batch", "mp"), None),
    )
    out_specs = (
        P(("batch", "mp"), None),
        P(("batch", "mp"), None),
        P(None, "mp"),
        P("mp"),
        P(None, "mp"),
        P(None, "mp"),
        P("mp"),
        P("mp", None),
        P(),
        P(),
        P(),
        P(None, "mp"),
        P("mp"),
        P("mp", None),
        P(),
        P(),
        P(),
    )
    paged = mesh.shape["mp"] == 2 and mesh.shape["batch"] == 16
    shards = shards_paged if paged else shards_general
    return jax.shard_map(shards, mesh=mesh, in_specs=in_specs, out_specs=out_specs, check_vma=False)
```

```python
import functools

import jax
import jax.numpy as jnp
from jax import lax
from jax.experimental import pallas as pl
from jax.experimental.pallas import tpu as pltpu
from jax.sharding import PartitionSpec as P

HDIM = 64
PAGE_LEN = 512
CELLS = 128


def contract_rows(left, right):
    return lax.dot_general(
        left, right, (((0,), (0,)), ((), ())), preferred_element_type=jnp.float32
    )


def contract_last(left, right):
    return lax.dot_general(
        left, right, (((1,), (1,)), ((), ())), preferred_element_type=jnp.float32
    )


def layer_norm(values, gain, shift):
    average = jnp.mean(values, axis=-1, keepdims=True)
    centred = values - average
    rstd_rows = lax.rsqrt(jnp.mean(centred * centred, axis=-1, keepdims=True) + 1e-12)
    normed = centred * rstd_rows
    return (normed * gain + shift, normed, rstd_rows)


def norm_back(upstream, normed, rstd_rows, gain):
    scaled = upstream * gain
    return rstd_rows * (
        scaled
        - jnp.mean(scaled, axis=-1, keepdims=True)
        - normed * jnp.mean(scaled * normed, axis=-1, keepdims=True)
    )


def gelu_slope(values):
    return (
        0.5 * (1.0 + lax.erf(values * 0.7071067811865476))
        + values * jnp.exp(-0.5 * values * values) * 0.3989422804014327
    )


def page_scores(queries, keys_page):
    return jnp.einsum(
        "qhd,khd->hqk", queries, keys_page, preferred_element_type=jnp.float32
    ) * HDIM ** (-0.5)


def attend(page_block):
    queries, keys_page, values_page = page_block
    scores = page_scores(queries, keys_page)
    maximum = jnp.max(scores, axis=-1, keepdims=True)
    log_total = maximum + jnp.log(jnp.sum(jnp.exp(scores - maximum), axis=-1, keepdims=True))
    weights = jnp.exp(scores - log_total).astype(jnp.bfloat16)
    context = jnp.einsum("hqk,khd->qhd", weights, values_page, preferred_element_type=jnp.float32)
    return (context.astype(jnp.bfloat16), log_total[..., 0])


def attend_back(page_block):
    queries, keys_page, values_page, log_total, d_context = page_block
    weights = jnp.exp(page_scores(queries, keys_page) - log_total[..., None])
    d_weights = jnp.einsum(
        "qhd,khd->hqk", d_context, values_page, preferred_element_type=jnp.float32
    )
    d_values = jnp.einsum(
        "hqk,qhd->khd", weights.astype(jnp.bfloat16), d_context, preferred_element_type=jnp.float32
    )
    d_scores = (
        weights * (d_weights - jnp.sum(weights * d_weights, axis=-1, keepdims=True))
    ).astype(jnp.bfloat16)
    factor = HDIM ** (-0.5)
    d_queries = (
        jnp.einsum("hqk,khd->qhd", d_scores, keys_page, preferred_element_type=jnp.float32) * factor
    )
    d_keys = (
        jnp.einsum("hqk,qhd->khd", d_scores, queries, preferred_element_type=jnp.float32) * factor
    )
    return (
        d_queries.astype(jnp.bfloat16),
        d_keys.astype(jnp.bfloat16),
        d_values.astype(jnp.bfloat16),
    )


def shards_general(
    hidden,
    cell_ids,
    boxes,
    x_table,
    y_table,
    w_query,
    b_query,
    w_key,
    w_value,
    b_value,
    w_out,
    b_out,
    ln1_gain,
    ln1_bias,
    w_up,
    b_up,
    w_down,
    b_down,
    ln2_gain,
    ln2_bias,
    d_out,
):
    row_count = hidden.shape[0]
    width_local = w_query.shape[1]
    first_row = lax.axis_index("mp") * row_count
    own_cells = lax.dynamic_slice_in_dim(cell_ids.reshape(-1), first_row, row_count)
    page_local = (first_row + jnp.arange(row_count, dtype=jnp.int32)) // PAGE_LEN
    cell_boxes = jnp.take(boxes.reshape(-1, 4), page_local * CELLS + own_cells, axis=0)
    layout = (
        jnp.take(x_table, cell_boxes[:, 0], axis=0).astype(jnp.float32)
        + jnp.take(y_table, cell_boxes[:, 1], axis=0).astype(jnp.float32)
        + jnp.take(x_table, cell_boxes[:, 2], axis=0).astype(jnp.float32)
        + jnp.take(y_table, cell_boxes[:, 3], axis=0).astype(jnp.float32)
    )
    inputs = hidden.astype(jnp.float32) + layout
    x_all = lax.all_gather(inputs.astype(jnp.bfloat16), "mp", axis=0, tiled=True)
    queries = (
        jnp.dot(x_all, w_query, preferred_element_type=jnp.float32) + b_query.astype(jnp.float32)
    ).astype(jnp.bfloat16)
    keys_all = jnp.dot(x_all, w_key, preferred_element_type=jnp.float32).astype(jnp.bfloat16)
    values_all = (
        jnp.dot(x_all, w_value, preferred_element_type=jnp.float32) + b_value.astype(jnp.float32)
    ).astype(jnp.bfloat16)
    page_shape = (-1, PAGE_LEN, width_local // HDIM, HDIM)
    page_split = (
        queries.reshape(page_shape),
        keys_all.reshape(page_shape),
        values_all.reshape(page_shape),
    )
    context, log_total = lax.map(attend, page_split)
    context = context.reshape(-1, width_local)
    attn_rows = lax.psum_scatter(
        jnp.dot(context, w_out, preferred_element_type=jnp.float32),
        "mp",
        scatter_dimension=0,
        tiled=True,
    )
    resid = inputs + attn_rows + b_out.astype(jnp.float32)
    hidden_mid, normed_one, rstd_one = layer_norm(
        resid, ln1_gain.astype(jnp.float32), ln1_bias.astype(jnp.float32)
    )
    mid_low = hidden_mid.astype(jnp.bfloat16)
    mid_all = lax.all_gather(mid_low, "mp", axis=0, tiled=True)
    pre_act = jnp.dot(mid_all, w_up, preferred_element_type=jnp.float32) + b_up.astype(jnp.float32)
    activ = jax.nn.gelu(pre_act, approximate=False).astype(jnp.bfloat16)
    ffn_rows = lax.psum_scatter(
        jnp.dot(activ, w_down, preferred_element_type=jnp.float32),
        "mp",
        scatter_dimension=0,
        tiled=True,
    )
    second = hidden_mid + ffn_rows + b_down.astype(jnp.float32)
    final, normed_two, rstd_two = layer_norm(
        second, ln2_gain.astype(jnp.float32), ln2_bias.astype(jnp.float32)
    )
    layer_out = final.astype(jnp.bfloat16)
    upstream = d_out.astype(jnp.float32)
    grad_ln2_gain = jnp.sum(upstream * normed_two, axis=0)
    grad_ln2_bias = jnp.sum(upstream, axis=0)
    d_second = norm_back(upstream, normed_two, rstd_two, ln2_gain.astype(jnp.float32))
    grad_b_down = jnp.sum(d_second, axis=0)
    second_low = d_second.astype(jnp.bfloat16)
    grads_all = lax.all_gather(second_low, "mp", axis=0, tiled=True)
    grad_w_down = contract_rows(activ, grads_all)
    d_pre = (contract_last(grads_all, w_down) * gelu_slope(pre_act)).astype(jnp.bfloat16)
    grad_w_up = contract_rows(mid_all, d_pre)
    grad_b_up = jnp.sum(d_pre.astype(jnp.float32), axis=0)
    d_mid_ffn = lax.psum_scatter(contract_last(d_pre, w_up), "mp", scatter_dimension=0, tiled=True)
    d_mid = d_second + d_mid_ffn
    grad_ln1_gain = jnp.sum(d_mid * normed_one, axis=0)
    grad_ln1_bias = jnp.sum(d_mid, axis=0)
    d_resid = norm_back(d_mid, normed_one, rstd_one, ln1_gain.astype(jnp.float32))
    grad_b_out = jnp.sum(d_resid, axis=0)
    resid_all = lax.all_gather(d_resid.astype(jnp.bfloat16), "mp", axis=0, tiled=True)
    grad_w_out = contract_rows(context, resid_all)
    d_context = contract_last(resid_all, w_out).astype(jnp.bfloat16).reshape(page_shape)
    d_queries, d_keys, d_values = lax.map(attend_back, page_split + (log_total, d_context))
    d_queries = d_queries.reshape(-1, width_local)
    d_keys = d_keys.reshape(-1, width_local)
    d_values = d_values.reshape(-1, width_local)
    grad_w_query = contract_rows(x_all, d_queries)
    grad_w_key = contract_rows(x_all, d_keys)
    grad_w_value = contract_rows(x_all, d_values)
    grad_b_query = jnp.sum(d_queries.astype(jnp.float32), axis=0)
    grad_b_value = jnp.sum(d_values.astype(jnp.float32), axis=0)
    d_hidden = d_resid + lax.psum_scatter(
        (
            contract_last(d_queries, w_query)
            + contract_last(d_keys, w_key)
            + contract_last(d_values, w_value)
        ).astype(jnp.bfloat16),
        "mp",
        scatter_dimension=0,
        tiled=True,
    ).astype(jnp.float32)
    (
        grad_w_query,
        grad_b_query,
        grad_w_key,
        grad_w_value,
        grad_b_value,
        grad_w_out,
        grad_w_up,
        grad_b_up,
        grad_w_down,
    ) = (
        lax.psum(grad_w_query.astype(jnp.bfloat16), "batch").astype(jnp.float32),
        lax.psum(grad_b_query.astype(jnp.bfloat16), "batch").astype(jnp.float32),
        lax.psum(grad_w_key.astype(jnp.bfloat16), "batch").astype(jnp.float32),
        lax.psum(grad_w_value.astype(jnp.bfloat16), "batch").astype(jnp.float32),
        lax.psum(grad_b_value.astype(jnp.bfloat16), "batch").astype(jnp.float32),
        lax.psum(grad_w_out.astype(jnp.bfloat16), "batch").astype(jnp.float32),
        lax.psum(grad_w_up.astype(jnp.bfloat16), "batch").astype(jnp.float32),
        lax.psum(grad_b_up.astype(jnp.bfloat16), "batch").astype(jnp.float32),
        lax.psum(grad_w_down.astype(jnp.bfloat16), "batch").astype(jnp.float32),
    )
    grad_b_out, grad_ln1_gain, grad_ln1_bias, grad_b_down, grad_ln2_gain, grad_ln2_bias = lax.psum(
        (grad_b_out, grad_ln1_gain, grad_ln1_bias, grad_b_down, grad_ln2_gain, grad_ln2_bias),
        ("batch", "mp"),
    )
    return (
        layer_out,
        d_hidden,
        grad_w_query,
        grad_b_query,
        grad_w_key,
        grad_w_value,
        grad_b_value,
        grad_w_out,
        grad_b_out,
        grad_ln1_gain,
        grad_ln1_bias,
        grad_w_up,
        grad_b_up,
        grad_w_down,
        grad_b_down,
        grad_ln2_gain,
        grad_ln2_bias,
    )


def dot(left, right):
    return jnp.dot(left, right, preferred_element_type=jnp.float32)


def fixed(shape):
    return pl.BlockSpec(shape, lambda i: (0,) * len(shape))


LITTLE = pl.CostEstimate(flops=1, transcendentals=0, bytes_accessed=1)


def room(mebibytes):
    return pltpu.CompilerParams(vmem_limit_bytes=mebibytes * 2**20)


def stay(values):
    return pltpu.with_memory_space_constraint(values, pltpu.HBM)


def row_of(ref):
    return ref[...].astype(jnp.float32).reshape(1, -1)


def part_of(row, step, columns):
    out = row[:, :columns]
    for j in range(1, row.shape[1] // columns):
        out = jnp.where(step == j, row[:, j * columns : (j + 1) * columns], out)
    return out


def like(shape, kind=jnp.bfloat16):
    return jax.ShapeDtypeStruct(shape, kind)


def embed_kernel(
    page_ref, cells_ref, boxes_ref, x_ref, y_ref, hidden_ref, inputs_ref, low_ref, counts_ref, member_ref
):
    @pl.when(pl.program_id(0) == 0)
    def _():
        page = page_ref[0]
        boxes = boxes_ref[page]
        place = lax.broadcasted_iota(jnp.int32, counts_ref.shape[1:], 1)
        for j in range(2):
            counts = (place == boxes[:, j : j + 1]).astype(jnp.float32)
            counts = counts + (place == boxes[:, j + 2 : j + 3]).astype(jnp.float32)
            counts_ref[j] = counts.astype(jnp.bfloat16)
        ids = cells_ref[pl.ds(page, 1), :]
        member = lax.broadcasted_iota(jnp.int32, member_ref.shape, 0) == ids
        member_ref[...] = member.astype(jnp.float32).astype(jnp.bfloat16)

    cells = dot(counts_ref[0], x_ref[...]) + dot(counts_ref[1], y_ref[...])
    high = cells.astype(jnp.bfloat16)
    rest = cells - high.astype(jnp.float32)
    middle = rest.astype(jnp.bfloat16)
    low = (rest - middle.astype(jnp.float32)).astype(jnp.bfloat16)
    member = member_ref[...]
    layout = (
        contract_rows(member, high) + contract_rows(member, middle) + contract_rows(member, low)
    )
    inputs = hidden_ref[...].astype(jnp.float32) + layout
    inputs_ref[...] = inputs
    low_ref[...] = inputs.astype(jnp.bfloat16)


def embed(page, cell_ids, boxes, x_table, y_table, hidden):
    tokens, width = hidden.shape
    positions = x_table.shape[0]
    columns = 256
    return pl.pallas_call(
        embed_kernel,
        grid_spec=pltpu.PrefetchScalarGridSpec(
            num_scalar_prefetch=1,
            grid=(width // columns,),
            in_specs=[
                pl.BlockSpec(cell_ids.shape, lambda i, p: (0, 0)),
                pl.BlockSpec(boxes.shape, lambda i, p: (0, 0, 0)),
                pl.BlockSpec((positions, columns), lambda i, p: (0, i)),
                pl.BlockSpec((positions, columns), lambda i, p: (0, i)),
                pl.BlockSpec((tokens, columns), lambda i, p: (0, i)),
            ],
            out_specs=[
                pl.BlockSpec((tokens, columns), lambda i, p: (0, i)),
                pl.BlockSpec((tokens, columns), lambda i, p: (0, i)),
            ],
            scratch_shapes=[
                pltpu.VMEM((2, CELLS, positions), jnp.bfloat16),
                pltpu.VMEM((CELLS, tokens), jnp.bfloat16),
            ],
        ),
        out_shape=[like((tokens, width), jnp.float32), like((tokens, width))],
        cost_estimate=LITTLE,
        compiler_params=room(16),
        name="embed",
    )(page, cell_ids, boxes, x_table, y_table, hidden)


def pick(values, head):
    lanes = lax.broadcasted_iota(jnp.int32, values.shape, 1) // HDIM
    return jnp.where(lanes == head, values, jnp.zeros_like(values))


def attend_kernel(
    x_ref, wq_ref, wk_ref, wv_ref, bq_ref, bv_ref, qkv_ref, context_ref, weights_ref
):
    rows = 512
    pair = 2 * HDIM
    factor = HDIM ** (-0.5) * 1.4426950408889634
    x = x_ref[...]
    step = pl.program_id(0)
    q = (dot(x, wq_ref[...]) + part_of(row_of(bq_ref), step, wq_ref.shape[1])).astype(jnp.bfloat16)
    k = dot(x, wk_ref[...]).astype(jnp.bfloat16)
    v = (dot(x, wv_ref[...]) + part_of(row_of(bv_ref), step, wv_ref.shape[1])).astype(jnp.bfloat16)
    qkv_ref[0] = q
    qkv_ref[1] = k
    qkv_ref[2] = v
    for start in range(0, x.shape[0], rows):
        here = slice(start, start + rows)
        for left in range(0, q.shape[1], pair):
            lanes = slice(left, left + pair)
            total = None
            for head in range(2):
                scores = contract_last(pick(q[here, lanes], head), k[:, lanes])
                maximum = jnp.max(scores, axis=-1, keepdims=True)
                powers = jnp.exp2((scores - maximum) * factor)
                weights = (powers * (1.0 / jnp.sum(powers, axis=-1, keepdims=True))).astype(
                    jnp.bfloat16
                )
                weights_ref[left // HDIM + head, here, :] = weights
                part = dot(weights, pick(v[:, lanes], head))
                total = part if total is None else total + part
            context_ref[here, lanes] = total.astype(jnp.bfloat16)


def attend_heads(x_low, w_query, w_key, w_value, b_query, b_value):
    tokens, depth = x_low.shape
    width = w_query.shape[1]
    columns = 4 * HDIM
    weight = pl.BlockSpec((depth, columns), lambda i: (0, i))
    bias = fixed(b_query.shape)
    return pl.pallas_call(
        attend_kernel,
        grid=(width // columns,),
        in_specs=[fixed((tokens, depth)), weight, weight, weight, bias, bias],
        out_specs=[
            pl.BlockSpec((3, tokens, columns), lambda i: (0, 0, i)),
            pl.BlockSpec((tokens, columns), lambda i: (0, i)),
            pl.BlockSpec((4, tokens, tokens), lambda i: (i, 0, 0)),
        ],
        out_shape=[
            pltpu.HBM((3, tokens, width), jnp.bfloat16),
            like((tokens, width)),
            pltpu.HBM((width // HDIM, tokens, tokens), jnp.bfloat16),
        ],
        cost_estimate=LITTLE,
        compiler_params=room(24),
        name="attend",
    )(x_low, w_query, w_key, w_value, b_query, b_value)


def resid_kernel(
    inputs_ref, c0_ref, c1_ref, w0_ref, w1_ref, b_ref, gain_ref, bias_ref, low_ref, normed_ref, rstd_ref
):
    resid = (
        inputs_ref[...]
        + (dot(c0_ref[...], w0_ref[...]) + dot(c1_ref[...], w1_ref[...]))
        + row_of(b_ref)
    )
    mid, normed, rstd = layer_norm(resid, row_of(gain_ref), row_of(bias_ref))
    low_ref[...] = mid.astype(jnp.bfloat16)
    normed_ref[...] = normed
    rstd_ref[...] = rstd


def resid_norm(inputs, context, w_out, b_out, gain, bias):
    tokens, width = inputs.shape
    part = context[0].shape[1]
    rows = 128
    wide = pl.BlockSpec((rows, width), lambda i: (i, 0))
    half = pl.BlockSpec((rows, part), lambda i: (i, 0))
    weight = fixed((part, width))
    return pl.pallas_call(
        resid_kernel,
        grid=(tokens // rows,),
        in_specs=[wide, half, half, weight, weight] + [fixed(b_out.shape)] * 3,
        out_specs=[wide, wide, pl.BlockSpec((rows, 1), lambda i: (i, 0))],
        out_shape=[
            like((tokens, width)),
            like((tokens, width), jnp.float32),
            like((tokens, 1), jnp.float32),
        ],
        cost_estimate=LITTLE,
        compiler_params=room(16),
        name="resid_norm",
    )(inputs, *context, *w_out, b_out, gain, bias)


def up_kernel(mid_ref, w0_ref, w1_ref, b0_ref, b1_ref, a0_ref, a1_ref, s0_ref, s1_ref):
    rows = 128
    step = pl.program_id(0)
    steps = pl.num_programs(0) // 2

    def part(w_ref, b_ref, activ_ref, slope_ref, number):
        bias = part_of(row_of(b_ref), number, w_ref.shape[1])
        for start in range(0, mid_ref.shape[0], rows):
            here = slice(start, start + rows)
            pre = dot(mid_ref[here, :], w_ref[...]) + bias
            below = 0.5 * (1.0 + lax.erf(pre * 0.7071067811865476))
            density = jnp.exp(-0.5 * pre * pre) * 0.3989422804014327
            activ_ref[here, :] = (pre * below).astype(jnp.bfloat16)
            slope_ref[here, :] = (below + pre * density).astype(jnp.bfloat16)

    @pl.when(step < steps)
    def _():
        part(w0_ref, b0_ref, a0_ref, s0_ref, step)

    @pl.when(step >= steps)
    def _():
        part(w1_ref, b1_ref, a1_ref, s1_ref, step - steps)


def up(mid_low, w_up, b_up):
    tokens, width = mid_low.shape
    units = w_up[0].shape[1]
    columns = 512
    steps = units // columns
    turns = (lambda i: jnp.minimum(i, steps - 1), lambda i: jnp.maximum(i - steps, 0))
    block = lambda rows: [pl.BlockSpec((rows, columns), lambda i, t=t: (0, t(i))) for t in turns]
    out = block(tokens)
    return pl.pallas_call(
        up_kernel,
        grid=(2 * steps,),
        in_specs=[fixed((tokens, width))] + block(width) + [fixed(b_up[0].shape)] * 2,
        out_specs=out + out,
        out_shape=[like((tokens, units))] * 4,
        cost_estimate=LITTLE,
        compiler_params=room(14),
        name="up",
    )(mid_low, *w_up, *b_up)


def column_sum(values):
    return jnp.sum(values, axis=0, keepdims=True)


def turn_kernel(
    a0_ref, a1_ref, w0_ref, w1_ref, normed_ref, gain1_ref, bias1_ref, b_ref, gain_ref, bias_ref, d_out_ref,
    out_ref, d_second_ref, low_ref, sums_ref, acc_ref,
):
    step = pl.program_id(0)
    rows = out_ref.shape[0]
    sums_of = pl.num_programs(0) - acc_ref.shape[0] // rows

    def products():
        return dot(a0_ref[...], w0_ref[...]) + dot(a1_ref[...], w1_ref[...])

    @pl.when(step == 0)
    def _():
        acc_ref[...] = products()
        sums_ref[...] = jnp.zeros_like(sums_ref)

    @pl.when((step > 0) & (step < sums_of))
    def _():
        acc_ref[...] += products()

    @pl.when(step >= sums_of)
    def _():
        gain1, bias1, b_down, gain, bias = [
            row_of(r) for r in (gain1_ref, bias1_ref, b_ref, gain_ref, bias_ref)
        ]
        first = (step - sums_of) * rows
        for start in range(0, rows, 64):
            here = slice(start, start + 64)
            acc = acc_ref[pl.ds(pl.multiple_of(first + start, 64), 64), :]
            second = normed_ref[here, :] * gain1 + bias1 + acc + b_down
            final, normed, rstd = layer_norm(second, gain, bias)
            out_ref[here, :] = final.astype(jnp.bfloat16)
            upstream = d_out_ref[here, :].astype(jnp.float32)
            d_second = norm_back(upstream, normed, rstd, gain)
            d_second_ref[here, :] = d_second
            low_ref[here, :] = d_second.astype(jnp.bfloat16)
            parts = (column_sum(upstream * normed), column_sum(upstream), column_sum(d_second))
            for j in range(3):
                sums_ref[j : j + 1, :] += parts[j]


def turn_back(activ, w_down, normed_one, vectors, d_out):
    tokens, units = activ[0].shape
    width = w_down[0].shape[1]
    columns, rows = 512, 128
    steps = units // columns
    wide = pl.BlockSpec((rows, width), lambda i: (jnp.maximum(i - steps, 0), 0))
    act = pl.BlockSpec((tokens, columns), lambda i: (0, jnp.minimum(i, steps - 1)))
    weight = pl.BlockSpec((columns, width), lambda i: (jnp.minimum(i, steps - 1), 0))
    return pl.pallas_call(
        turn_kernel,
        grid=(steps + tokens // rows,),
        in_specs=[act, act, weight, weight, wide] + [fixed(v.shape) for v in vectors] + [wide],
        out_specs=[wide, wide, wide, fixed((8, width))],
        out_shape=[
            like((tokens, width)),
            like((tokens, width), jnp.float32),
            like((tokens, width)),
            like((8, width), jnp.float32),
        ],
        scratch_shapes=[pltpu.VMEM((tokens, width), jnp.float32)],
        cost_estimate=LITTLE,
        compiler_params=room(30),
        name="turn_back",
    )(*activ, *w_down, normed_one, *vectors, d_out)


def grad_kernel(at_ref, left_ref, right_ref, *refs):
    right = right_ref[...] if len(right_ref.shape) == 2 else right_ref[0]
    out = contract_rows(left_ref[...], right)
    if len(refs) == 2:
        out = out + refs[0][...].astype(jnp.float32)
    refs[-1][...] = out.astype(jnp.bfloat16)


def weight_grad(at, left, right, start, rows, sent=None, which=None):
    tokens = left.shape[0]
    columns = right.shape[1]
    count = rows if which is None else rows // 2
    which = which or (lambda p: 0)
    take = min(count, 2**19 // columns)
    steps = count // take
    first = start // take
    assert start % take == 0 and count % take == 0
    return pl.pallas_call(
        grad_kernel,
        grid_spec=pltpu.PrefetchScalarGridSpec(
            num_scalar_prefetch=1,
            grid=(steps,),
            in_specs=[
                pl.BlockSpec((tokens, take), lambda i, p: (0, first + which(p) * steps + i)),
                pl.BlockSpec((tokens, columns), lambda i, p: (0, 0)),
            ]
            + [pl.BlockSpec((take, columns), lambda i, p: (first + which(p) * steps + i, 0))]
            * (sent is not None),
            out_specs=pl.BlockSpec((take, columns), lambda i, p: (i, 0)),
        ),
        out_shape=like((count, columns)),
        cost_estimate=LITTLE,
        compiler_params=room(12),
        name="weight_grad",
    )(at, left, right, *(() if sent is None else (sent,)))


def heads_grad(at, left, right, sent=None, which=None):
    tokens, rows = left.shape
    kinds, _, columns = right.shape
    count = rows if which is None else rows // 2
    parts = rows // count
    which = which or (lambda p: 0)
    return pl.pallas_call(
        grad_kernel,
        grid_spec=pltpu.PrefetchScalarGridSpec(
            num_scalar_prefetch=1,
            grid=(kinds,),
            in_specs=[
                pl.BlockSpec((tokens, count), lambda i, p: (0, which(p))),
                pl.BlockSpec((1, tokens, columns), lambda i, p: (i, 0, 0)),
            ]
            + [pl.BlockSpec((count, columns), lambda i, p: (i * parts + which(p), 0))]
            * (sent is not None),
            out_specs=pl.BlockSpec((count, columns), lambda i, p: (i, 0)),
        ),
        out_shape=like((kinds * count, columns)),
        cost_estimate=LITTLE,
        compiler_params=room(12),
        name="heads_grad",
    )(at, left, right, *(() if sent is None else (sent,)))


def combine_kernel(count, at_ref, *refs):
    terms = refs[:count]
    out = terms[0][...].astype(jnp.float32)
    for term in terms[1:]:
        out = out + term[...].astype(jnp.float32)
    refs[-1][...] = out.astype(refs[-1].dtype)


def combine(at, terms, rows, kind=jnp.bfloat16, slab=None, slabs=1, into=None):
    columns = terms[0][0].shape[1]
    blocks = 1
    while rows * columns // blocks > 2**19 or rows % blocks:
        blocks += 1
    take = rows // blocks
    slab = slab or (lambda p: 0)

    def spec(number):
        return pl.BlockSpec((take, columns), lambda i, p: (number(p) * blocks + i, 0))

    extra = [] if into is None else [into]
    return pl.pallas_call(
        functools.partial(combine_kernel, len(terms)),
        grid_spec=pltpu.PrefetchScalarGridSpec(
            num_scalar_prefetch=1,
            grid=(blocks,),
            in_specs=[spec(number) for _, number in terms]
            + [pl.BlockSpec(memory_space=pl.ANY) for _ in extra],
            out_specs=spec(slab),
        ),
        out_shape=like((rows * slabs, columns), kind),
        input_output_aliases={} if into is None else {1 + len(terms): 0},
        cost_estimate=LITTLE,
        compiler_params=room(10),
        name="combine",
    )(at, *[array for array, _ in terms], *extra)


def whole(p):
    return 0


def spread_kernel(count, at_ref, *refs):
    for j in range(count):
        refs[j - count][...] = refs[j][...].astype(jnp.float32)


def spread(at, values, count, slab, into):
    rows, columns = values.shape[0] // count, values.shape[1]
    extra = into or ()
    run = lambda j: pl.BlockSpec((rows, columns), lambda i, p: (j, 0))
    return pl.pallas_call(
        functools.partial(spread_kernel, count),
        grid_spec=pltpu.PrefetchScalarGridSpec(
            num_scalar_prefetch=1,
            grid=(1,),
            in_specs=[run(j) for j in range(count)]
            + [pl.BlockSpec(memory_space=pl.ANY) for _ in extra],
            out_specs=[pl.BlockSpec((rows, columns), lambda i, p: (slab(p), 0))] * count,
        ),
        out_shape=[like((2 * rows, columns), jnp.float32)] * count,
        input_output_aliases={1 + count + j: j for j in range(len(extra))},
        cost_estimate=LITTLE,
        compiler_params=room(16),
        name="spread",
    )(at, *[values] * count, *extra)


def pre_kernel(low_ref, w_ref, slope_ref, out_ref, sums_ref):
    d_pre = (contract_last(low_ref[...], w_ref[...]) * slope_ref[...].astype(jnp.float32)).astype(
        jnp.bfloat16
    )
    out_ref[...] = d_pre
    sums_ref[...] = column_sum(d_pre.astype(jnp.float32))


def pre_back(second_low, w_down, slope):
    tokens, width = second_low.shape
    units = w_down.shape[0]
    columns = 512
    out = pl.BlockSpec((tokens, columns), lambda i: (0, i))
    return pl.pallas_call(
        pre_kernel,
        grid=(units // columns,),
        in_specs=[fixed((tokens, width)), pl.BlockSpec((columns, width), lambda i: (i, 0)), out],
        out_specs=[out, pl.BlockSpec((1, columns), lambda i: (0, i))],
        out_shape=[like((tokens, units)), like((1, units), jnp.float32)],
        cost_estimate=LITTLE,
        compiler_params=room(14),
        name="pre_back",
    )(second_low, w_down, slope)


def mid_kernel(
    p0_ref, p1_ref, w0_ref, w1_ref, d_second_ref, normed_ref, rstd_ref, gain_ref,
    resid_ref, low_ref, sums_ref, acc_ref,
):
    step = pl.program_id(0)
    rows = low_ref.shape[0]
    sums_of = pl.num_programs(0) - acc_ref.shape[0] // rows

    def products():
        return contract_last(p0_ref[...], w0_ref[...]) + contract_last(p1_ref[...], w1_ref[...])

    @pl.when(step == 0)
    def _():
        acc_ref[...] = products()
        sums_ref[...] = jnp.zeros_like(sums_ref)

    @pl.when((step > 0) & (step < sums_of))
    def _():
        acc_ref[...] += products()

    @pl.when(step >= sums_of)
    def _():
        gain = row_of(gain_ref)
        first = (step - sums_of) * rows
        for start in range(0, rows, 64):
            here = slice(start, start + 64)
            acc = acc_ref[pl.ds(pl.multiple_of(first + start, 64), 64), :]
            d_mid = d_second_ref[here, :] + acc
            normed = normed_ref[here, :]
            d_resid = norm_back(d_mid, normed, rstd_ref[here, :], gain)
            resid_ref[here, :] = d_resid
            low_ref[here, :] = d_resid.astype(jnp.bfloat16)
            parts = (column_sum(d_resid), column_sum(d_mid * normed), column_sum(d_mid))
            for j in range(3):
                sums_ref[j : j + 1, :] += parts[j]


def mid_back(d_pre, w_up, d_second, normed, rstd, gain):
    tokens, units = d_pre[0].shape
    width = w_up[0].shape[0]
    columns, rows = 512, 128
    steps = units // columns
    wide = pl.BlockSpec((rows, width), lambda i: (jnp.maximum(i - steps, 0), 0))
    part = pl.BlockSpec((tokens, columns), lambda i: (0, jnp.minimum(i, steps - 1)))
    weight = pl.BlockSpec((width, columns), lambda i: (0, jnp.minimum(i, steps - 1)))
    return pl.pallas_call(
        mid_kernel,
        grid=(steps + tokens // rows,),
        in_specs=[
            part, part, weight, weight, wide, wide,
            pl.BlockSpec((rows, 1), lambda i: (jnp.maximum(i - steps, 0), 0)), fixed(gain.shape),
        ],
        out_specs=[wide, wide, fixed((8, width))],
        out_shape=[
            like((tokens, width), jnp.float32),
            like((tokens, width)),
            like((8, width), jnp.float32),
        ],
        scratch_shapes=[pltpu.VMEM((tokens, width), jnp.float32)],
        cost_estimate=LITTLE,
        compiler_params=room(30),
        name="mid_back",
    )(*d_pre, *w_up, d_second, normed, rstd, gain)


def attend_back_kernel(qkv_ref, context_ref, weights_ref, low_ref, w_ref, out_ref, sums_ref):
    factor = HDIM ** (-0.5)
    queries, keys, values = qkv_ref[0], qkv_ref[1], qkv_ref[2]
    d_context = contract_last(low_ref[...], w_ref[...]).astype(jnp.bfloat16)
    product = d_context.astype(jnp.float32) * context_ref[...].astype(jnp.float32)
    grads = None
    for head in range(2):
        d_head = pick(d_context, head)
        d_weights = contract_last(d_head, values)
        inner = jnp.sum(pick(product, head), axis=-1, keepdims=True)
        weights = weights_ref[head]
        d_scores = (weights.astype(jnp.float32) * (d_weights - inner)).astype(jnp.bfloat16)
        parts = (
            dot(d_scores, pick(keys, head)),
            contract_rows(d_scores, pick(queries, head)),
            contract_rows(weights, d_head),
        )
        grads = parts if grads is None else tuple(a + b for a, b in zip(grads, parts))
    for j, scale in enumerate((factor, factor, 1.0)):
        grad = (grads[j] * scale).astype(jnp.bfloat16)
        out_ref[j] = grad
        sums_ref[j : j + 1, :] = column_sum(grad.astype(jnp.float32))


def attend_back_heads(qkv, context, weights, resid_low, w_out):
    _, tokens, width = qkv.shape
    depth = resid_low.shape[1]
    pair = 2 * HDIM
    block = pl.BlockSpec((3, tokens, pair), lambda i: (0, 0, i))
    return pl.pallas_call(
        attend_back_kernel,
        grid=(width // pair,),
        in_specs=[
            block,
            pl.BlockSpec((tokens, pair), lambda i: (0, i)),
            pl.BlockSpec((2, tokens, tokens), lambda i: (i, 0, 0)),
            fixed((tokens, depth)),
            pl.BlockSpec((pair, depth), lambda i: (i, 0)),
        ],
        out_specs=[block, pl.BlockSpec((8, pair), lambda i: (0, i))],
        out_shape=[like((3, tokens, width)), like((8, width), jnp.float32)],
        cost_estimate=LITTLE,
        compiler_params=room(16),
        name="attend_back",
    )(qkv, context, weights, resid_low, w_out)


def gather_kernel(h0_ref, h1_ref, p0_ref, p1_ref, mid_ref, second_ref, own_ref, other_ref):
    width = own_ref.shape[1]
    part = h0_ref.shape[1]
    for h_ref, p_ref, out_ref in ((h0_ref, p0_ref, own_ref), (h1_ref, p1_ref, other_ref)):
        out_ref[...] = jnp.zeros_like(out_ref)
        out_ref[0:1, :part] = h_ref[0:1, :]
        out_ref[0:1, part : 2 * part] = h_ref[2:3, :]
        for j in range(p_ref.shape[1] // width):
            out_ref[1 + j : 2 + j, :] = p_ref[:, j * width : (j + 1) * width]
        out_ref[8:11, :] = mid_ref[0:3, :]
        out_ref[11:14, :] = second_ref[0:3, :]


def gather_sums(heads, pre, mid, second):
    out = like((16, mid.shape[1]), jnp.float32)
    return pl.pallas_call(
        gather_kernel,
        out_shape=[out, out],
        cost_estimate=LITTLE,
        compiler_params=room(4),
        name="gather_sums",
    )(*heads, *pre, mid, second)


def last_kernel(d0_ref, d1_ref, *refs):
    resid_ref, out_ref = refs[6:]
    out = resid_ref[...]
    for j in range(3):
        out = out + (
            contract_last(d0_ref[j], refs[2 * j][...]) + contract_last(d1_ref[j], refs[2 * j + 1][...])
        )
    out_ref[...] = out


def last_back(d_heads, w_query, w_key, w_value, d_resid):
    tokens, width = d_resid.shape
    part = d_heads[0].shape[2]
    columns = 256
    heads = fixed((3, tokens, part))
    wide = pl.BlockSpec((tokens, columns), lambda i: (0, i))
    weight = pl.BlockSpec((columns, part), lambda i: (i, 0))
    return pl.pallas_call(
        last_kernel,
        grid=(width // columns,),
        in_specs=[heads, heads] + [weight] * 6 + [wide],
        out_specs=wide,
        out_shape=like((tokens, width), jnp.float32),
        cost_estimate=LITTLE,
        compiler_params=room(16),
        name="last_back",
    )(*d_heads, *w_query, *w_key, *w_value, d_resid)


def move(values, target):
    pairs = []
    for z in range(4):
        for y in range(2):
            for x in range(2):
                for core in range(2):
                    there = target(x, y, z, core)
                    if there is not None:
                        tx, ty, tz, tcore = there
                        pairs.append(
                            ((z * 4 + y * 2 + x) * 2 + core, (tz * 4 + ty * 2 + tx) * 2 + tcore)
                        )
    return lax.ppermute(values, ("batch", "mp"), pairs)


def swap_core(values):
    return move(values, lambda x, y, z, core: (x, y, z, 1 - core))


def turn(x, y, z, core, along):
    return (1 - x, y, z, core) if along == 0 else (x, 1 - y, z, core)


def swap_first(values):
    return move(values, lambda x, y, z, core: turn(x, y, z, core, core))


def swap_second(values):
    return move(values, lambda x, y, z, core: turn(x, y, z, core, 1 - core))


def swap_near(values):
    return move(values, lambda x, y, z, core: (x, y, z ^ 1, core))


def swap_far(values):
    return move(values, lambda x, y, z, core: (x, y, 3 - z, core))


def placement():
    batch, core = lax.axis_index("batch"), lax.axis_index("mp")
    x, y, z = batch % 2, batch // 2 % 2, batch // 4
    first, second = jnp.where(core == 0, x, y), jnp.where(core == 0, y, x)
    near = jnp.where((z == 1) | (z == 2), 1, 0)
    return jnp.stack([first, second, near, z // 2, core]).astype(jnp.int32)


PLANE_FIRST = ((0, swap_first), (1, swap_second), (2, swap_near), (3, swap_far))
LINE_FIRST = ((2, swap_near), (3, swap_far), (0, swap_first), (1, swap_second))


ORDER = (
    "down", "pre", "up", "D", "pre", "mid", "out", "U", "O", "O", "attn", "D", "D", "O",
    "heads", "U", "U", "attn", "U", "small", "O", "H", "U", "D", "O", "U", "D", "H",
    "H", "U", "small", "H", "U", "small", "O", "O", "H", "D", "small", "D", "H", "H",
    "D", "O", "U", "small", "small", "H", "last", "D", "O", "H",
)


class Line:
    def __init__(self):
        self.last = ()

    def after(self, *values):
        tied = lax.optimization_barrier((values, self.last))[0]
        return tied[0] if len(values) == 1 else tied

    def did(self, *results):
        self.last = results
        return results[0] if len(results) == 1 else results


def sum_chips(line, at, order, make, finish):
    (a, move_a), (b, move_b), (c, move_c), (_, move_d) = order
    mine = lambda k: lambda p: p[k]
    theirs = lambda k: lambda p: 1 - p[k]
    got_a = move_a(make(theirs(a)))
    yield
    half = make(mine(a))
    yield
    half, got_a = line.after(half, got_a)
    rows = half.shape[0] // 2
    got_b = move_b(line.did(combine(at, [(half, theirs(b)), (got_a, theirs(b))], rows)))
    yield
    got_b = line.after(got_b)
    rows //= 2
    there = lambda p: 2 * p[b] + 1 - p[c]
    here = lambda p: 2 * p[b] + p[c]
    got_c = move_c(line.did(combine(at, [(half, there), (got_a, there), (got_b, theirs(c))], rows)))
    yield
    got_c = line.after(got_c)
    part = line.did(combine(at, [(half, here), (got_a, here), (got_b, mine(c)), (got_c, whole)], rows))
    got_d = move_d(part)
    yield
    part, got_d = line.after(part, got_d)
    part = line.did(combine(at, [(part, whole), (got_d, whole)], rows))
    got_c = move_c(part)
    quarter = line.did(combine(at, [(part, whole)], rows, slab=mine(c), slabs=2))
    yield
    quarter, got_c = line.after(quarter, got_c)
    quarter = line.did(combine(at, [(got_c, whole)], rows, slab=theirs(c), slabs=2, into=quarter))
    got_b = move_b(quarter)
    half = line.did(combine(at, [(quarter, whole)], 2 * rows, slab=mine(b), slabs=2))
    yield
    half, got_b = line.after(half, got_b)
    half = line.did(combine(at, [(got_b, whole)], 2 * rows, slab=theirs(b), slabs=2, into=half))
    got_a = move_a(half)
    out = line.did(finish(half, mine(a), None))
    yield
    got_a = line.after(got_a)
    line.did(finish(got_a, theirs(a), out))
    yield


def sum_small(line, values):
    for move_on in (swap_first, swap_second, swap_near, swap_far):
        values = line.did(line.after(values))
        got = move_on(values)
        yield
        values, got = line.after(values, got)
        values = line.did(values + got)
    return values


def shards_paged(
    hidden,
    cell_ids,
    boxes,
    x_table,
    y_table,
    w_query,
    b_query,
    w_key,
    w_value,
    b_value,
    w_out,
    b_out,
    ln1_gain,
    ln1_bias,
    w_up,
    b_up,
    w_down,
    b_down,
    ln2_gain,
    ln2_bias,
    d_out,
):
    at = placement()
    page = lax.axis_index("mp").reshape(1)
    line = Line()
    part = b_query.shape[0]
    b_query, b_value, b_up = [(b, swap_core(b)) for b in (b_query, b_value, b_up)]
    line.did(b_query[1], b_value[1], b_up[1])
    hidden = line.after(hidden)
    x_table, y_table, hidden, d_out, cell_ids = [
        stay(v) for v in (x_table, y_table, hidden, d_out, cell_ids)
    ]
    w_query, w_key, w_value = [(stay(w), stay(swap_core(w))) for w in (w_query, w_key, w_value)]
    both = (0, 1)

    inputs, x_low = embed(page, cell_ids, boxes, x_table, y_table, hidden)
    attended = [
        attend_heads(x_low, w_query[i], w_key[i], w_value[i], b_query[i], b_value[i]) for i in both
    ]
    qkv, context, weights = zip(*attended)
    line.did(x_low, w_query[1], w_key[1], w_value[1])
    w_out, w_up, w_down = [
        (stay(w), stay(swap_core(line.after(w)))) for w in (w_out, w_up, w_down)
    ]
    mid_low, normed_one, rstd_one = resid_norm(inputs, context, w_out, b_out, ln1_gain, ln1_bias)
    raised = up(mid_low, w_up, b_up)
    activ, slope = raised[:2], raised[2:]
    layer_out, d_second, second_low, second_sums = turn_back(
        activ, w_down, normed_one, (ln1_gain, ln1_bias, b_down, ln2_gain, ln2_bias), d_out
    )
    line.did(second_low)
    found = {"d_pre": {}, "pre sums": {}, "heads": {}, "heads sums": {}}

    def grads(name, product, left, right):
        found[name] = swap_core(line.did(product(line.after(left(1)), right(1))))
        yield

    def halves(name, product, left, right):
        def make(which):
            mine, sent = line.after(left(0), found[name])
            return line.did(product(mine, right(0), sent, which))

        return make

    def pre_steps():
        for i in (1, 0):
            low = line.after(second_low)
            found["d_pre"][i], found["pre sums"][i] = pre_back(low, w_down[i], slope[i])
            line.did(found["d_pre"][i])
            yield

    def mid_steps():
        d_pre = [found["d_pre"][i] for i in both]
        d_pre[0] = line.after(d_pre[0])
        found["d_resid"], found["resid_low"], found["mid sums"] = mid_back(
            d_pre, w_up, d_second, normed_one, rstd_one, ln1_gain
        )
        line.did(found["resid_low"])
        yield

    def attend_steps():
        for i in (1, 0):
            low = line.after(found["resid_low"])
            found["heads"][i], found["heads sums"][i] = attend_back_heads(
                stay(qkv[i]), context[i], stay(weights[i]), low, w_out[i]
            )
            line.did(found["heads"][i])
            yield

    def last_steps():
        d_heads = [found["heads"][i] for i in both]
        d_heads[0] = line.after(d_heads[0])
        found["d_hidden"] = line.did(
            last_back(d_heads, w_query, w_key, w_value, found["d_resid"])
        )
        yield

    def small_steps():
        own, other = line.did(
            gather_sums(
                [line.after(found["heads sums"][i]) for i in both],
                [found["pre sums"][i] for i in both],
                found["mid sums"],
                second_sums,
            )
        )
        got = swap_core(other)
        yield
        own, got = line.after(own, got)
        found["small"] = yield from sum_small(line, own + got)
        line.did(found["small"])
        yield

    def store(name):
        def finish(values, slab, into):
            rows = values.shape[0]
            found[name] = combine(
                at, [(values, whole)], rows, kind=jnp.float32, slab=slab, slabs=2, into=into
            )
            return found[name]

        return finish

    def store_heads(values, slab, into):
        found["heads grads"] = tuple(spread(at, values, 3, slab, into))
        return found["heads grads"]

    units, depth = activ[0].shape[1], mid_low.shape[1]
    second_of = lambda i: second_low
    mid_of = lambda i: mid_low
    pre_of = lambda i: found["d_pre"][i]
    resid_of = lambda i: found["resid_low"]
    activ_of = lambda i: activ[i]
    context_of = lambda i: context[i]
    x_of = lambda i: x_low
    heads_of = lambda i: found["heads"][i]

    def span(start, rows):
        def product(left, right, sent=None, which=None):
            return weight_grad(at, left, right, start, rows, sent, which)

        return product

    def heads_product(left, right, sent=None, which=None):
        return heads_grad(at, left, right, sent, which)

    cut = depth * 3 // 4
    steps = {
        "down": grads("down", span(0, units), activ_of, second_of),
        "pre": pre_steps(),
        "up": grads("up", span(0, depth), mid_of, pre_of),
        "mid": mid_steps(),
        "out": grads("out", span(0, context[0].shape[1]), context_of, resid_of),
        "attn": attend_steps(),
        "heads": grads("qkv", heads_product, x_of, heads_of),
        "last": last_steps(),
        "small": small_steps(),
    }
    chunks = {
        "D": (PLANE_FIRST, lambda: halves("down", span(0, units), activ_of, second_of), store("grad down")),
        "U": (PLANE_FIRST, lambda: halves("up", span(0, depth), mid_of, pre_of), store("grad up")),
        "O": (LINE_FIRST, lambda: halves("out", span(0, context[0].shape[1]), context_of, resid_of), store("grad out")),
        "H": (PLANE_FIRST, lambda: halves("qkv", heads_product, x_of, heads_of), store_heads),
    }
    for name in ORDER:
        if name not in steps:
            order, make, finish = chunks[name]
            steps[name] = sum_chips(line, at, order, make(), finish)
        next(steps[name])
    d_hidden = found["d_hidden"]
    grad_w_down, grad_w_up, grad_w_out = [found["grad " + n] for n in ("down", "up", "out")]
    grad_w_query, grad_w_key, grad_w_value = found["heads grads"]
    small = found["small"]
    grad_b_query, grad_b_value = small[0, :part], small[0, part : 2 * part]
    grad_b_up = small[1 : 1 + units // depth].reshape(-1)
    grad_b_out, grad_ln1_gain, grad_ln1_bias, grad_ln2_gain, grad_ln2_bias, grad_b_down = [
        small[j] for j in range(8, 14)
    ]
    return (
        layer_out,
        d_hidden,
        grad_w_query,
        grad_b_query,
        grad_w_key,
        grad_w_value,
        grad_b_value,
        grad_w_out,
        grad_b_out,
        grad_ln1_gain,
        grad_ln1_bias,
        grad_w_up,
        grad_b_up,
        grad_w_down,
        grad_b_down,
        grad_ln2_gain,
        grad_ln2_bias,
    )


def solution(mesh):
    in_specs = (
        P(("batch", "mp"), None),
        P("batch", None),
        P("batch", None, None),
        P(),
        P(),
        P(None, "mp"),
        P("mp"),
        P(None, "mp"),
        P(None, "mp"),
        P("mp"),
        P("mp", None),
        P(),
        P(),
        P(),
        P(None, "mp"),
        P("mp"),
        P("mp", None),
        P(),
        P(),
        P(),
        P(("batch", "mp"), None),
    )
    out_specs = (
        P(("batch", "mp"), None),
        P(("batch", "mp"), None),
        P(None, "mp"),
        P("mp"),
        P(None, "mp"),
        P(None, "mp"),
        P("mp"),
        P("mp", None),
        P(),
        P(),
        P(),
        P(None, "mp"),
        P("mp"),
        P("mp", None),
        P(),
        P(),
        P(),
    )
    paged = mesh.shape["mp"] == 2 and mesh.shape["batch"] == 16
    shards = shards_paged if paged else shards_general
    return jax.shard_map(shards, mesh=mesh, in_specs=in_specs, out_specs=out_specs, check_vma=False)
```
